256 devices in a mesh: dp: 16 (over y, x_hi, core), seq: 16 (over x_lo, z).
Axes of the slice: x: 4 (x_hi: 2, x_lo: 2; x = x_hi * 2 + x_lo), y: 4, z: 8, core: 2. Of those that a mesh axis runs over, the one named last changes fastest.
Arguments:
- frames: bfloat16 [16, 2048, 1024], P('dp', 'seq'), may hold values from -6 to 6
- cotangent: bfloat16 [16, 2048, 1024], P('dp', 'seq'), may hold values from -6 to 6
- w_qkv: bfloat16 [1024, 3072], replicated, may hold values from -3 to 3
- w_out: bfloat16 [1024, 1024], replicated, may hold values from -0.1875 to 0.1875
- w_conv: float32 [31, 1024], replicated, may hold values from -1 to 1
- lengths: int32 [16], P('dp'), may hold values from 512 to 2048, as said below
Outputs:
- output: bfloat16 [16, 2048, 1024], P('dp', 'seq')
- input_grad: bfloat16 [16, 2048, 1024], P('dp', 'seq')
- qkv_grad: float32 [1024, 3, 1024], P('dp', None, 'seq')
- out_grad: float32 [1024, 1024], P(('dp', 'seq'))
- conv_grad: float32 [31, 1024], replicated
The draws below stay inside these ranges and needn't reach their ends.
Inputs may be any that keep to these rules, and one draw needn't show every extreme that they name: `lengths`: at least one utterance has all 2048 frames valid.
All inputs are finite; a program needn't handle non-finite values.
Results may differ from the reference program's by a relative error of at most 0.017.
The reference program's roundings to bfloat16 on the way (of `normed`, `joined_proj`, `attended`, `residual`, `conv_in`, `grad_round`, `attended_grad` and `joined_grad`) count: a program that leaves them out, or rounds other values in their place, can miss the bound.
Values may be sent and summed in bfloat16 or wider, within the bound.
No kernel may reach another device: no remote copies, remote signals or barrier semaphores. Data moves between devices by JAX's collectives and lax.ppermute only.
A program may use at most 128 MiB of HBM per device.

```python
import math
import jax
import jax.numpy as jnp
from jax import lax

D = 1024
HEADS = 16
KW = 31
SEQ_LEN = 2048
UTTS = 16


def draw_lengths(key, part):
    base_lengths = jax.random.randint(jax.random.fold_in(key, 11), (UTTS,), SEQ_LEN // 4, SEQ_LEN + 1)
    whole_one = jax.random.randint(jax.random.fold_in(key, 12), (), 0, UTTS)
    return jnp.where(jnp.arange(UTTS) == whole_one, SEQ_LEN, base_lengths).astype(jnp.int32)


def draw_w_qkv(key, part):
    weights = jnp.clip(jax.random.normal(jax.random.fold_in(key, 21), (D, 3 * D), jnp.float32), -5.0, 5.0) * D ** (-0.5)
    return weights.astype(jnp.bfloat16)


def block_levels(own_key, extent, split, smallest, largest):
    def one(position, shards_of):
        draws = jax.random.uniform(jax.random.fold_in(jax.random.fold_in(own_key, 6), position), (shards_of,), jnp.float32, smallest / len(split), largest / len(split))
        return jnp.repeat(jnp.exp(draws), extent[position] // shards_of).reshape((-1,) + (1,) * (len(extent) - position - 1))

    factor_of = one(*split[0])
    for cut in split[1:]:
        factor_of = factor_of * one(*cut)
    return factor_of


def normal_values(own_key, extent, scale, reach, cuts=(), kind=jnp.bfloat16):
    factor_of = block_levels(own_key, extent, cuts, -0.22, 0.18) if cuts else 1.0
    values = jax.random.normal(own_key, extent, jnp.float32) * scale * factor_of
    return jnp.minimum(jnp.maximum(values, -reach), reach).astype(kind)


def setup_inputs(seed: int = 0) -> dict:
    streams_of = jax.random.split(jax.random.key(seed), 7)
    frames = normal_values(streams_of[0], (UTTS, SEQ_LEN, D), 1.0, 6.0, ((0, 16), (1, 16)))
    cotangent = normal_values(streams_of[1], (UTTS, SEQ_LEN, D), 1.0, 6.0, ((0, 16), (1, 16)))
    w_qkv = draw_w_qkv(jax.random.fold_in(streams_of[6], 71), 0)
    w_out = normal_values(streams_of[3], (D, D), D ** -0.5, 0.1875)
    w_conv = normal_values(streams_of[4], (KW, D), KW ** -0.5, 1.0, (), jnp.float32)
    lengths = draw_lengths(jax.random.fold_in(streams_of[6], 71), 0)
    return dict(frames=frames, cotangent=cotangent, w_qkv=w_qkv, w_out=w_out, w_conv=w_conv, lengths=lengths)


def layer_norm(inputs):
    center = inputs - lax.optimization_barrier(jnp.mean(inputs, axis=-1, keepdims=True))
    spread = lax.optimization_barrier(jnp.mean(center * center, axis=-1, keepdims=True))
    return center * lax.rsqrt(spread + 1e-05)

def norm_backward(inputs, upstream):
    unused_out, pullback = jax.vjp(layer_norm, inputs)
    return pullback(upstream)[0]

def block_probs(query_block, key_rows, key_keep, score_scale):
    scores = lax.dot_general(query_block, key_rows, (((1,), (1,)), ((), ())), preferred_element_type=jnp.float32) * score_scale
    scores = jnp.where(key_keep[None, :], scores, -1000000000.0)
    row_peak = lax.optimization_barrier(jnp.max(scores, axis=-1, keepdims=True))
    expo_rows = jnp.exp(scores - row_peak)
    return expo_rows / lax.optimization_barrier(jnp.sum(expo_rows, axis=-1, keepdims=True))

def attention_forward(query_rows, key_rows, value_rows, key_keep):
    length_all, head_dim = query_rows.shape
    block_size = min(512, length_all)
    score_scale = 1.0 / math.sqrt(head_dim)

    def one_block(query_block):
        probabilities = block_probs(query_block, key_rows, key_keep, score_scale)
        return jnp.dot(probabilities.astype(jnp.bfloat16), value_rows, preferred_element_type=jnp.float32).astype(jnp.bfloat16)
    blocked = query_rows.reshape(length_all // block_size, block_size, head_dim)
    return lax.map(one_block, blocked).reshape(length_all, head_dim)

def attention_backward(query_rows, key_rows, value_rows, grad_rows, key_keep):
    length_all, head_dim = query_rows.shape
    block_size = min(512, length_all)
    block_count = length_all // block_size
    score_scale = 1.0 / math.sqrt(head_dim)

    def one_block(running, block_items):
        key_grad, value_grad = running
        query_block, grad_block = block_items
        probabilities = block_probs(query_block, key_rows, key_keep, score_scale)
        prob_grad = lax.dot_general(grad_block, value_rows, (((1,), (1,)), ((), ())), preferred_element_type=jnp.float32)
        score_grad = (probabilities * (prob_grad - lax.optimization_barrier(jnp.sum(prob_grad * probabilities, axis=-1, keepdims=True))) * score_scale).astype(jnp.bfloat16)
        query_grad = jnp.dot(score_grad, key_rows, preferred_element_type=jnp.float32)
        key_grad = key_grad + lax.dot_general(score_grad, query_block, (((0,), (0,)), ((), ())), preferred_element_type=jnp.float32)
        value_grad = value_grad + lax.dot_general(probabilities.astype(jnp.bfloat16), grad_block, (((0,), (0,)), ((), ())), preferred_element_type=jnp.float32)
        return ((key_grad, value_grad), query_grad)
    zero_rows = jnp.zeros((length_all, head_dim), jnp.float32)
    blocked_q = query_rows.reshape(block_count, block_size, head_dim)
    blocked_g = grad_rows.reshape(block_count, block_size, head_dim)
    (key_grad, value_grad), query_grad = lax.scan(one_block, (zero_rows, zero_rows), (blocked_q, blocked_g))
    return (query_grad.reshape(length_all, head_dim).astype(jnp.bfloat16), key_grad.astype(jnp.bfloat16), value_grad.astype(jnp.bfloat16))

def conv_apply(padded, kernel, row_count):
    result = jnp.zeros((row_count, padded.shape[1]), jnp.float32)
    for offset in range(kernel.shape[0]):
        result = result + kernel[offset][None, :] * padded[offset:offset + row_count].astype(jnp.float32)
    return result

def conv_adjoint(padded_grad, kernel, row_count):
    taps_count = kernel.shape[0]
    result = jnp.zeros((row_count, padded_grad.shape[1]), jnp.float32)
    for offset in range(taps_count):
        first = taps_count - 1 - offset
        result = result + kernel[offset][None, :] * padded_grad[first:first + row_count]
    return result

def conv_kernel_grad(padded, conv_back, taps_count):
    row_count = conv_back.shape[0]
    pieces = [lax.optimization_barrier(jnp.sum(padded[offset:offset + row_count].astype(jnp.float32) * conv_back, axis=0)) for offset in range(taps_count)]
    return jnp.stack(pieces, axis=0)

def utterance(frame_rows, grad_rows, length, w_qkv, w_out, w_conv):
    length_all, model_width = frame_rows.shape
    head_count = HEADS
    head_dim = model_width // head_count
    half_width = KW // 2
    key_keep = jnp.arange(length_all, dtype=jnp.int32) < length
    keep_col = key_keep.astype(jnp.float32)[:, None]
    inputs = frame_rows.astype(jnp.float32)
    normed = layer_norm(inputs).astype(jnp.bfloat16)
    joined_proj = jnp.dot(normed, w_qkv, preferred_element_type=jnp.float32).astype(jnp.bfloat16)
    per_head = jnp.transpose(joined_proj.reshape(length_all, 3, head_count, head_dim), (1, 2, 0, 3))

    def head_forward(head_set):
        return attention_forward(head_set[0], head_set[1], head_set[2], key_keep)
    attended_heads = lax.map(head_forward, (per_head[0], per_head[1], per_head[2]))
    attended = jnp.transpose(attended_heads, (1, 0, 2)).reshape(length_all, model_width)
    residual = (inputs + jnp.dot(attended, w_out, preferred_element_type=jnp.float32)).astype(jnp.bfloat16)
    residual_float = residual.astype(jnp.float32)
    conv_in = (layer_norm(residual_float) * keep_col).astype(jnp.bfloat16)
    padded = jnp.pad(conv_in, ((half_width, half_width), (0, 0)))
    conv_out = conv_apply(padded, w_conv, length_all)
    sigmoid_gate = jax.nn.sigmoid(conv_out)
    output = (residual_float + conv_out * sigmoid_gate).astype(jnp.bfloat16)
    grad_float = grad_rows.astype(jnp.float32)
    conv_back = grad_float * (sigmoid_gate + conv_out * sigmoid_gate * (1.0 - sigmoid_gate))
    conv_in_grad = conv_adjoint(jnp.pad(conv_back, ((half_width, half_width), (0, 0))), w_conv, length_all)
    kernel_part = conv_kernel_grad(padded, conv_back, KW)
    residual_grad = grad_float + norm_backward(residual_float, conv_in_grad * keep_col)
    grad_round = residual_grad.astype(jnp.bfloat16)
    out_part = lax.dot_general(attended, grad_round, (((0,), (0,)), ((), ())), preferred_element_type=jnp.float32)
    attended_grad = lax.dot_general(grad_round, w_out, (((1,), (1,)), ((), ())), preferred_element_type=jnp.float32).astype(jnp.bfloat16)
    head_grads = jnp.transpose(attended_grad.reshape(length_all, head_count, head_dim), (1, 0, 2))

    def head_backward(head_set):
        return attention_backward(head_set[0], head_set[1], head_set[2], head_set[3], key_keep)
    query_grad, key_grad, value_grad = lax.map(head_backward, (per_head[0], per_head[1], per_head[2], head_grads))
    joined_grad = jnp.transpose(jnp.stack([query_grad, key_grad, value_grad], axis=0), (2, 0, 1, 3)).reshape(length_all, 3 * model_width)
    qkv_part = lax.dot_general(normed, joined_grad, (((0,), (0,)), ((), ())), preferred_element_type=jnp.float32)
    normed_grad = lax.dot_general(joined_grad, w_qkv, (((1,), (1,)), ((), ())), preferred_element_type=jnp.float32)
    input_grad = (residual_grad + norm_backward(inputs, normed_grad)).astype(jnp.bfloat16)
    return (output, input_grad, qkv_part, out_part, kernel_part)

def reference(frames, cotangent, w_qkv, w_out, w_conv, lengths):
    utterance_count, length_all, model_width = frames.shape

    def utterance_step(running, slices):
        results = utterance(slices[0], slices[1], slices[2], w_qkv, w_out, w_conv)
        sums = (running[0] + results[2], running[1] + results[3], running[2] + results[4])
        return (sums, (results[0], results[1]))
    start_sums = (jnp.zeros((model_width, 3 * model_width), jnp.float32), jnp.zeros((model_width, model_width), jnp.float32), jnp.zeros((KW, model_width), jnp.float32))
    (qkv_sum, out_sum, kernel_sum), (output, input_grad) = lax.scan(utterance_step, start_sums, (frames, cotangent, lengths))
    grad_scale = 1.0 / math.sqrt(utterance_count * length_all)
    qkv_grad = (qkv_sum * grad_scale).reshape(model_width, 3, model_width)
    return (output, input_grad, qkv_grad, out_sum * grad_scale, kernel_sum * grad_scale)
```

```python
import math

import jax
import jax.numpy as jnp
from jax import lax
from jax.experimental import pallas as pl
from jax.experimental.pallas import tpu as pltpu
from jax.sharding import PartitionSpec as P

HEADS = 16
KW = 31
HD = 64
HALO = 32
QB = 256
KB = 256
F32 = jnp.float32
BF16 = jnp.bfloat16
LIMIT = 56 * 1024 * 1024


def dot(a, b, ca=1, cb=0):
    return lax.dot_general(a, b, (((ca,), (cb,)), ((), ())), preferred_element_type=F32)


def normalize(rows):
    center = rows - jnp.mean(rows, axis=-1, keepdims=True)
    scale = lax.rsqrt(jnp.mean(center * center, axis=-1, keepdims=True) + 1e-05)
    return center * scale, scale


def normalize_back(unit, scale, upstream):
    return scale * (
        upstream
        - jnp.mean(upstream, axis=-1, keepdims=True)
        - unit * jnp.mean(upstream * unit, axis=-1, keepdims=True)
    )


def params(**kw):
    return pltpu.CompilerParams(vmem_limit_bytes=LIMIT, **kw)


def whole(shape):
    return pl.BlockSpec(shape, lambda *_: (0,) * len(shape))


def halves(exact):
    top = exact.astype(BF16)
    rest = (exact - top.astype(F32)).astype(BF16)
    return jnp.concatenate([top, rest], axis=1)


def joined_halves(pair):
    return pair[:, : pair.shape[1] // 2] + pair[:, pair.shape[1] // 2 :]


SMEM = pl.BlockSpec(memory_space=pltpu.SMEM)


def project_kernel(frames_ref, weight_ref, normed_ref, send_ref):
    @pl.when(pl.program_id(0) == 0)
    def _():
        unit, _ = normalize(frames_ref[...].astype(F32))
        normed_ref[...] = unit.astype(BF16)

    part = dot(normed_ref[...], weight_ref[...]).astype(BF16)
    send_ref[...] = part.T.reshape(send_ref.shape)


def project(frames, w_qkv):
    rows, width = frames.shape
    cols = 512
    per = cols // HD
    groups = HEADS // per
    return pl.pallas_call(
        project_kernel,
        grid=(3 * groups,),
        in_specs=[whole(frames.shape), pl.BlockSpec((width, cols), lambda j: (0, j))],
        out_specs=[
            whole(frames.shape),
            pl.BlockSpec((per, HD, rows), lambda j: (j % groups, j // groups, 0)),
        ],
        out_shape=[
            jax.ShapeDtypeStruct(frames.shape, BF16),
            jax.ShapeDtypeStruct((HEADS, 3 * HD, rows), BF16),
        ],
        compiler_params=params(),
        name="project",
    )(frames, w_qkv)


def load_heads(length, heads_ref, query, keys, count, rows):
    extra = lax.broadcasted_iota(jnp.int32, (HD, rows), 0)
    frame = lax.broadcasted_iota(jnp.int32, (HD, rows), 1)
    for i in range(count):
        cols = slice(i * rows, (i + 1) * rows)
        query[0:HD, cols] = (heads_ref[i, 0:HD, :].astype(F32) * 0.125).astype(BF16)
        query[HD : 2 * HD, cols] = jnp.where(extra == 0, 1.0, 0.0).astype(BF16)
        masked = jnp.logical_and(extra == 0, frame + i * rows >= length)
        mask = jnp.where(masked, -1e30, 0.0).astype(BF16)
        joined = jnp.concatenate([heads_ref[i, HD : 2 * HD, :], mask], axis=0)
        keys[cols, :] = joined.T


def attend_kernel(
    scalars, heads_ref, send_ref, own_ref, out_ref, lse_ref, query, keys, value, scores
):
    count, _, rows = heads_ref.shape
    total = count * rows
    load_heads(scalars[0], heads_ref, query, keys, count, rows)
    for i in range(count):
        value[:, i * rows : (i + 1) * rows] = heads_ref[i, 2 * HD : 3 * HD, :]

    def one_block(block, carry):
        cols = pl.ds(pl.multiple_of(block * QB, QB), QB)
        query_cols = query[:, cols]
        peak = None
        for k in range(total // KB):
            part = dot(keys[k * KB : (k + 1) * KB, :], query_cols)
            scores[k * KB : (k + 1) * KB, :] = part
            top = jnp.max(part.reshape(KB // 8, 8, QB), axis=0)
            peak = top if peak is None else jnp.maximum(peak, top)
        peak = jnp.max(peak, axis=0, keepdims=True)
        total_row = jnp.zeros((8, QB), F32)
        acc = jnp.zeros((HD, QB), F32)
        for k in range(total // KB):
            expo = jnp.exp(scores[k * KB : (k + 1) * KB, :] - peak)
            total_row = total_row + jnp.sum(expo.reshape(KB // 8, 8, QB), axis=0)
            acc = acc + dot(value[:, k * KB : (k + 1) * KB], expo.astype(BF16))
        total_row = jnp.sum(total_row, axis=0, keepdims=True)
        result = acc / total_row
        out_ref[:, cols] = result
        own_ref[:, cols] = result.astype(BF16)
        lse_ref[:, cols] = peak + jnp.log(total_row)
        return carry

    lax.fori_loop(0, total // QB, one_block, 0)
    none = jnp.zeros((HD, HALO), F32)
    for i in range(count):
        send_ref[i, 0:HD, :] = own_ref[:, i * rows : (i + 1) * rows]
        low = out_ref[:, i * rows - HALO : i * rows] if i else none
        high = out_ref[:, (i + 1) * rows : (i + 1) * rows + HALO] if i < count - 1 else none
        sides = jnp.concatenate([low, high], axis=1)
        packed = jnp.concatenate([sides[0 : HD // 2], sides[HD // 2 :]], axis=1)
        send_ref[i, HD : HD + HD // 2, :] = packed.astype(BF16)


def attend(scalars, heads):
    count, _, rows = heads.shape
    total = count * rows
    return pl.pallas_call(
        attend_kernel,
        in_specs=[SMEM, pl.BlockSpec(memory_space=pltpu.VMEM)],
        out_shape=[
            jax.ShapeDtypeStruct((count, HD + HD // 2, rows), BF16),
            jax.ShapeDtypeStruct((HD, total), BF16),
            jax.ShapeDtypeStruct((HD, total), F32),
            jax.ShapeDtypeStruct((1, total), F32),
        ],
        scratch_shapes=[
            pltpu.VMEM((2 * HD, total), BF16),
            pltpu.VMEM((total, 2 * HD), BF16),
            pltpu.VMEM((HD, total), BF16),
            pltpu.VMEM((total, QB), F32),
        ],
        compiler_params=params(),
        name="attend",
    )(scalars, heads)


def middle_kernel(
    scalars,
    att_ref,
    frames_ref,
    frames_side,
    grads_ref,
    grads_side,
    w_out_ref,
    w_conv_ref,
    output_ref,
    res_grad_ref,
    send_ref,
    taps_ref,
    conv_in,
    grad_all,
    residual,
    window,
    window_back,
    conv_grad,
):
    rows, width = frames_ref.shape
    heads = att_ref.shape[0]
    length = scalars[0]
    first = scalars[1]
    zero = scalars[2]
    half = HD // 2
    body = slice(HALO, HALO + rows)

    attended = att_ref[:, 0:HD, :].reshape(width, rows).T
    main = frames_ref[...].astype(F32) + dot(attended, w_out_ref[...])
    packed = att_ref[:, HD : HD + half, :].reshape(heads * half, rows).T
    split_w = w_out_ref[...].reshape(heads, 2, half, width)
    side = dot(packed[0 : 2 * HALO], split_w[:, 0].reshape(heads * half, width))
    side = side + dot(packed[2 * HALO :], split_w[:, 1].reshape(heads * half, width))
    side = frames_side[...].astype(F32) + side

    def keep_of(count, start):
        frame = lax.broadcasted_iota(jnp.int32, (count, 1), 0) + start
        return jnp.where(jnp.logical_and(frame >= 0, frame < length), 1.0, 0.0)

    main = main.astype(BF16).astype(F32)
    residual[...] = main
    unit, scale = normalize(main)
    keep = keep_of(rows, first)
    conv_in[body, :] = (unit * keep).astype(BF16).astype(F32)
    unit_side, _ = normalize(side.astype(BF16).astype(F32))
    low = unit_side[0:HALO] * keep_of(HALO, first - HALO)
    high = unit_side[HALO:] * keep_of(HALO, first + rows)
    conv_in[0:HALO, :] = low.astype(BF16).astype(F32)
    conv_in[HALO + rows :, :] = high.astype(BF16).astype(F32)
    grad_all[0:HALO, :] = grads_side[0:HALO, :].astype(F32)
    grad_all[body, :] = grads_ref[...].astype(F32)
    grad_all[HALO + rows :, :] = grads_side[HALO:, :].astype(F32)

    reach = rows + HALO
    edge = HALO // 2

    def one_chunk(chunk, carry):
        lanes = pl.ds(pl.multiple_of(chunk * 128, 128), 128)
        window[...] = conv_in[:, lanes]
        acc = jnp.zeros((reach, 128), F32)
        for j in range(KW):
            acc = acc + w_conv_ref[j : j + 1, lanes] * window[pl.ds(zero + (1 + j), reach), :]
        gate = jax.nn.sigmoid(acc)
        back = grad_all[edge : edge + reach, lanes] * (gate + acc * gate * (1.0 - gate))
        window_back[...] = back
        gated = acc[edge : edge + rows] * gate[edge : edge + rows]
        output_ref[:, lanes] = (residual[:, lanes] + gated).astype(BF16)
        own = window_back[edge : edge + rows, :]
        acc = jnp.zeros((rows, 128), F32)
        for j in range(KW):
            acc = acc + w_conv_ref[j : j + 1, lanes] * window_back[
                pl.ds(zero + (KW - j), rows), :
            ]
            moved = window[pl.ds(zero + (edge + 1 + j), rows), :]
            taps_ref[j : j + 1, lanes] = jnp.sum(moved * own, axis=0, keepdims=True)
        taps_ref[KW : KW + 1, lanes] = jnp.zeros((1, 128), F32)
        conv_grad[:, lanes] = acc
        return carry

    lax.fori_loop(0, width // 128, one_chunk, 0)
    res_grad = grads_ref[...].astype(F32) + normalize_back(unit, scale, conv_grad[...] * keep)
    res_grad_ref[...] = res_grad
    rounded = res_grad.astype(BF16)
    columns = rounded.T
    send_ref[:, 0:HD, :] = dot(w_out_ref[...], columns).astype(BF16).reshape(heads, HD, rows)
    send_ref[:, HD : 2 * HD, :] = columns.reshape(heads, HD, rows)
    for h in range(heads):
        send_ref[h, 2 * HD :, :] = halves(taps_ref[:, h * HD : (h + 1) * HD])


def middle(scalars, att, frames, frames_side, grads, grads_side, w_out, w_conv):
    rows, width = frames.shape
    vmem = pl.BlockSpec(memory_space=pltpu.VMEM)
    return pl.pallas_call(
        middle_kernel,
        in_specs=[SMEM] + [vmem] * 7,
        out_shape=[
            jax.ShapeDtypeStruct((rows, width), BF16),
            jax.ShapeDtypeStruct((rows, width), F32),
            jax.ShapeDtypeStruct((HEADS, 2 * HD + KW + 1, rows), BF16),
        ],
        scratch_shapes=[
            pltpu.VMEM((KW + 1, width), F32),
            pltpu.VMEM((rows + 2 * HALO, width), F32),
            pltpu.VMEM((rows + 2 * HALO, width), F32),
            pltpu.VMEM((rows, width), F32),
            pltpu.VMEM((rows + 2 * HALO, 128), F32),
            pltpu.VMEM((rows + HALO, 128), F32),
            pltpu.VMEM((rows, width), F32),
        ],
        compiler_params=params(),
        name="middle",
    )(scalars, att, frames, frames_side, grads, grads_side, w_out, w_conv)


def attend_back_kernel(
    scalars, heads_ref, grads_ref, out_ref, lse_ref, send_ref,
    query, keys, value_t, grad_t, query_rows, grad_rows, query_grad, probs, score_grads,
):
    count, _, rows = heads_ref.shape
    total = count * rows
    load_heads(scalars[0], heads_ref, query, keys, count, rows)
    for i in range(count):
        cols = slice(i * rows, (i + 1) * rows)
        block = grads_ref[i, 0:HD, :]
        grad_t[:, cols] = block
        both = jnp.concatenate([query[0:HD, cols], block], axis=0).T
        query_rows[cols, :] = both[:, 0:HD]
        grad_rows[cols, :] = both[:, HD:]
        value_t[cols, :] = heads_ref[i, 2 * HD : 3 * HD, :].T
    query_grad[...] = jnp.zeros_like(query_grad)
    lse = lse_ref[...]
    delta = jnp.sum(grad_t[...].astype(F32) * out_ref[...], axis=0, keepdims=True)

    def one_block(block, carry):
        span = pl.ds(pl.multiple_of(block * KB, KB), KB)
        key_rows = keys[span, :]
        value_rows = value_t[span, :]
        for q in range(total // QB):
            cols = slice(q * QB, (q + 1) * QB)
            prob = jnp.exp(dot(key_rows, query[:, cols]) - lse[:, cols])
            prob_grad = dot(value_rows, grad_t[:, cols])
            probs[:, cols] = prob.astype(BF16)
            score_grads[:, cols] = (prob * (prob_grad - delta[:, cols])).astype(BF16)
        key_grad = dot(score_grads[...], query_rows[...])
        value_grad = dot(probs[...], grad_rows[...])
        key_cols = key_rows[:, 0:HD].T
        query_grad[...] += dot(key_cols, score_grads[...])
        joined = jnp.concatenate([key_grad, value_grad], axis=1).T.astype(BF16)
        for i in range(KB // rows):
            send_ref[block * (KB // rows) + i, HD : 3 * HD, :] = joined[:, i * rows : (i + 1) * rows]
        return carry

    lax.fori_loop(0, total // KB, one_block, 0)
    for i in range(count):
        cols = slice(i * rows, (i + 1) * rows)
        send_ref[i, 0:HD, :] = (query_grad[:, cols] * 0.125).astype(BF16)


def attend_back(scalars, heads, grads, out, lse):
    count, _, rows = heads.shape
    total = count * rows
    vmem = pl.BlockSpec(memory_space=pltpu.VMEM)
    return pl.pallas_call(
        attend_back_kernel,
        in_specs=[SMEM] + [vmem] * 4,
        out_shape=jax.ShapeDtypeStruct(heads.shape, BF16),
        scratch_shapes=[
            pltpu.VMEM((2 * HD, total), BF16),
            pltpu.VMEM((total, 2 * HD), BF16),
            pltpu.VMEM((total, HD), BF16),
            pltpu.VMEM((HD, total), BF16),
            pltpu.VMEM((total, HD), BF16),
            pltpu.VMEM((total, HD), BF16),
            pltpu.VMEM((HD, total), F32),
            pltpu.VMEM((KB, total), BF16),
            pltpu.VMEM((KB, total), BF16),
        ],
        compiler_params=params(),
        name="attend_back",
    )(scalars, heads, grads, out, lse)


def input_grad_kernel(joined_ref, weight_ref, frames_ref, res_grad_ref, out_ref, joined, grads):
    step = pl.program_id(0)
    heads = joined_ref.shape[0]

    @pl.when(step == 0)
    def _():
        for h in range(heads):
            for t in range(3):
                row = (t * heads + h) * HD
                joined[row : row + HD, :] = joined_ref[h, t * HD : (t + 1) * HD, :]

    block = weight_ref.shape[0]
    start = pl.multiple_of(step * block, block)
    grads[pl.ds(start, block), :] = dot(weight_ref[...], joined[...])

    @pl.when(step == pl.num_programs(0) - 1)
    def _():
        unit, scale = normalize(frames_ref[...].astype(F32))
        back = normalize_back(unit, scale, grads[...].T)
        out_ref[...] = (res_grad_ref[...] + back).astype(BF16)


def input_gradient(joined, w_qkv, frames, res_grad):
    rows, width = frames.shape
    block = 256
    return pl.pallas_call(
        input_grad_kernel,
        grid=(width // block,),
        in_specs=[
            whole(joined.shape),
            pl.BlockSpec((block, w_qkv.shape[1]), lambda j: (j, 0)),
            whole(frames.shape),
            whole(frames.shape),
        ],
        out_specs=whole(frames.shape),
        out_shape=jax.ShapeDtypeStruct(frames.shape, BF16),
        scratch_shapes=[
            pltpu.VMEM((w_qkv.shape[1], rows), BF16),
            pltpu.VMEM((width, rows), F32),
        ],
        compiler_params=params(),
        name="input_gradient",
    )(joined, w_qkv, frames, res_grad)


def parts_kernel(grads_ref, back_ref, normed_ref, att_ref, send_ref, columns, back_rows):
    count, wide, rows = grads_ref.shape
    slow = pl.program_id(0)
    fast = send_ref.shape[0]

    @pl.when(slow == 0)
    def _():
        taps = jnp.zeros((KW + 1, rows), F32)
        for i in range(count):
            columns[:, i * rows : (i + 1) * rows] = grads_ref[i]
            back_rows[i * rows : (i + 1) * rows, :] = back_ref[i, HD : 2 * HD, :].T
            taps = taps + back_ref[i, 2 * HD :, :].astype(F32)
        pair = halves(joined_halves(taps))
        for i in range(fast):
            send_ref[i, TAPS:, :] = pair

    part = dot(columns[...], normed_ref[...])
    outer = dot(att_ref[...], back_rows[...])
    each = part.shape[1] // fast
    for i in range(fast):
        piece = part[:, i * each : (i + 1) * each]
        first = pl.multiple_of(slow * CUT, CUT)
        send_ref[i, pl.ds(first, wide // 2), :] = jnp.concatenate(
            [piece[0 : wide // 2], piece[wide // 2 :]], axis=1
        ).astype(BF16)
        piece = outer[i * each : (i + 1) * each, :]
        send_ref[i, pl.ds(first + wide // 2, each // 2), :] = jnp.concatenate(
            [piece[0 : each // 2], piece[each // 2 :]], axis=1
        ).astype(BF16)


CUT = 128
FAST = 4
SLOW = 4
TAPS = SLOW * CUT


def gradient_parts(grads, back, normed_all, att_all):
    count, wide, rows = grads.shape
    total, width = normed_all.shape
    return pl.pallas_call(
        parts_kernel,
        grid=(SLOW,),
        in_specs=[
            whole(grads.shape),
            whole(back.shape),
            pl.BlockSpec((total, width // SLOW), lambda j: (0, j)),
            pl.BlockSpec((width // SLOW, total), lambda j: (j, 0)),
        ],
        out_specs=whole((FAST, TAPS + KW + 1, 128)),
        out_shape=jax.ShapeDtypeStruct((FAST, TAPS + KW + 1, 128), BF16),
        scratch_shapes=[pltpu.VMEM((wide, total), BF16), pltpu.VMEM((total, HD), BF16)],
        compiler_params=params(),
        name="gradient_parts",
    )(grads, back, normed_all, att_all)


def fold_fast_kernel(scalars, own_ref, one, two, three, out_ref):
    own = own_ref[scalars[3]]
    for i in range(SLOW):
        cut = slice(i * CUT, (i + 1) * CUT)
        total = own[cut].astype(F32) + one[cut, :].astype(F32)
        total = total + (two[cut, :].astype(F32) + three[cut, :].astype(F32))
        out_ref[i, 0:CUT, :] = total.astype(BF16)
    cut = slice(TAPS, TAPS + KW + 1)
    total = own[cut].astype(F32) + one[cut, :].astype(F32)
    total = total + (two[cut, :].astype(F32) + three[cut, :].astype(F32))
    pair = halves(joined_halves(total))
    for i in range(SLOW):
        out_ref[i, CUT:, :] = pair


def fold_fast(scalars, own, others):
    vmem = pl.BlockSpec(memory_space=pltpu.VMEM)
    return pl.pallas_call(
        fold_fast_kernel,
        in_specs=[SMEM] + [vmem] * 4,
        out_shape=jax.ShapeDtypeStruct((SLOW, CUT + KW + 1, 128), BF16),
        compiler_params=params(),
        name="fold_fast",
    )(scalars, own, *others)


def fold_slow_kernel(scalars, own_ref, one, two, three, qkv_ref, send_ref, *, scale):
    total = own_ref[scalars[4]].astype(F32) + one[...].astype(F32)
    total = (total + (two[...].astype(F32) + three[...].astype(F32))) * scale
    wide = 3 * HD // 2
    whole_rows = total[0:wide].T
    qkv_ref[:, 0:wide] = whole_rows[0:HD]
    qkv_ref[:, wide:] = whole_rows[HD:]
    outer = total[wide:CUT]
    rows = jnp.concatenate([outer[:, 0:HD], outer[:, HD:]], axis=0)
    taps = joined_halves(total[CUT:])
    half = (KW + 1) // 2
    pair = jnp.concatenate([taps[0:half], taps[half:]], axis=1)
    count = send_ref.shape[0]
    each = HD // count
    for i in range(count):
        piece = rows[i * each : (i + 1) * each]
        send_ref[i, 0:half, :] = pair
        send_ref[i, half : half + each, 0:HD] = piece
        send_ref[i, half : half + each, HD:] = piece
        send_ref[i, half + each :, :] = jnp.zeros((8 - each, 128), F32)


def fold_slow(scalars, own, others, seq_count, scale):
    vmem = pl.BlockSpec(memory_space=pltpu.VMEM)
    return pl.pallas_call(
        lambda *refs: fold_slow_kernel(*refs, scale=scale),
        in_specs=[SMEM] + [vmem] * 4,
        out_shape=[
            jax.ShapeDtypeStruct((HD, 3 * HD), F32),
            jax.ShapeDtypeStruct((seq_count, 24, 128), F32),
        ],
        compiler_params=params(),
        name="fold_slow",
    )(scalars, own, *others)


def finish_kernel(recv_ref, out_ref, taps_ref):
    count = recv_ref.shape[0]
    each = out_ref.shape[0]
    half = (KW + 1) // 2
    for i in range(count // 2):
        a = recv_ref[2 * i]
        b = recv_ref[2 * i + 1]
        lanes = slice(i * 2 * HD, (i + 1) * 2 * HD)
        out_ref[:, lanes] = jnp.concatenate(
            [a[half : half + each, 0:HD], b[half : half + each, HD:]], axis=1
        )
        taps_ref[0:half, lanes] = jnp.concatenate([a[0:half, 0:HD], b[0:half, 0:HD]], axis=1)
        taps_ref[half:KW, lanes] = jnp.concatenate(
            [a[0 : half - 1, HD:], b[0 : half - 1, HD:]], axis=1
        )


def finish(recv, width):
    count = recv.shape[0]
    vmem = pl.BlockSpec(memory_space=pltpu.VMEM)
    return pl.pallas_call(
        finish_kernel,
        in_specs=[vmem],
        out_shape=[
            jax.ShapeDtypeStruct((HD // count, width), F32),
            jax.ShapeDtypeStruct((KW, width), F32),
        ],
        compiler_params=params(),
        name="finish",
    )(recv)


def exchange(blocks, index, partner):
    pairs = lambda k: [(d, partner(d, k)) for d in range(FAST * SLOW)]
    received = []
    for k in range(1, 4):
        block = lax.dynamic_index_in_dim(blocks, index ^ k, 0, keepdims=False)
        received.append(lax.ppermute(block, "dp", pairs(k)))
    return received


def local(frames, cotangent, w_qkv, w_out, w_conv, lengths):
    seq_count = lax.axis_size("seq")
    data_count = lax.axis_size("dp")
    rows, width = frames.shape[1:]
    first = lax.axis_index("seq") * rows
    grad_scale = 1.0 / math.sqrt(data_count * rows * seq_count)
    position = lax.axis_index("dp")
    fast = position % FAST
    slow = position // FAST
    scalars = jnp.stack([lengths[0], first, jnp.zeros((), jnp.int32), fast, slow])
    x = frames[0]
    g = cotangent[0]

    forward = [(i, i + 1) for i in range(seq_count - 1)]
    backward = [(i + 1, i) for i in range(seq_count - 1)]
    low = lax.ppermute(jnp.concatenate([x[-HALO:], g[-HALO:]], axis=0), "seq", forward)
    high = lax.ppermute(jnp.concatenate([x[:HALO], g[:HALO]], axis=0), "seq", backward)
    x_side = jnp.concatenate([low[:HALO], high[:HALO]], axis=0)
    g_side = jnp.concatenate([low[HALO:], high[HALO:]], axis=0)

    normed, send = project(x, w_qkv)
    heads = lax.all_to_all(send, "seq", 0, 0, tiled=True)
    normed_all = lax.all_gather(normed, "seq", axis=0, tiled=True)
    send, own, out, lse = attend(scalars, heads)
    att = lax.all_to_all(send, "seq", 0, 0, tiled=True)
    att_all = lax.all_gather(own, "seq", axis=0, tiled=True)
    output, res_grad, send = middle(scalars, att, x, x_side, g, g_side, w_out, w_conv)
    back = lax.all_to_all(send, "seq", 0, 0, tiled=True)
    send = attend_back(scalars, heads, back, out, lse)
    joined = lax.all_to_all(send, "seq", 0, 0, tiled=True)
    parts = gradient_parts(send, back, normed_all, att_all)
    others = exchange(parts, fast, lambda d, k: d ^ k)
    parts = fold_fast(scalars, parts, others)
    others = exchange(parts, slow, lambda d, k: d ^ (FAST * k))
    qkv, send = fold_slow(scalars, parts, others, seq_count, grad_scale)
    input_grad = input_gradient(joined, w_qkv, x, res_grad)
    out_total, taps_total = finish(lax.all_to_all(send, "seq", 0, 0, tiled=True), width)
    return (
        output[None],
        input_grad[None],
        qkv.reshape(width // data_count, 3, HD),
        out_total,
        taps_total,
    )


def solution(mesh):
    placed = (P("dp", "seq", None), P("dp", "seq", None), P(), P(), P(), P("dp"))
    return jax.shard_map(
        local,
        mesh=mesh,
        in_specs=placed,
        out_specs=(
            P("dp", "seq", None),
            P("dp", "seq", None),
            P("dp", None, "seq"),
            P(("dp", "seq"), None),
            P(),
        ),
        check_vma=False,
    )
```

```python
import math

import jax
import jax.numpy as jnp
from jax import lax
from jax.experimental import pallas as pl
from jax.experimental.pallas import tpu as pltpu
from jax.sharding import PartitionSpec as P

HEADS = 16
KW = 31
HD = 64
HALO = 32
QB = 256
KB = 256
F32 = jnp.float32
BF16 = jnp.bfloat16
LIMIT = 56 * 1024 * 1024


def dot(a, b, ca=1, cb=0):
    return lax.dot_general(a, b, (((ca,), (cb,)), ((), ())), preferred_element_type=F32)


def normalize(rows):
    center = rows - jnp.mean(rows, axis=-1, keepdims=True)
    scale = lax.rsqrt(jnp.mean(center * center, axis=-1, keepdims=True) + 1e-05)
    return center * scale, scale


def normalize_back(unit, scale, upstream):
    return scale * (
        upstream
        - jnp.mean(upstream, axis=-1, keepdims=True)
        - unit * jnp.mean(upstream * unit, axis=-1, keepdims=True)
    )


def params(**kw):
    return pltpu.CompilerParams(vmem_limit_bytes=LIMIT, **kw)


def cost(flops, moved, expos=0):
    return pl.CostEstimate(flops=flops, bytes_accessed=moved, transcendentals=expos)


def whole(shape):
    return pl.BlockSpec(shape, lambda *_: (0,) * len(shape))


def halves(exact):
    top = exact.astype(BF16)
    rest = (exact - top.astype(F32)).astype(BF16)
    return jnp.concatenate([top, rest], axis=1)


def joined_halves(pair):
    return pair[:, : pair.shape[1] // 2] + pair[:, pair.shape[1] // 2 :]


SMEM = pl.BlockSpec(memory_space=pltpu.SMEM)


def project_kernel(frames_ref, weight_ref, normed_ref, send_ref):
    @pl.when(pl.program_id(0) == 0)
    def _():
        unit, _ = normalize(frames_ref[...].astype(F32))
        normed_ref[...] = unit.astype(BF16)

    part = dot(normed_ref[...], weight_ref[...]).astype(BF16)
    send_ref[...] = part.T.reshape(send_ref.shape)


def project(frames, w_qkv):
    rows, width = frames.shape
    cols = 512
    per = cols // HD
    groups = HEADS // per
    return pl.pallas_call(
        project_kernel,
        grid=(3 * groups,),
        in_specs=[whole(frames.shape), pl.BlockSpec((width, cols), lambda j: (0, j))],
        out_specs=[
            whole(frames.shape),
            pl.BlockSpec((per, HD, rows), lambda j: (j % groups, j // groups, 0)),
        ],
        out_shape=[
            jax.ShapeDtypeStruct(frames.shape, BF16),
            jax.ShapeDtypeStruct((HEADS, 3 * HD, rows), BF16),
        ],
        compiler_params=params(),
        name="project",
    )(frames, w_qkv)


def load_heads(length, heads_ref, query, keys, count, rows):
    extra = lax.broadcasted_iota(jnp.int32, (HD, rows), 0)
    frame = lax.broadcasted_iota(jnp.int32, (HD, rows), 1)
    for i in range(count):
        cols = slice(i * rows, (i + 1) * rows)
        query[0:HD, cols] = (heads_ref[i, 0:HD, :].astype(F32) * 0.125).astype(BF16)
        query[HD : 2 * HD, cols] = jnp.where(extra == 0, 1.0, 0.0).astype(BF16)
        masked = jnp.logical_and(extra == 0, frame + i * rows >= length)
        mask = jnp.where(masked, -1e30, 0.0).astype(BF16)
        joined = jnp.concatenate([heads_ref[i, HD : 2 * HD, :], mask], axis=0)
        keys[cols, :] = joined.T


def attend_kernel(
    scalars, heads_ref, send_ref, out_ref, lse_ref, query, keys, value, scores
):
    count, _, rows = heads_ref.shape
    total = count * rows
    load_heads(scalars[0], heads_ref, query, keys, count, rows)
    for i in range(count):
        value[:, i * rows : (i + 1) * rows] = heads_ref[i, 2 * HD : 3 * HD, :]

    def one_block(block, carry):
        cols = pl.ds(pl.multiple_of(block * QB, QB), QB)
        query_cols = query[:, cols]
        peak = None
        for k in range(total // KB):
            part = dot(keys[k * KB : (k + 1) * KB, :], query_cols)
            scores[k * KB : (k + 1) * KB, :] = part
            top = jnp.max(part.reshape(KB // 8, 8, QB), axis=0)
            peak = top if peak is None else jnp.maximum(peak, top)
        peak = jnp.max(peak, axis=0, keepdims=True)
        total_row = jnp.zeros((8, QB), F32)
        acc = jnp.zeros((HD, QB), F32)
        for k in range(total // KB):
            expo = jnp.exp(scores[k * KB : (k + 1) * KB, :] - peak)
            total_row = total_row + jnp.sum(expo.reshape(KB // 8, 8, QB), axis=0)
            acc = acc + dot(value[:, k * KB : (k + 1) * KB], expo.astype(BF16))
        total_row = jnp.sum(total_row, axis=0, keepdims=True)
        out_ref[:, cols] = acc / total_row
        lse_ref[:, cols] = peak + jnp.log(total_row)
        return carry

    lax.fori_loop(0, total // QB, one_block, 0)
    none = jnp.zeros((HD, HALO), F32)
    for i in range(count):
        send_ref[i, 0:HD, :] = out_ref[:, i * rows : (i + 1) * rows].astype(BF16)
        low = out_ref[:, i * rows - HALO : i * rows] if i else none
        high = out_ref[:, (i + 1) * rows : (i + 1) * rows + HALO] if i < count - 1 else none
        sides = jnp.concatenate([low, high], axis=1)
        packed = jnp.concatenate([sides[0 : HD // 2], sides[HD // 2 :]], axis=1)
        send_ref[i, HD : HD + HD // 2, :] = packed.astype(BF16)


def attend(scalars, heads):
    count, _, rows = heads.shape
    total = count * rows
    return pl.pallas_call(
        attend_kernel,
        in_specs=[SMEM, pl.BlockSpec(memory_space=pltpu.VMEM)],
        out_shape=[
            jax.ShapeDtypeStruct((count, HD + HD // 2, rows), BF16),
            jax.ShapeDtypeStruct((HD, total), F32),
            jax.ShapeDtypeStruct((1, total), F32),
        ],
        scratch_shapes=[
            pltpu.VMEM((2 * HD, total), BF16),
            pltpu.VMEM((total, 2 * HD), BF16),
            pltpu.VMEM((HD, total), BF16),
            pltpu.VMEM((total, QB), F32),
        ],
        compiler_params=params(),
        cost_estimate=cost(2 * 2 * total * total * 256, heads.size * 2, total * total),
        name="attend",
    )(scalars, heads)


def middle_kernel(
    scalars,
    att_ref,
    frames_ref,
    frames_side,
    grads_ref,
    grads_side,
    w_out_ref,
    w_conv_ref,
    output_ref,
    res_grad_ref,
    round_ref,
    send_ref,
    taps_ref,
    conv_in,
    grad_all,
    residual,
    window,
    window_back,
    conv_grad,
):
    rows, width = frames_ref.shape
    heads = att_ref.shape[0]
    length = scalars[0]
    first = scalars[1]
    zero = scalars[2]
    half = HD // 2
    body = slice(HALO, HALO + rows)

    attended = att_ref[:, 0:HD, :].reshape(width, rows).T
    main = frames_ref[...].astype(F32) + dot(attended, w_out_ref[...])
    packed = att_ref[:, HD : HD + half, :].reshape(heads * half, rows).T
    split_w = w_out_ref[...].reshape(heads, 2, half, width)
    side = dot(packed[0 : 2 * HALO], split_w[:, 0].reshape(heads * half, width))
    side = side + dot(packed[2 * HALO :], split_w[:, 1].reshape(heads * half, width))
    side = frames_side[...].astype(F32) + side

    def keep_of(count, start):
        frame = lax.broadcasted_iota(jnp.int32, (count, 1), 0) + start
        return jnp.where(jnp.logical_and(frame >= 0, frame < length), 1.0, 0.0)

    main = main.astype(BF16).astype(F32)
    residual[...] = main
    unit, scale = normalize(main)
    keep = keep_of(rows, first)
    conv_in[body, :] = (unit * keep).astype(BF16).astype(F32)
    unit_side, _ = normalize(side.astype(BF16).astype(F32))
    low = unit_side[0:HALO] * keep_of(HALO, first - HALO)
    high = unit_side[HALO:] * keep_of(HALO, first + rows)
    conv_in[0:HALO, :] = low.astype(BF16).astype(F32)
    conv_in[HALO + rows :, :] = high.astype(BF16).astype(F32)
    grad_all[0:HALO, :] = grads_side[0:HALO, :].astype(F32)
    grad_all[body, :] = grads_ref[...].astype(F32)
    grad_all[HALO + rows :, :] = grads_side[HALO:, :].astype(F32)

    reach = rows + HALO
    edge = HALO // 2

    def one_chunk(chunk, carry):
        lanes = pl.ds(pl.multiple_of(chunk * 128, 128), 128)
        window[...] = conv_in[:, lanes]
        acc = jnp.zeros((reach, 128), F32)
        for j in range(KW):
            acc = acc + w_conv_ref[j : j + 1, lanes] * window[pl.ds(zero + (1 + j), reach), :]
        gate = jax.nn.sigmoid(acc)
        back = grad_all[edge : edge + reach, lanes] * (gate + acc * gate * (1.0 - gate))
        window_back[...] = back
        gated = acc[edge : edge + rows] * gate[edge : edge + rows]
        output_ref[:, lanes] = (residual[:, lanes] + gated).astype(BF16)
        own = window_back[edge : edge + rows, :]
        acc = jnp.zeros((rows, 128), F32)
        for j in range(KW):
            acc = acc + w_conv_ref[j : j + 1, lanes] * window_back[
                pl.ds(zero + (KW - j), rows), :
            ]
            moved = window[pl.ds(zero + (edge + 1 + j), rows), :]
            taps_ref[j : j + 1, lanes] = jnp.sum(moved * own, axis=0, keepdims=True)
        taps_ref[KW : KW + 1, lanes] = jnp.zeros((1, 128), F32)
        conv_grad[:, lanes] = acc
        return carry

    lax.fori_loop(0, width // 128, one_chunk, 0)
    res_grad = grads_ref[...].astype(F32) + normalize_back(unit, scale, conv_grad[...] * keep)
    res_grad_ref[...] = res_grad
    rounded = res_grad.astype(BF16)
    round_ref[...] = rounded
    back = dot(w_out_ref[...], rounded, 1, 1).astype(BF16)
    send_ref[:, 0:HD, :] = back.reshape(heads, HD, rows)
    for h in range(heads):
        send_ref[h, HD:, :] = halves(taps_ref[:, h * HD : (h + 1) * HD])


def middle(scalars, att, frames, frames_side, grads, grads_side, w_out, w_conv):
    rows, width = frames.shape
    vmem = pl.BlockSpec(memory_space=pltpu.VMEM)
    return pl.pallas_call(
        middle_kernel,
        in_specs=[SMEM] + [vmem] * 7,
        out_shape=[
            jax.ShapeDtypeStruct((rows, width), BF16),
            jax.ShapeDtypeStruct((rows, width), F32),
            jax.ShapeDtypeStruct((rows, width), BF16),
            jax.ShapeDtypeStruct((HEADS, HD + KW + 1, rows), BF16),
        ],
        scratch_shapes=[
            pltpu.VMEM((KW + 1, width), F32),
            pltpu.VMEM((rows + 2 * HALO, width), F32),
            pltpu.VMEM((rows + 2 * HALO, width), F32),
            pltpu.VMEM((rows, width), F32),
            pltpu.VMEM((rows + 2 * HALO, 128), F32),
            pltpu.VMEM((rows + HALO, 128), F32),
            pltpu.VMEM((rows, width), F32),
        ],
        compiler_params=params(),
        name="middle",
    )(scalars, att, frames, frames_side, grads, grads_side, w_out, w_conv)


def attend_back_kernel(
    scalars, heads_ref, grads_ref, out_ref, lse_ref, send_ref,
    query, keys, value_t, grad_t, query_rows, grad_rows, query_grad, probs, score_grads,
):
    count, _, rows = heads_ref.shape
    total = count * rows
    load_heads(scalars[0], heads_ref, query, keys, count, rows)
    for i in range(count):
        cols = slice(i * rows, (i + 1) * rows)
        block = grads_ref[i, 0:HD, :]
        grad_t[:, cols] = block
        both = jnp.concatenate([query[0:HD, cols], block], axis=0).T
        query_rows[cols, :] = both[:, 0:HD]
        grad_rows[cols, :] = both[:, HD:]
        value_t[cols, :] = heads_ref[i, 2 * HD : 3 * HD, :].T
    query_grad[...] = jnp.zeros_like(query_grad)
    lse = lse_ref[...]
    delta = jnp.sum(grad_t[...].astype(F32) * out_ref[...], axis=0, keepdims=True)

    def one_block(block, carry):
        span = pl.ds(pl.multiple_of(block * KB, KB), KB)
        key_rows = keys[span, :]
        value_rows = value_t[span, :]
        for q in range(total // QB):
            cols = slice(q * QB, (q + 1) * QB)
            prob = jnp.exp(dot(key_rows, query[:, cols]) - lse[:, cols])
            prob_grad = dot(value_rows, grad_t[:, cols])
            probs[:, cols] = prob.astype(BF16)
            score_grads[:, cols] = (prob * (prob_grad - delta[:, cols])).astype(BF16)
        key_grad = dot(score_grads[...], query_rows[...])
        value_grad = dot(probs[...], grad_rows[...])
        key_cols = key_rows[:, 0:HD].T
        query_grad[...] += dot(key_cols, score_grads[...])
        joined = jnp.concatenate([key_grad, value_grad], axis=1).T.astype(BF16)
        for i in range(KB // rows):
            send_ref[block * (KB // rows) + i, HD : 3 * HD, :] = joined[:, i * rows : (i + 1) * rows]
        return carry

    lax.fori_loop(0, total // KB, one_block, 0)
    for i in range(count):
        cols = slice(i * rows, (i + 1) * rows)
        send_ref[i, 0:HD, :] = (query_grad[:, cols] * 0.125).astype(BF16)


def attend_back(scalars, heads, grads, out, lse):
    count, _, rows = heads.shape
    total = count * rows
    vmem = pl.BlockSpec(memory_space=pltpu.VMEM)
    return pl.pallas_call(
        attend_back_kernel,
        in_specs=[SMEM] + [vmem] * 4,
        out_shape=jax.ShapeDtypeStruct(heads.shape, BF16),
        scratch_shapes=[
            pltpu.VMEM((2 * HD, total), BF16),
            pltpu.VMEM((total, 2 * HD), BF16),
            pltpu.VMEM((total, HD), BF16),
            pltpu.VMEM((HD, total), BF16),
            pltpu.VMEM((total, HD), BF16),
            pltpu.VMEM((total, HD), BF16),
            pltpu.VMEM((HD, total), F32),
            pltpu.VMEM((KB, total), BF16),
            pltpu.VMEM((KB, total), BF16),
        ],
        compiler_params=params(),
        cost_estimate=cost(5 * 2 * total * total * 256, heads.size * 4, total * total),
        name="attend_back",
    )(scalars, heads, grads, out, lse)


def input_grad_kernel(joined_ref, weight_ref, frames_ref, res_grad_ref, out_ref, joined, grads):
    step = pl.program_id(0)
    heads = joined_ref.shape[0]

    @pl.when(step == 0)
    def _():
        for h in range(heads):
            for t in range(3):
                row = (t * heads + h) * HD
                joined[row : row + HD, :] = joined_ref[h, t * HD : (t + 1) * HD, :]

    block = weight_ref.shape[0]
    start = pl.multiple_of(step * block, block)
    grads[pl.ds(start, block), :] = dot(weight_ref[...], joined[...])

    @pl.when(step == pl.num_programs(0) - 1)
    def _():
        unit, scale = normalize(frames_ref[...].astype(F32))
        back = normalize_back(unit, scale, grads[...].T)
        out_ref[...] = (res_grad_ref[...] + back).astype(BF16)


def input_gradient(joined, w_qkv, frames, res_grad):
    rows, width = frames.shape
    block = 256
    return pl.pallas_call(
        input_grad_kernel,
        grid=(width // block,),
        in_specs=[
            whole(joined.shape),
            pl.BlockSpec((block, w_qkv.shape[1]), lambda j: (j, 0)),
            whole(frames.shape),
            whole(frames.shape),
        ],
        out_specs=whole(frames.shape),
        out_shape=jax.ShapeDtypeStruct(frames.shape, BF16),
        scratch_shapes=[
            pltpu.VMEM((w_qkv.shape[1], rows), BF16),
            pltpu.VMEM((width, rows), F32),
        ],
        compiler_params=params(),
        name="input_gradient",
    )(joined, w_qkv, frames, res_grad)


CUT = 96
FAST = 4
SLOW = 4
TAPS = SLOW * CUT
OUT = 8 * HD


def out_part_kernel(scalars, att_ref, round_ref, *send_refs):
    lanes = send_refs[0].shape[2]
    for k, send_ref in enumerate(send_refs):
        part = dot(att_ref[scalars[3] ^ k, 0:HD, :], round_ref[...])
        for c in range(part.shape[1] // lanes):
            piece = part[:, c * lanes : (c + 1) * lanes]
            send_ref[0, c * HD : (c + 1) * HD, :] = piece.astype(BF16)


def out_part(scalars, att, rounded):
    heads, wide, rows = att.shape
    return pl.pallas_call(
        out_part_kernel,
        grid=(SLOW,),
        in_specs=[
            SMEM,
            pl.BlockSpec((FAST, wide, rows), lambda j: (j, 0, 0)),
            whole(rounded.shape),
        ],
        out_specs=[pl.BlockSpec((1, OUT, 128), lambda j: (j, 0, 0))] * FAST,
        out_shape=[jax.ShapeDtypeStruct((SLOW, OUT, 128), BF16)] * FAST,
        compiler_params=params(),
        cost_estimate=cost(2 * heads * HD * 256 * rounded.shape[1], heads * HD * rounded.shape[1] * 2),
        name="out_part",
    )(scalars, att, rounded)


def parts_kernel(scalars, grads_ref, back_ref, normed_ref, *rest):
    send_refs, columns, pieces = rest[:FAST], rest[FAST], rest[FAST + 1]
    count, wide, rows = grads_ref.shape
    slow = pl.program_id(0)

    @pl.when(slow == 0)
    def _():
        taps = jnp.zeros((KW + 1, rows), F32)
        for i in range(count):
            columns[:, i * rows : (i + 1) * rows] = grads_ref[i]
            taps = taps + back_ref[i, HD:, :].astype(F32)
        pair = halves(joined_halves(taps))
        for send_ref in send_refs:
            send_ref[TAPS:, :] = pair

    part = dot(columns[...], normed_ref[...])
    each = part.shape[1] // FAST
    for i in range(FAST):
        piece = part[:, i * each : (i + 1) * each]
        pieces[i] = jnp.concatenate([piece[0:CUT], piece[CUT:]], axis=1).astype(BF16)
    for k, send_ref in enumerate(send_refs):
        send_ref[pl.ds(pl.multiple_of(slow * CUT, CUT), CUT), :] = pieces[scalars[3] ^ k]


def gradient_parts(scalars, grads, back, normed_all):
    count, wide, rows = grads.shape
    total, width = normed_all.shape
    return pl.pallas_call(
        parts_kernel,
        grid=(SLOW,),
        in_specs=[
            SMEM,
            whole(grads.shape),
            whole(back.shape),
            pl.BlockSpec((total, width // SLOW), lambda j: (0, j)),
        ],
        out_specs=[whole((TAPS + KW + 1, 128))] * FAST,
        out_shape=[jax.ShapeDtypeStruct((TAPS + KW + 1, 128), BF16)] * FAST,
        scratch_shapes=[pltpu.VMEM((wide, total), BF16), pltpu.VMEM((FAST, CUT, 128), BF16)],
        compiler_params=params(),
        cost_estimate=cost(2 * 256 * total * width, total * width * 2),
        name="gradient_parts",
    )(scalars, grads, back, normed_all)


def sum_four(own, one, two, three):
    return (own.astype(F32) + one.astype(F32)) + (two.astype(F32) + three.astype(F32))


def fold_out_kernel(scalars, one, two, three, four, *send_refs):
    for k, send_ref in enumerate(send_refs):
        i = scalars[4] ^ k
        send_ref[...] = sum_four(one[i], two[i], three[i], four[i]).astype(BF16)


def fold_out(scalars, blocks):
    vmem = pl.BlockSpec(memory_space=pltpu.VMEM)
    return pl.pallas_call(
        fold_out_kernel,
        in_specs=[SMEM] + [vmem] * 4,
        out_shape=[jax.ShapeDtypeStruct((OUT, 128), BF16)] * SLOW,
        compiler_params=params(),
        cost_estimate=cost(0, 5 * SLOW * OUT * 128 * 2),
        name="fold_out",
    )(scalars, *blocks)


def fold_fast_kernel(scalars, one, two, three, four, *rest):
    send_refs, pieces = rest[:SLOW], rest[SLOW]
    total = sum_four(one[...], two[...], three[...], four[...])
    pair = halves(joined_halves(total[TAPS:]))
    for i in range(SLOW):
        pieces[i] = total[i * CUT : (i + 1) * CUT].astype(BF16)
    for k, send_ref in enumerate(send_refs):
        send_ref[0:CUT, :] = pieces[scalars[4] ^ k]
        send_ref[CUT:, :] = pair


def fold_fast(scalars, blocks):
    vmem = pl.BlockSpec(memory_space=pltpu.VMEM)
    return pl.pallas_call(
        fold_fast_kernel,
        in_specs=[SMEM] + [vmem] * 4,
        out_shape=[jax.ShapeDtypeStruct((CUT + KW + 1, 128), BF16)] * SLOW,
        scratch_shapes=[pltpu.VMEM((SLOW, CUT, 128), BF16)],
        compiler_params=params(),
        name="fold_fast",
    )(scalars, *blocks)


def fold_slow_kernel(*refs, scale):
    qkv_ref, send_ref = refs[8:]
    total = sum_four(*(ref[...] for ref in refs[0:4]))
    model_rows = (total[0:CUT] * scale).T
    qkv_ref[:, 0:CUT] = model_rows[0:HD]
    qkv_ref[:, CUT:] = model_rows[HD:]
    pair = halves(joined_halves(total[CUT:]))
    outer = sum_four(*(ref[...] for ref in refs[4:8]))
    count = send_ref.shape[0]
    each = HD // count
    for i in range(count):
        pieces = [outer[c * HD + i * each : c * HD + (i + 1) * each] for c in range(OUT // HD)]
        send_ref[i, 0 : OUT // count, :] = jnp.concatenate(pieces, axis=0).astype(BF16)
        send_ref[i, OUT // count :, :] = pair


def fold_slow(blocks, out_blocks, seq_count, scale):
    vmem = pl.BlockSpec(memory_space=pltpu.VMEM)
    return pl.pallas_call(
        lambda *refs: fold_slow_kernel(*refs, scale=scale),
        in_specs=[vmem] * 8,
        out_shape=[
            jax.ShapeDtypeStruct((HD, 3 * HD), F32),
            jax.ShapeDtypeStruct((seq_count, OUT // seq_count + KW + 1, 128), BF16),
        ],
        compiler_params=params(),
        name="fold_slow",
    )(*blocks, *out_blocks)


def finish_kernel(recv_ref, out_ref, taps_ref, *, scale):
    count = recv_ref.shape[0]
    each = out_ref.shape[0]
    wide = OUT // count
    total = recv_ref[0, 0:wide, :].astype(F32)
    for i in range(1, count):
        total = total + recv_ref[i, 0:wide, :].astype(F32)
    total = total * scale
    for c in range(OUT // HD):
        out_ref[:, c * 128 : (c + 1) * 128] = total[c * each : (c + 1) * each]
    for i in range(count // 2):
        both = [joined_halves(recv_ref[2 * i + k, wide:, :].astype(F32)) for k in range(2)]
        both = jnp.concatenate(both, axis=1) * scale
        taps_ref[:, i * 2 * HD : (i + 1) * 2 * HD] = both[0:KW]


def finish(recv, width, scale):
    count = recv.shape[0]
    vmem = pl.BlockSpec(memory_space=pltpu.VMEM)
    return pl.pallas_call(
        lambda *refs: finish_kernel(*refs, scale=scale),
        in_specs=[vmem],
        out_shape=[
            jax.ShapeDtypeStruct((HD // count, width), F32),
            jax.ShapeDtypeStruct((KW, width), F32),
        ],
        compiler_params=params(),
        name="finish",
    )(recv)


def exchange(blocks, step):
    pairs = lambda k: [(d, d ^ (step * k)) for d in range(FAST * SLOW)]
    moved = [lax.ppermute(block, "dp", pairs(k)) for k, block in enumerate(blocks) if k]
    return [blocks[0]] + moved


def local(frames, cotangent, w_qkv, w_out, w_conv, lengths):
    seq_count = lax.axis_size("seq")
    data_count = lax.axis_size("dp")
    rows, width = frames.shape[1:]
    first = lax.axis_index("seq") * rows
    grad_scale = 1.0 / math.sqrt(data_count * rows * seq_count)
    position = lax.axis_index("dp")
    fast = position % FAST
    slow = position // FAST
    scalars = jnp.stack([lengths[0], first, jnp.zeros((), jnp.int32), fast, slow])
    x = frames[0]
    g = cotangent[0]

    forward = [(i, i + 1) for i in range(seq_count - 1)]
    backward = [(i + 1, i) for i in range(seq_count - 1)]
    low = lax.ppermute(jnp.concatenate([x[-HALO:], g[-HALO:]], axis=0), "seq", forward)
    high = lax.ppermute(jnp.concatenate([x[:HALO], g[:HALO]], axis=0), "seq", backward)
    x_side = jnp.concatenate([low[:HALO], high[:HALO]], axis=0)
    g_side = jnp.concatenate([low[HALO:], high[HALO:]], axis=0)

    normed, send = project(x, w_qkv)
    heads = lax.all_to_all(send, "seq", 0, 0, tiled=True)
    normed_all = lax.all_gather(normed, "seq", axis=0, tiled=True)
    send, out, lse = attend(scalars, heads)
    att = lax.all_to_all(send, "seq", 0, 0, tiled=True)
    output, res_grad, rounded, send = middle(scalars, att, x, x_side, g, g_side, w_out, w_conv)
    back = lax.all_to_all(send, "seq", 0, 0, tiled=True)
    outer = out_part(scalars, att, rounded)
    back, outer = lax.optimization_barrier((back, outer))
    outer = exchange(outer, 1)
    send = attend_back(scalars, heads, back, out, lse)
    joined = lax.all_to_all(send, "seq", 0, 0, tiled=True)
    parts = exchange(gradient_parts(scalars, send, back, normed_all), 1)
    outer = exchange(fold_out(scalars, outer), FAST)
    parts = exchange(fold_fast(scalars, parts), FAST)
    qkv, send = fold_slow(parts, outer, seq_count, grad_scale)
    input_grad = input_gradient(joined, w_qkv, x, res_grad)
    recv = lax.all_to_all(send, "seq", 0, 0, tiled=True)
    out_total, taps_total = finish(recv, width, grad_scale)
    return (
        output[None],
        input_grad[None],
        qkv.reshape(width // data_count, 3, HD),
        out_total,
        taps_total,
    )


def solution(mesh):
    placed = (P("dp", "seq", None), P("dp", "seq", None), P(), P(), P(), P("dp"))
    return jax.shard_map(
        local,
        mesh=mesh,
        in_specs=placed,
        out_specs=(
            P("dp", "seq", None),
            P("dp", "seq", None),
            P("dp", None, "seq"),
            P(("dp", "seq"), None),
            P(),
        ),
        check_vma=False,
    )
```

```python
import math

import jax
import jax.numpy as jnp
from jax import lax
from jax.experimental import pallas as pl
from jax.experimental.pallas import tpu as pltpu
from jax.sharding import PartitionSpec as P

HEADS = 16
KW = 31
HD = 64
HALO = 32
QB = 256
KB = 256
F32 = jnp.float32
BF16 = jnp.bfloat16
LIMIT = 56 * 1024 * 1024


def dot(a, b, ca=1, cb=0):
    return lax.dot_general(a, b, (((ca,), (cb,)), ((), ())), preferred_element_type=F32)


def normalize(rows):
    center = rows - jnp.mean(rows, axis=-1, keepdims=True)
    scale = lax.rsqrt(jnp.mean(center * center, axis=-1, keepdims=True) + 1e-05)
    return center * scale, scale


def normalize_back(unit, scale, upstream):
    return scale * (
        upstream
        - jnp.mean(upstream, axis=-1, keepdims=True)
        - unit * jnp.mean(upstream * unit, axis=-1, keepdims=True)
    )


def params(**kw):
    return pltpu.CompilerParams(vmem_limit_bytes=LIMIT, **kw)


def cost(flops, moved, expos=0):
    return pl.CostEstimate(flops=flops, bytes_accessed=moved, transcendentals=expos)


def whole(shape):
    return pl.BlockSpec(shape, lambda *_: (0,) * len(shape))


def halves(exact):
    top = exact.astype(BF16)
    rest = (exact - top.astype(F32)).astype(BF16)
    return jnp.concatenate([top, rest], axis=1)


def joined_halves(pair):
    return pair[:, : pair.shape[1] // 2] + pair[:, pair.shape[1] // 2 :]


SMEM = pl.BlockSpec(memory_space=pltpu.SMEM)


def project_kernel(frames_ref, weight_ref, normed_ref, send_ref):
    @pl.when(pl.program_id(0) == 0)
    def _():
        unit, _ = normalize(frames_ref[...].astype(F32))
        normed_ref[...] = unit.astype(BF16)

    part = dot(normed_ref[...], weight_ref[...]).astype(BF16)
    send_ref[...] = part.T.reshape(send_ref.shape)


def project(frames, w_qkv):
    rows, width = frames.shape
    cols = 512
    per = cols // HD
    groups = HEADS // per
    return pl.pallas_call(
        project_kernel,
        grid=(3 * groups,),
        in_specs=[whole(frames.shape), pl.BlockSpec((width, cols), lambda j: (0, j))],
        out_specs=[
            whole(frames.shape),
            pl.BlockSpec((per, HD, rows), lambda j: (j % groups, j // groups, 0)),
        ],
        out_shape=[
            jax.ShapeDtypeStruct(frames.shape, BF16),
            jax.ShapeDtypeStruct((HEADS, 3 * HD, rows), BF16),
        ],
        compiler_params=params(),
        name="project",
    )(frames, w_qkv)


def load_heads(length, heads_ref, query, keys, count, rows):
    extra = lax.broadcasted_iota(jnp.int32, (HD, rows), 0)
    frame = lax.broadcasted_iota(jnp.int32, (HD, rows), 1)
    for i in range(count):
        cols = slice(i * rows, (i + 1) * rows)
        query[0:HD, cols] = (heads_ref[i, 0:HD, :].astype(F32) * 0.125).astype(BF16)
        query[HD : 2 * HD, cols] = jnp.where(extra == 0, 1.0, 0.0).astype(BF16)
        masked = jnp.logical_and(extra == 0, frame + i * rows >= length)
        mask = jnp.where(masked, -1e30, 0.0).astype(BF16)
        joined = jnp.concatenate([heads_ref[i, HD : 2 * HD, :], mask], axis=0)
        keys[cols, :] = joined.T


def attend_kernel(
    scalars, heads_ref, send_ref, out_ref, lse_ref, query, keys, value, scores
):
    count, _, rows = heads_ref.shape
    total = count * rows
    load_heads(scalars[0], heads_ref, query, keys, count, rows)
    for i in range(count):
        value[:, i * rows : (i + 1) * rows] = heads_ref[i, 2 * HD : 3 * HD, :]

    def one_block(block, carry):
        cols = pl.ds(pl.multiple_of(block * QB, QB), QB)
        query_cols = query[:, cols]
        peak = None
        for k in range(total // KB):
            part = dot(keys[k * KB : (k + 1) * KB, :], query_cols)
            scores[k * KB : (k + 1) * KB, :] = part
            top = jnp.max(part.reshape(KB // 8, 8, QB), axis=0)
            peak = top if peak is None else jnp.maximum(peak, top)
        peak = jnp.max(peak, axis=0, keepdims=True)
        total_row = jnp.zeros((8, QB), F32)
        acc = jnp.zeros((HD, QB), F32)
        for k in range(total // KB):
            expo = jnp.exp(scores[k * KB : (k + 1) * KB, :] - peak)
            total_row = total_row + jnp.sum(expo.reshape(KB // 8, 8, QB), axis=0)
            acc = acc + dot(value[:, k * KB : (k + 1) * KB], expo.astype(BF16))
        total_row = jnp.sum(total_row, axis=0, keepdims=True)
        out_ref[:, cols] = acc / total_row
        lse_ref[:, cols] = peak + jnp.log(total_row)
        return carry

    lax.fori_loop(0, total // QB, one_block, 0)
    none = jnp.zeros((HD, HALO), F32)
    for i in range(count):
        send_ref[i, 0:HD, :] = out_ref[:, i * rows : (i + 1) * rows].astype(BF16)
        low = out_ref[:, i * rows - HALO : i * rows] if i else none
        high = out_ref[:, (i + 1) * rows : (i + 1) * rows + HALO] if i < count - 1 else none
        sides = jnp.concatenate([low, high], axis=1)
        packed = jnp.concatenate([sides[0 : HD // 2], sides[HD // 2 :]], axis=1)
        send_ref[i, HD : HD + HD // 2, :] = packed.astype(BF16)


def attend(scalars, heads):
    count, _, rows = heads.shape
    total = count * rows
    return pl.pallas_call(
        attend_kernel,
        in_specs=[SMEM, pl.BlockSpec(memory_space=pltpu.VMEM)],
        out_shape=[
            jax.ShapeDtypeStruct((count, HD + HD // 2, rows), BF16),
            jax.ShapeDtypeStruct((HD, total), F32),
            jax.ShapeDtypeStruct((1, total), F32),
        ],
        scratch_shapes=[
            pltpu.VMEM((2 * HD, total), BF16),
            pltpu.VMEM((total, 2 * HD), BF16),
            pltpu.VMEM((HD, total), BF16),
            pltpu.VMEM((total, QB), F32),
        ],
        compiler_params=params(),
        cost_estimate=cost(2 * 2 * total * total * 256, heads.size * 2, total * total),
        name="attend",
    )(scalars, heads)


def middle_kernel(
    scalars,
    att_ref,
    frames_ref,
    frames_side,
    grads_ref,
    grads_side,
    w_out_ref,
    w_conv_ref,
    output_ref,
    res_grad_ref,
    round_ref,
    send_ref,
    taps_ref,
    conv_in,
    grad_all,
    residual,
    window,
    window_back,
    conv_grad,
):
    rows, width = frames_ref.shape
    heads = att_ref.shape[0]
    length = scalars[0]
    first = scalars[1]
    zero = scalars[2]
    half = HD // 2
    body = slice(HALO, HALO + rows)

    attended = att_ref[:, 0:HD, :].reshape(width, rows).T
    main = frames_ref[...].astype(F32) + dot(attended, w_out_ref[...])
    packed = att_ref[:, HD : HD + half, :].reshape(heads * half, rows).T
    split_w = w_out_ref[...].reshape(heads, 2, half, width)
    side = dot(packed[0 : 2 * HALO], split_w[:, 0].reshape(heads * half, width))
    side = side + dot(packed[2 * HALO :], split_w[:, 1].reshape(heads * half, width))
    side = frames_side[...].astype(F32) + side

    def keep_of(count, start):
        frame = lax.broadcasted_iota(jnp.int32, (count, 1), 0) + start
        return jnp.where(jnp.logical_and(frame >= 0, frame < length), 1.0, 0.0)

    main = main.astype(BF16).astype(F32)
    residual[...] = main
    unit, scale = normalize(main)
    keep = keep_of(rows, first)
    conv_in[body, :] = (unit * keep).astype(BF16).astype(F32)
    unit_side, _ = normalize(side.astype(BF16).astype(F32))
    low = unit_side[0:HALO] * keep_of(HALO, first - HALO)
    high = unit_side[HALO:] * keep_of(HALO, first + rows)
    conv_in[0:HALO, :] = low.astype(BF16).astype(F32)
    conv_in[HALO + rows :, :] = high.astype(BF16).astype(F32)
    grad_all[0:HALO, :] = grads_side[0:HALO, :].astype(F32)
    grad_all[body, :] = grads_ref[...].astype(F32)
    grad_all[HALO + rows :, :] = grads_side[HALO:, :].astype(F32)

    reach = rows + HALO
    edge = HALO // 2

    def one_chunk(chunk, carry):
        lanes = pl.ds(pl.multiple_of(chunk * 128, 128), 128)
        window[...] = conv_in[:, lanes]
        acc = jnp.zeros((reach, 128), F32)
        for j in range(KW):
            acc = acc + w_conv_ref[j : j + 1, lanes] * window[pl.ds(zero + (1 + j), reach), :]
        gate = jax.nn.sigmoid(acc)
        back = grad_all[edge : edge + reach, lanes] * (gate + acc * gate * (1.0 - gate))
        window_back[...] = back
        gated = acc[edge : edge + rows] * gate[edge : edge + rows]
        output_ref[:, lanes] = (residual[:, lanes] + gated).astype(BF16)
        own = window_back[edge : edge + rows, :]
        acc = jnp.zeros((rows, 128), F32)
        for j in range(KW):
            acc = acc + w_conv_ref[j : j + 1, lanes] * window_back[
                pl.ds(zero + (KW - j), rows), :
            ]
            moved = window[pl.ds(zero + (edge + 1 + j), rows), :]
            taps_ref[j : j + 1, lanes] = jnp.sum(moved * own, axis=0, keepdims=True)
        taps_ref[KW : KW + 1, lanes] = jnp.zeros((1, 128), F32)
        conv_grad[:, lanes] = acc
        return carry

    lax.fori_loop(0, width // 128, one_chunk, 0)
    res_grad = grads_ref[...].astype(F32) + normalize_back(unit, scale, conv_grad[...] * keep)
    res_grad_ref[...] = res_grad
    rounded = res_grad.astype(BF16)
    round_ref[...] = rounded
    back = dot(w_out_ref[...], rounded, 1, 1).astype(BF16)
    send_ref[:, 0:HD, :] = back.reshape(heads, HD, rows)
    for h in range(heads):
        send_ref[h, HD:, :] = halves(taps_ref[:, h * HD : (h + 1) * HD])


def middle(scalars, att, frames, frames_side, grads, grads_side, w_out, w_conv):
    rows, width = frames.shape
    vmem = pl.BlockSpec(memory_space=pltpu.VMEM)
    return pl.pallas_call(
        middle_kernel,
        in_specs=[SMEM] + [vmem] * 7,
        out_shape=[
            jax.ShapeDtypeStruct((rows, width), BF16),
            jax.ShapeDtypeStruct((rows, width), F32),
            jax.ShapeDtypeStruct((rows, width), BF16),
            jax.ShapeDtypeStruct((HEADS, HD + KW + 1, rows), BF16),
        ],
        scratch_shapes=[
            pltpu.VMEM((KW + 1, width), F32),
            pltpu.VMEM((rows + 2 * HALO, width), F32),
            pltpu.VMEM((rows + 2 * HALO, width), F32),
            pltpu.VMEM((rows, width), F32),
            pltpu.VMEM((rows + 2 * HALO, 128), F32),
            pltpu.VMEM((rows + HALO, 128), F32),
            pltpu.VMEM((rows, width), F32),
        ],
        compiler_params=params(),
        name="middle",
    )(scalars, att, frames, frames_side, grads, grads_side, w_out, w_conv)


def attend_back_kernel(
    scalars, heads_ref, grads_ref, out_ref, lse_ref, send_ref,
    query, keys, value_t, grad_t, query_rows, grad_rows, query_grad, probs, score_grads,
):
    count, _, rows = heads_ref.shape
    total = count * rows
    load_heads(scalars[0], heads_ref, query, keys, count, rows)
    for i in range(count):
        cols = slice(i * rows, (i + 1) * rows)
        block = grads_ref[i, 0:HD, :]
        grad_t[:, cols] = block
        both = jnp.concatenate([query[0:HD, cols], block], axis=0).T
        query_rows[cols, :] = both[:, 0:HD]
        grad_rows[cols, :] = both[:, HD:]
        value_t[cols, :] = heads_ref[i, 2 * HD : 3 * HD, :].T
    query_grad[...] = jnp.zeros_like(query_grad)
    lse = lse_ref[...]
    delta = jnp.sum(grad_t[...].astype(F32) * out_ref[...], axis=0, keepdims=True)

    def one_block(block, carry):
        span = pl.ds(pl.multiple_of(block * KB, KB), KB)
        key_rows = keys[span, :]
        value_rows = value_t[span, :]
        for q in range(total // QB):
            cols = slice(q * QB, (q + 1) * QB)
            prob = jnp.exp(dot(key_rows, query[:, cols]) - lse[:, cols])
            prob_grad = dot(value_rows, grad_t[:, cols])
            probs[:, cols] = prob.astype(BF16)
            score_grads[:, cols] = (prob * (prob_grad - delta[:, cols])).astype(BF16)
        key_grad = dot(score_grads[...], query_rows[...])
        value_grad = dot(probs[...], grad_rows[...])
        key_cols = key_rows[:, 0:HD].T
        query_grad[...] += dot(key_cols, score_grads[...])
        joined = jnp.concatenate([key_grad, value_grad], axis=1).T.astype(BF16)
        for i in range(KB // rows):
            send_ref[block * (KB // rows) + i, HD : 3 * HD, :] = joined[:, i * rows : (i + 1) * rows]
        return carry

    lax.fori_loop(0, total // KB, one_block, 0)
    for i in range(count):
        cols = slice(i * rows, (i + 1) * rows)
        send_ref[i, 0:HD, :] = (query_grad[:, cols] * 0.125).astype(BF16)


def attend_back(scalars, heads, grads, out, lse):
    count, _, rows = heads.shape
    total = count * rows
    vmem = pl.BlockSpec(memory_space=pltpu.VMEM)
    return pl.pallas_call(
        attend_back_kernel,
        in_specs=[SMEM] + [vmem] * 4,
        out_shape=jax.ShapeDtypeStruct(heads.shape, BF16),
        scratch_shapes=[
            pltpu.VMEM((2 * HD, total), BF16),
            pltpu.VMEM((total, 2 * HD), BF16),
            pltpu.VMEM((total, HD), BF16),
            pltpu.VMEM((HD, total), BF16),
            pltpu.VMEM((total, HD), BF16),
            pltpu.VMEM((total, HD), BF16),
            pltpu.VMEM((HD, total), F32),
            pltpu.VMEM((KB, total), BF16),
            pltpu.VMEM((KB, total), BF16),
        ],
        compiler_params=params(),
        cost_estimate=cost(5 * 2 * total * total * 256, heads.size * 4, total * total),
        name="attend_back",
    )(scalars, heads, grads, out, lse)


def input_grad_kernel(joined_ref, weight_ref, frames_ref, res_grad_ref, out_ref, joined, grads):
    step = pl.program_id(0)
    heads = joined_ref.shape[0]

    @pl.when(step == 0)
    def _():
        for h in range(heads):
            for t in range(3):
                row = (t * heads + h) * HD
                joined[row : row + HD, :] = joined_ref[h, t * HD : (t + 1) * HD, :]

    block = weight_ref.shape[0]
    start = pl.multiple_of(step * block, block)
    grads[pl.ds(start, block), :] = dot(weight_ref[...], joined[...])

    @pl.when(step == pl.num_programs(0) - 1)
    def _():
        unit, scale = normalize(frames_ref[...].astype(F32))
        back = normalize_back(unit, scale, grads[...].T)
        out_ref[...] = (res_grad_ref[...] + back).astype(BF16)


def input_gradient(joined, w_qkv, frames, res_grad):
    rows, width = frames.shape
    block = 256
    return pl.pallas_call(
        input_grad_kernel,
        grid=(width // block,),
        in_specs=[
            whole(joined.shape),
            pl.BlockSpec((block, w_qkv.shape[1]), lambda j: (j, 0)),
            whole(frames.shape),
            whole(frames.shape),
        ],
        out_specs=whole(frames.shape),
        out_shape=jax.ShapeDtypeStruct(frames.shape, BF16),
        scratch_shapes=[
            pltpu.VMEM((w_qkv.shape[1], rows), BF16),
            pltpu.VMEM((width, rows), F32),
        ],
        compiler_params=params(),
        name="input_gradient",
    )(joined, w_qkv, frames, res_grad)


CUT = 96
FAST = 4
SLOW = 4
TAPS = SLOW * CUT
OUT = 8 * HD


def out_part_kernel(att_ref, round_ref, send_ref):
    fast, _, _, lanes = send_ref.shape
    rows = att_ref.shape[2]
    part = dot(att_ref[:, 0:HD, :].reshape(fast * HD, rows), round_ref[...])
    for i in range(fast):
        for c in range(part.shape[1] // lanes):
            piece = part[i * HD : (i + 1) * HD, c * lanes : (c + 1) * lanes]
            send_ref[i, 0, c * HD : (c + 1) * HD, :] = piece.astype(BF16)


def out_part(att, rounded):
    heads, wide, rows = att.shape
    return pl.pallas_call(
        out_part_kernel,
        grid=(SLOW,),
        in_specs=[
            pl.BlockSpec((FAST, wide, rows), lambda j: (j, 0, 0)),
            whole(rounded.shape),
        ],
        out_specs=pl.BlockSpec((FAST, 1, OUT, 128), lambda j: (0, j, 0, 0)),
        out_shape=jax.ShapeDtypeStruct((FAST, SLOW, OUT, 128), BF16),
        compiler_params=params(),
        cost_estimate=cost(2 * heads * HD * 256 * rounded.shape[1], heads * HD * rounded.shape[1] * 2),
        name="out_part",
    )(att, rounded)


def parts_kernel(scalars, grads_ref, back_ref, normed_ref, *rest):
    send_refs, columns, pieces = rest[:FAST], rest[FAST], rest[FAST + 1]
    count, wide, rows = grads_ref.shape
    slow = pl.program_id(0)

    @pl.when(slow == 0)
    def _():
        taps = jnp.zeros((KW + 1, rows), F32)
        for i in range(count):
            columns[:, i * rows : (i + 1) * rows] = grads_ref[i]
            taps = taps + back_ref[i, HD:, :].astype(F32)
        pair = halves(joined_halves(taps))
        for send_ref in send_refs:
            send_ref[TAPS:, :] = pair

    part = dot(columns[...], normed_ref[...])
    each = part.shape[1] // FAST
    for i in range(FAST):
        piece = part[:, i * each : (i + 1) * each]
        pieces[i] = jnp.concatenate([piece[0:CUT], piece[CUT:]], axis=1).astype(BF16)
    for k, send_ref in enumerate(send_refs):
        send_ref[pl.ds(pl.multiple_of(slow * CUT, CUT), CUT), :] = pieces[scalars[3] ^ k]


def gradient_parts(scalars, grads, back, normed_all):
    count, wide, rows = grads.shape
    total, width = normed_all.shape
    return pl.pallas_call(
        parts_kernel,
        grid=(SLOW,),
        in_specs=[
            SMEM,
            whole(grads.shape),
            whole(back.shape),
            pl.BlockSpec((total, width // SLOW), lambda j: (0, j)),
        ],
        out_specs=[whole((TAPS + KW + 1, 128))] * FAST,
        out_shape=[jax.ShapeDtypeStruct((TAPS + KW + 1, 128), BF16)] * FAST,
        scratch_shapes=[pltpu.VMEM((wide, total), BF16), pltpu.VMEM((FAST, CUT, 128), BF16)],
        compiler_params=params(),
        cost_estimate=cost(2 * 256 * total * width, total * width * 2),
        name="gradient_parts",
    )(scalars, grads, back, normed_all)


def sum_four(own, one, two, three):
    return (own.astype(F32) + one.astype(F32)) + (two.astype(F32) + three.astype(F32))


def fold_fast_kernel(scalars, one, two, three, four, *rest):
    send_refs, pieces = rest[:SLOW], rest[SLOW]
    total = sum_four(one[...], two[...], three[...], four[...])
    pair = halves(joined_halves(total[TAPS:]))
    for i in range(SLOW):
        pieces[i] = total[i * CUT : (i + 1) * CUT].astype(BF16)
    for k, send_ref in enumerate(send_refs):
        send_ref[0:CUT, :] = pieces[scalars[4] ^ k]
        send_ref[CUT:, :] = pair


def fold_fast(scalars, blocks):
    vmem = pl.BlockSpec(memory_space=pltpu.VMEM)
    return pl.pallas_call(
        fold_fast_kernel,
        in_specs=[SMEM] + [vmem] * 4,
        out_shape=[jax.ShapeDtypeStruct((CUT + KW + 1, 128), BF16)] * SLOW,
        scratch_shapes=[pltpu.VMEM((SLOW, CUT, 128), BF16)],
        compiler_params=params(),
        name="fold_fast",
    )(scalars, *blocks)


def fold_slow_kernel(*refs, scale):
    outer_ref, qkv_ref, send_ref = refs[4:]
    total = sum_four(*(ref[...] for ref in refs[0:4]))
    model_rows = (total[0:CUT] * scale).T
    qkv_ref[:, 0:CUT] = model_rows[0:HD]
    qkv_ref[:, CUT:] = model_rows[HD:]
    pair = halves(joined_halves(total[CUT:]))
    outer = outer_ref[0].astype(F32)
    count = send_ref.shape[0]
    each = HD // count
    for i in range(count):
        pieces = [outer[c * HD + i * each : c * HD + (i + 1) * each] for c in range(OUT // HD)]
        send_ref[i, 0 : OUT // count, :] = jnp.concatenate(pieces, axis=0).astype(BF16)
        send_ref[i, OUT // count :, :] = pair


def fold_slow(blocks, outer, seq_count, scale):
    vmem = pl.BlockSpec(memory_space=pltpu.VMEM)
    return pl.pallas_call(
        lambda *refs: fold_slow_kernel(*refs, scale=scale),
        in_specs=[vmem] * 5,
        out_shape=[
            jax.ShapeDtypeStruct((HD, 3 * HD), F32),
            jax.ShapeDtypeStruct((seq_count, OUT // seq_count + KW + 1, 128), BF16),
        ],
        compiler_params=params(),
        name="fold_slow",
    )(*blocks, outer)


def finish_kernel(recv_ref, out_ref, taps_ref, *, scale):
    count = recv_ref.shape[0]
    each = out_ref.shape[0]
    wide = OUT // count
    total = recv_ref[0, 0:wide, :].astype(F32)
    for i in range(1, count):
        total = total + recv_ref[i, 0:wide, :].astype(F32)
    total = total * scale
    for c in range(OUT // HD):
        out_ref[:, c * 128 : (c + 1) * 128] = total[c * each : (c + 1) * each]
    for i in range(count // 2):
        both = [joined_halves(recv_ref[2 * i + k, wide:, :].astype(F32)) for k in range(2)]
        both = jnp.concatenate(both, axis=1) * scale
        taps_ref[:, i * 2 * HD : (i + 1) * 2 * HD] = both[0:KW]


def finish(recv, width, scale):
    count = recv.shape[0]
    vmem = pl.BlockSpec(memory_space=pltpu.VMEM)
    return pl.pallas_call(
        lambda *refs: finish_kernel(*refs, scale=scale),
        in_specs=[vmem],
        out_shape=[
            jax.ShapeDtypeStruct((HD // count, width), F32),
            jax.ShapeDtypeStruct((KW, width), F32),
        ],
        compiler_params=params(),
        name="finish",
    )(recv)


def exchange(blocks, step):
    pairs = lambda k: [(d, d ^ (step * k)) for d in range(FAST * SLOW)]
    moved = [lax.ppermute(block, "dp", pairs(k)) for k, block in enumerate(blocks) if k]
    return [blocks[0]] + moved


def local(frames, cotangent, w_qkv, w_out, w_conv, lengths):
    seq_count = lax.axis_size("seq")
    data_count = lax.axis_size("dp")
    rows, width = frames.shape[1:]
    first = lax.axis_index("seq") * rows
    grad_scale = 1.0 / math.sqrt(data_count * rows * seq_count)
    position = lax.axis_index("dp")
    fast = position % FAST
    slow = position // FAST
    scalars = jnp.stack([lengths[0], first, jnp.zeros((), jnp.int32), fast, slow])
    x = frames[0]
    g = cotangent[0]

    forward = [(i, i + 1) for i in range(seq_count - 1)]
    backward = [(i + 1, i) for i in range(seq_count - 1)]
    low = lax.ppermute(jnp.concatenate([x[-HALO:], g[-HALO:]], axis=0), "seq", forward)
    high = lax.ppermute(jnp.concatenate([x[:HALO], g[:HALO]], axis=0), "seq", backward)
    x_side = jnp.concatenate([low[:HALO], high[:HALO]], axis=0)
    g_side = jnp.concatenate([low[HALO:], high[HALO:]], axis=0)

    normed, send = project(x, w_qkv)
    heads = lax.all_to_all(send, "seq", 0, 0, tiled=True)
    normed_all = lax.all_gather(normed, "seq", axis=0, tiled=True)
    send, out, lse = attend(scalars, heads)
    att = lax.all_to_all(send, "seq", 0, 0, tiled=True)
    output, res_grad, rounded, send = middle(scalars, att, x, x_side, g, g_side, w_out, w_conv)
    back = lax.all_to_all(send, "seq", 0, 0, tiled=True)
    near = [[FAST * i + j for j in range(FAST)] for i in range(SLOW)]
    far = [[FAST * i + j for i in range(SLOW)] for j in range(FAST)]
    outer = out_part(att, rounded)
    back, outer, normed_all = lax.optimization_barrier((back, outer, normed_all))
    outer = lax.psum_scatter(
        outer, "dp", scatter_dimension=0, axis_index_groups=near, tiled=True
    )
    send = attend_back(scalars, heads, back, out, lse)
    joined = lax.all_to_all(send, "seq", 0, 0, tiled=True)
    outer, after = lax.optimization_barrier((outer, send))
    outer = lax.psum_scatter(
        outer[0], "dp", scatter_dimension=0, axis_index_groups=far, tiled=True
    )
    parts = exchange(gradient_parts(scalars, send, back, normed_all), 1)
    parts = exchange(fold_fast(scalars, parts), FAST)
    qkv, send = fold_slow(parts, outer, seq_count, grad_scale)
    input_grad = input_gradient(joined, w_qkv, x, res_grad)
    recv = lax.all_to_all(send, "seq", 0, 0, tiled=True)
    out_total, taps_total = finish(recv, width, grad_scale)
    return (
        output[None],
        input_grad[None],
        qkv.reshape(width // data_count, 3, HD),
        out_total,
        taps_total,
    )


def solution(mesh):
    placed = (P("dp", "seq", None), P("dp", "seq", None), P(), P(), P(), P("dp"))
    return jax.shard_map(
        local,
        mesh=mesh,
        in_specs=placed,
        out_specs=(
            P("dp", "seq", None),
            P("dp", "seq", None),
            P("dp", None, "seq"),
            P(("dp", "seq"), None),
            P(),
        ),
        check_vma=False,
    )
```

```python
import math

import jax
import jax.numpy as jnp
from jax import lax
from jax.experimental import pallas as pl
from jax.experimental.pallas import tpu as pltpu
from jax.sharding import PartitionSpec as P

HEADS = 16
KW = 31
HD = 64
HALO = 32
QB = 256
KB = 256
F32 = jnp.float32
BF16 = jnp.bfloat16
LIMIT = 56 * 1024 * 1024


def dot(a, b, ca=1, cb=0):
    return lax.dot_general(a, b, (((ca,), (cb,)), ((), ())), preferred_element_type=F32)


def normalize(rows):
    center = rows - jnp.mean(rows, axis=-1, keepdims=True)
    scale = lax.rsqrt(jnp.mean(center * center, axis=-1, keepdims=True) + 1e-05)
    return center * scale, scale


def normalize_back(unit, scale, upstream):
    return scale * (
        upstream
        - jnp.mean(upstream, axis=-1, keepdims=True)
        - unit * jnp.mean(upstream * unit, axis=-1, keepdims=True)
    )


def params(**kw):
    return pltpu.CompilerParams(vmem_limit_bytes=LIMIT, **kw)


def cost(flops, moved, expos=0):
    return pl.CostEstimate(flops=flops, bytes_accessed=moved, transcendentals=expos)


def local_memory(array):
    return pltpu.with_memory_space_constraint(array, pltpu.VMEM)


def whole(shape):
    return pl.BlockSpec(shape, lambda *_: (0,) * len(shape))


def halves(exact):
    top = exact.astype(BF16)
    rest = (exact - top.astype(F32)).astype(BF16)
    return jnp.concatenate([top, rest], axis=1)


def joined_halves(pair):
    return pair[:, : pair.shape[1] // 2] + pair[:, pair.shape[1] // 2 :]


SMEM = pl.BlockSpec(memory_space=pltpu.SMEM)


def project_kernel(frames_ref, weight_ref, normed_ref, send_ref):
    @pl.when(pl.program_id(0) == 0)
    def _():
        unit, _ = normalize(frames_ref[...].astype(F32))
        normed_ref[...] = unit.astype(BF16)

    part = dot(normed_ref[...], weight_ref[...]).astype(BF16)
    send_ref[...] = part.T.reshape(send_ref.shape)


def project(frames, w_qkv):
    rows, width = frames.shape
    cols = 512
    per = cols // HD
    groups = HEADS // per
    return pl.pallas_call(
        project_kernel,
        grid=(3 * groups,),
        in_specs=[whole(frames.shape), pl.BlockSpec((width, cols), lambda j: (0, j))],
        out_specs=[
            whole(frames.shape),
            pl.BlockSpec((per, HD, rows), lambda j: (j % groups, j // groups, 0)),
        ],
        out_shape=[
            jax.ShapeDtypeStruct(frames.shape, BF16),
            jax.ShapeDtypeStruct((HEADS, 3 * HD, rows), BF16),
        ],
        compiler_params=params(),
        name="project",
    )(frames, w_qkv)


def load_heads(length, heads_ref, query, keys, count, rows):
    extra = lax.broadcasted_iota(jnp.int32, (HD, rows), 0)
    frame = lax.broadcasted_iota(jnp.int32, (HD, rows), 1)
    for i in range(count):
        cols = slice(i * rows, (i + 1) * rows)
        query[0:HD, cols] = (heads_ref[i, 0:HD, :].astype(F32) * 0.125).astype(BF16)
        query[HD : 2 * HD, cols] = jnp.where(extra == 0, 1.0, 0.0).astype(BF16)
        masked = jnp.logical_and(extra == 0, frame + i * rows >= length)
        mask = jnp.where(masked, -1e30, 0.0).astype(BF16)
        joined = jnp.concatenate([heads_ref[i, HD : 2 * HD, :], mask], axis=0)
        keys[cols, :] = joined.T


def attend_kernel(
    scalars, heads_ref, send_ref, out_ref, lse_ref, query, keys, value, scores
):
    count, _, rows = heads_ref.shape
    total = count * rows
    load_heads(scalars[0], heads_ref, query, keys, count, rows)
    for i in range(count):
        value[:, i * rows : (i + 1) * rows] = heads_ref[i, 2 * HD : 3 * HD, :]

    def one_block(block, carry):
        cols = pl.ds(pl.multiple_of(block * QB, QB), QB)
        query_cols = query[:, cols]
        peak = None
        for k in range(total // KB):
            part = dot(keys[k * KB : (k + 1) * KB, :], query_cols)
            scores[k * KB : (k + 1) * KB, :] = part
            top = jnp.max(part.reshape(KB // 8, 8, QB), axis=0)
            peak = top if peak is None else jnp.maximum(peak, top)
        peak = jnp.max(peak, axis=0, keepdims=True)
        total_row = jnp.zeros((8, QB), F32)
        acc = jnp.zeros((HD, QB), F32)
        for k in range(total // KB):
            expo = jnp.exp(scores[k * KB : (k + 1) * KB, :] - peak)
            total_row = total_row + jnp.sum(expo.reshape(KB // 8, 8, QB), axis=0)
            acc = acc + dot(value[:, k * KB : (k + 1) * KB], expo.astype(BF16))
        total_row = jnp.sum(total_row, axis=0, keepdims=True)
        out_ref[:, cols] = acc / total_row
        lse_ref[:, cols] = peak + jnp.log(total_row)
        return carry

    lax.fori_loop(0, total // QB, one_block, 0)
    none = jnp.zeros((HD, HALO), F32)
    for i in range(count):
        send_ref[i, 0:HD, :] = out_ref[:, i * rows : (i + 1) * rows].astype(BF16)
        low = out_ref[:, i * rows - HALO : i * rows] if i else none
        high = out_ref[:, (i + 1) * rows : (i + 1) * rows + HALO] if i < count - 1 else none
        sides = jnp.concatenate([low, high], axis=1)
        packed = jnp.concatenate([sides[0 : HD // 2], sides[HD // 2 :]], axis=1)
        send_ref[i, HD : HD + HD // 2, :] = packed.astype(BF16)


def attend(scalars, heads):
    count, _, rows = heads.shape
    total = count * rows
    return pl.pallas_call(
        attend_kernel,
        in_specs=[SMEM, pl.BlockSpec(memory_space=pltpu.VMEM)],
        out_shape=[
            jax.ShapeDtypeStruct((count, HD + HD // 2, rows), BF16),
            jax.ShapeDtypeStruct((HD, total), F32),
            jax.ShapeDtypeStruct((1, total), F32),
        ],
        scratch_shapes=[
            pltpu.VMEM((2 * HD, total), BF16),
            pltpu.VMEM((total, 2 * HD), BF16),
            pltpu.VMEM((HD, total), BF16),
            pltpu.VMEM((total, QB), F32),
        ],
        compiler_params=params(),
        cost_estimate=cost(2 * 2 * total * total * 256, heads.size * 2, total * total),
        name="attend",
    )(scalars, heads)


def middle_kernel(
    scalars,
    att_ref,
    frames_ref,
    frames_side,
    grads_ref,
    grads_side,
    w_out_ref,
    w_conv_ref,
    output_ref,
    res_grad_ref,
    round_ref,
    send_ref,
    taps_ref,
    conv_in,
    grad_all,
    residual,
    window,
    window_back,
    conv_grad,
):
    rows, width = frames_ref.shape
    heads = att_ref.shape[0]
    length = scalars[0]
    first = scalars[1]
    zero = scalars[2]
    half = HD // 2
    body = slice(HALO, HALO + rows)

    attended = att_ref[:, 0:HD, :].reshape(width, rows).T
    main = frames_ref[...].astype(F32) + dot(attended, w_out_ref[...])
    packed = att_ref[:, HD : HD + half, :].reshape(heads * half, rows).T
    split_w = w_out_ref[...].reshape(heads, 2, half, width)
    side = dot(packed[0 : 2 * HALO], split_w[:, 0].reshape(heads * half, width))
    side = side + dot(packed[2 * HALO :], split_w[:, 1].reshape(heads * half, width))
    side = frames_side[...].astype(F32) + side

    def keep_of(count, start):
        frame = lax.broadcasted_iota(jnp.int32, (count, 1), 0) + start
        return jnp.where(jnp.logical_and(frame >= 0, frame < length), 1.0, 0.0)

    main = main.astype(BF16).astype(F32)
    residual[...] = main
    unit, scale = normalize(main)
    keep = keep_of(rows, first)
    conv_in[body, :] = (unit * keep).astype(BF16).astype(F32)
    unit_side, _ = normalize(side.astype(BF16).astype(F32))
    low = unit_side[0:HALO] * keep_of(HALO, first - HALO)
    high = unit_side[HALO:] * keep_of(HALO, first + rows)
    conv_in[0:HALO, :] = low.astype(BF16).astype(F32)
    conv_in[HALO + rows :, :] = high.astype(BF16).astype(F32)
    grad_all[0:HALO, :] = grads_side[0:HALO, :].astype(F32)
    grad_all[body, :] = grads_ref[...].astype(F32)
    grad_all[HALO + rows :, :] = grads_side[HALO:, :].astype(F32)

    reach = rows + HALO
    edge = HALO // 2

    def one_chunk(chunk, carry):
        lanes = pl.ds(pl.multiple_of(chunk * 128, 128), 128)
        window[...] = conv_in[:, lanes]
        acc = jnp.zeros((reach, 128), F32)
        for j in range(KW):
            acc = acc + w_conv_ref[j : j + 1, lanes] * window[pl.ds(zero + (1 + j), reach), :]
        gate = jax.nn.sigmoid(acc)
        back = grad_all[edge : edge + reach, lanes] * (gate + acc * gate * (1.0 - gate))
        window_back[...] = back
        gated = acc[edge : edge + rows] * gate[edge : edge + rows]
        output_ref[:, lanes] = (residual[:, lanes] + gated).astype(BF16)
        own = window_back[edge : edge + rows, :]
        acc = jnp.zeros((rows, 128), F32)
        for j in range(KW):
            acc = acc + w_conv_ref[j : j + 1, lanes] * window_back[
                pl.ds(zero + (KW - j), rows), :
            ]
            moved = window[pl.ds(zero + (edge + 1 + j), rows), :]
            taps_ref[j : j + 1, lanes] = jnp.sum(moved * own, axis=0, keepdims=True)
        taps_ref[KW : KW + 1, lanes] = jnp.zeros((1, 128), F32)
        conv_grad[:, lanes] = acc
        return carry

    lax.fori_loop(0, width // 128, one_chunk, 0)
    res_grad = grads_ref[...].astype(F32) + normalize_back(unit, scale, conv_grad[...] * keep)
    res_grad_ref[...] = res_grad
    rounded = res_grad.astype(BF16)
    round_ref[...] = rounded
    back = dot(w_out_ref[...], rounded, 1, 1).astype(BF16)
    send_ref[:, 0:HD, :] = back.reshape(heads, HD, rows)
    for h in range(heads):
        send_ref[h, HD:, :] = halves(taps_ref[:, h * HD : (h + 1) * HD])


def middle(scalars, att, frames, frames_side, grads, grads_side, w_out, w_conv):
    rows, width = frames.shape
    vmem = pl.BlockSpec(memory_space=pltpu.VMEM)
    return pl.pallas_call(
        middle_kernel,
        in_specs=[SMEM] + [vmem] * 7,
        out_shape=[
            jax.ShapeDtypeStruct((rows, width), BF16),
            jax.ShapeDtypeStruct((rows, width), F32),
            jax.ShapeDtypeStruct((rows, width), BF16),
            jax.ShapeDtypeStruct((HEADS, HD + KW + 1, rows), BF16),
        ],
        scratch_shapes=[
            pltpu.VMEM((KW + 1, width), F32),
            pltpu.VMEM((rows + 2 * HALO, width), F32),
            pltpu.VMEM((rows + 2 * HALO, width), F32),
            pltpu.VMEM((rows, width), F32),
            pltpu.VMEM((rows + 2 * HALO, 128), F32),
            pltpu.VMEM((rows + HALO, 128), F32),
            pltpu.VMEM((rows, width), F32),
        ],
        compiler_params=params(),
        name="middle",
    )(scalars, att, frames, frames_side, grads, grads_side, w_out, w_conv)


def attend_back_kernel(
    scalars, heads_ref, grads_ref, out_ref, lse_ref, send_ref,
    query, keys, value_t, grad_t, query_rows, grad_rows, query_grad, probs, score_grads,
):
    count, _, rows = heads_ref.shape
    total = count * rows
    load_heads(scalars[0], heads_ref, query, keys, count, rows)
    for i in range(count):
        cols = slice(i * rows, (i + 1) * rows)
        block = grads_ref[i, 0:HD, :]
        grad_t[:, cols] = block
        both = jnp.concatenate([query[0:HD, cols], block], axis=0).T
        query_rows[cols, :] = both[:, 0:HD]
        grad_rows[cols, :] = both[:, HD:]
        value_t[cols, :] = heads_ref[i, 2 * HD : 3 * HD, :].T
    query_grad[...] = jnp.zeros_like(query_grad)
    lse = lse_ref[...]
    delta = jnp.sum(grad_t[...].astype(F32) * out_ref[...], axis=0, keepdims=True)

    def one_block(block, carry):
        span = pl.ds(pl.multiple_of(block * KB, KB), KB)
        key_rows = keys[span, :]
        value_rows = value_t[span, :]
        for q in range(total // QB):
            cols = slice(q * QB, (q + 1) * QB)
            prob = jnp.exp(dot(key_rows, query[:, cols]) - lse[:, cols])
            prob_grad = dot(value_rows, grad_t[:, cols])
            probs[:, cols] = prob.astype(BF16)
            score_grads[:, cols] = (prob * (prob_grad - delta[:, cols])).astype(BF16)
        key_grad = dot(score_grads[...], query_rows[...])
        value_grad = dot(probs[...], grad_rows[...])
        key_cols = key_rows[:, 0:HD].T
        query_grad[...] += dot(key_cols, score_grads[...])
        joined = jnp.concatenate([key_grad, value_grad], axis=1).T.astype(BF16)
        for i in range(KB // rows):
            send_ref[block * (KB // rows) + i, HD : 3 * HD, :] = joined[:, i * rows : (i + 1) * rows]
        return carry

    lax.fori_loop(0, total // KB, one_block, 0)
    for i in range(count):
        cols = slice(i * rows, (i + 1) * rows)
        send_ref[i, 0:HD, :] = (query_grad[:, cols] * 0.125).astype(BF16)


def attend_back(scalars, heads, grads, out, lse):
    count, _, rows = heads.shape
    total = count * rows
    vmem = pl.BlockSpec(memory_space=pltpu.VMEM)
    return pl.pallas_call(
        attend_back_kernel,
        in_specs=[SMEM] + [vmem] * 4,
        out_shape=jax.ShapeDtypeStruct(heads.shape, BF16),
        scratch_shapes=[
            pltpu.VMEM((2 * HD, total), BF16),
            pltpu.VMEM((total, 2 * HD), BF16),
            pltpu.VMEM((total, HD), BF16),
            pltpu.VMEM((HD, total), BF16),
            pltpu.VMEM((total, HD), BF16),
            pltpu.VMEM((total, HD), BF16),
            pltpu.VMEM((HD, total), F32),
            pltpu.VMEM((KB, total), BF16),
            pltpu.VMEM((KB, total), BF16),
        ],
        compiler_params=params(),
        cost_estimate=cost(5 * 2 * total * total * 256, heads.size * 4, total * total),
        name="attend_back",
    )(scalars, heads, grads, out, lse)


def input_grad_kernel(joined_ref, weight_ref, frames_ref, res_grad_ref, out_ref, joined, grads):
    step = pl.program_id(0)
    heads = joined_ref.shape[0]

    @pl.when(step == 0)
    def _():
        for h in range(heads):
            for t in range(3):
                row = (t * heads + h) * HD
                joined[row : row + HD, :] = joined_ref[h, t * HD : (t + 1) * HD, :]

    block = weight_ref.shape[0]
    start = pl.multiple_of(step * block, block)
    grads[pl.ds(start, block), :] = dot(weight_ref[...], joined[...])

    @pl.when(step == pl.num_programs(0) - 1)
    def _():
        unit, scale = normalize(frames_ref[...].astype(F32))
        back = normalize_back(unit, scale, grads[...].T)
        out_ref[...] = (res_grad_ref[...] + back).astype(BF16)


def input_gradient(joined, w_qkv, frames, res_grad):
    rows, width = frames.shape
    block = 256
    return pl.pallas_call(
        input_grad_kernel,
        grid=(width // block,),
        in_specs=[
            pl.BlockSpec(memory_space=pltpu.VMEM),
            pl.BlockSpec((block, w_qkv.shape[1]), lambda j: (j, 0)),
            whole(frames.shape),
            whole(frames.shape),
        ],
        out_specs=whole(frames.shape),
        out_shape=jax.ShapeDtypeStruct(frames.shape, BF16),
        scratch_shapes=[
            pltpu.VMEM((w_qkv.shape[1], rows), BF16),
            pltpu.VMEM((width, rows), F32),
        ],
        compiler_params=params(),
        name="input_gradient",
    )(local_memory(joined), w_qkv, frames, res_grad)


CUT = 96
FAST = 4
SLOW = 4
TAPS = SLOW * CUT
OUT = 8 * HD


def out_part_kernel(scalars, att_ref, round_ref, *send_refs):
    lanes = send_refs[0].shape[3]
    for k, send_ref in enumerate(send_refs):
        for p in range(FAST // 2):
            part = dot(att_ref[2 * p + (scalars[5] ^ k), 0:HD, :], round_ref[...])
            for c in range(part.shape[1] // lanes):
                piece = part[:, c * lanes : (c + 1) * lanes]
                send_ref[0, p, c * HD : (c + 1) * HD, :] = piece.astype(BF16)


def out_part(scalars, att, rounded):
    heads, wide, rows = att.shape
    return pl.pallas_call(
        out_part_kernel,
        grid=(SLOW,),
        in_specs=[
            SMEM,
            pl.BlockSpec((FAST, wide, rows), lambda j: (j, 0, 0)),
            whole(rounded.shape),
        ],
        out_specs=[pl.BlockSpec((1, FAST // 2, OUT, 128), lambda j: (j, 0, 0, 0))] * 2,
        out_shape=[jax.ShapeDtypeStruct((SLOW, FAST // 2, OUT, 128), BF16)] * 2,
        compiler_params=params(),
        cost_estimate=cost(2 * heads * HD * 256 * rounded.shape[1], heads * HD * rounded.shape[1] * 2),
        name="out_part",
    )(scalars, att, rounded)


def parts_kernel(scalars, grads_ref, back_ref, normed_ref, *rest):
    send_refs, columns, pieces = rest[:FAST], rest[FAST], rest[FAST + 1]
    count, wide, rows = grads_ref.shape
    slow = pl.program_id(0)

    @pl.when(slow == 0)
    def _():
        taps = jnp.zeros((KW + 1, rows), F32)
        for i in range(count):
            columns[:, i * rows : (i + 1) * rows] = grads_ref[i]
            taps = taps + back_ref[i, HD:, :].astype(F32)
        pair = halves(joined_halves(taps))
        for send_ref in send_refs:
            send_ref[TAPS:, :] = pair

    part = dot(columns[...], normed_ref[...])
    each = part.shape[1] // FAST
    for i in range(FAST):
        piece = part[:, i * each : (i + 1) * each]
        pieces[i] = jnp.concatenate([piece[0:CUT], piece[CUT:]], axis=1).astype(BF16)
    for k, send_ref in enumerate(send_refs):
        send_ref[pl.ds(pl.multiple_of(slow * CUT, CUT), CUT), :] = pieces[scalars[3] ^ k]


def gradient_parts(scalars, grads, back, normed_all):
    count, wide, rows = grads.shape
    total, width = normed_all.shape
    return pl.pallas_call(
        parts_kernel,
        grid=(SLOW,),
        in_specs=[
            SMEM,
            whole(grads.shape),
            whole(back.shape),
            pl.BlockSpec((total, width // SLOW), lambda j: (0, j)),
        ],
        out_specs=[whole((TAPS + KW + 1, 128))] * FAST,
        out_shape=[jax.ShapeDtypeStruct((TAPS + KW + 1, 128), BF16)] * FAST,
        scratch_shapes=[pltpu.VMEM((wide, total), BF16), pltpu.VMEM((FAST, CUT, 128), BF16)],
        compiler_params=params(),
        cost_estimate=cost(2 * 256 * total * width, total * width * 2),
        name="gradient_parts",
    )(scalars, grads, back, normed_all)


def sum_four(own, one, two, three):
    return (own.astype(F32) + one.astype(F32)) + (two.astype(F32) + three.astype(F32))


def fold_core_kernel(scalars, one, two, *send_refs):
    for k, send_ref in enumerate(send_refs):
        i = scalars[4] ^ k
        send_ref[...] = (one[i].astype(F32) + two[i].astype(F32)).astype(BF16)


def fold_core(scalars, blocks):
    vmem = pl.BlockSpec(memory_space=pltpu.VMEM)
    return pl.pallas_call(
        fold_core_kernel,
        in_specs=[SMEM] + [vmem] * 2,
        out_shape=[jax.ShapeDtypeStruct((FAST // 2, OUT, 128), BF16)] * SLOW,
        compiler_params=params(),
        cost_estimate=cost(0, 3 * SLOW * FAST // 2 * OUT * 128 * 2),
        name="fold_core",
    )(scalars, *blocks)


def fold_out_kernel(scalars, one, two, three, four, *send_refs):
    for k, send_ref in enumerate(send_refs):
        i = scalars[6] ^ k
        send_ref[...] = sum_four(one[i], two[i], three[i], four[i]).astype(BF16)


def fold_out(scalars, blocks):
    vmem = pl.BlockSpec(memory_space=pltpu.VMEM)
    return pl.pallas_call(
        fold_out_kernel,
        in_specs=[SMEM] + [vmem] * 4,
        out_shape=[jax.ShapeDtypeStruct((OUT, 128), BF16)] * 2,
        compiler_params=params(),
        cost_estimate=cost(0, 5 * OUT * 128 * 4),
        name="fold_out",
    )(scalars, *blocks)


def fold_fast_kernel(scalars, one, two, three, four, *rest):
    send_refs, pieces = rest[:SLOW], rest[SLOW]
    total = sum_four(one[...], two[...], three[...], four[...])
    pair = halves(joined_halves(total[TAPS:]))
    for i in range(SLOW):
        pieces[i] = total[i * CUT : (i + 1) * CUT].astype(BF16)
    for k, send_ref in enumerate(send_refs):
        send_ref[0:CUT, :] = pieces[scalars[4] ^ k]
        send_ref[CUT:, :] = pair


def fold_fast(scalars, blocks):
    vmem = pl.BlockSpec(memory_space=pltpu.VMEM)
    return pl.pallas_call(
        fold_fast_kernel,
        in_specs=[SMEM] + [vmem] * 4,
        out_shape=[jax.ShapeDtypeStruct((CUT + KW + 1, 128), BF16)] * SLOW,
        scratch_shapes=[pltpu.VMEM((SLOW, CUT, 128), BF16)],
        compiler_params=params(),
        name="fold_fast",
    )(scalars, *blocks)


def fold_slow_kernel(*refs, scale):
    qkv_ref, send_ref = refs[6:]
    total = sum_four(*(ref[...] for ref in refs[0:4]))
    model_rows = (total[0:CUT] * scale).T
    qkv_ref[:, 0:CUT] = model_rows[0:HD]
    qkv_ref[:, CUT:] = model_rows[HD:]
    pair = halves(joined_halves(total[CUT:]))
    outer = refs[4][...].astype(F32) + refs[5][...].astype(F32)
    count = send_ref.shape[0]
    each = HD // count
    for i in range(count):
        pieces = [outer[c * HD + i * each : c * HD + (i + 1) * each] for c in range(OUT // HD)]
        send_ref[i, 0 : OUT // count, :] = jnp.concatenate(pieces, axis=0).astype(BF16)
        send_ref[i, OUT // count :, :] = pair


def fold_slow(blocks, out_blocks, seq_count, scale):
    vmem = pl.BlockSpec(memory_space=pltpu.VMEM)
    return pl.pallas_call(
        lambda *refs: fold_slow_kernel(*refs, scale=scale),
        in_specs=[vmem] * 6,
        out_shape=[
            jax.ShapeDtypeStruct((HD, 3 * HD), F32),
            jax.ShapeDtypeStruct((seq_count, OUT // seq_count + KW + 1, 128), BF16),
        ],
        compiler_params=params(),
        name="fold_slow",
    )(*blocks, *out_blocks)


def finish_kernel(recv_ref, out_ref, taps_ref, *, scale):
    count = recv_ref.shape[0]
    each = out_ref.shape[0]
    wide = OUT // count
    total = recv_ref[0, 0:wide, :].astype(F32)
    for i in range(1, count):
        total = total + recv_ref[i, 0:wide, :].astype(F32)
    total = total * scale
    for c in range(OUT // HD):
        out_ref[:, c * 128 : (c + 1) * 128] = total[c * each : (c + 1) * each]
    for i in range(count // 2):
        both = [joined_halves(recv_ref[2 * i + k, wide:, :].astype(F32)) for k in range(2)]
        both = jnp.concatenate(both, axis=1) * scale
        taps_ref[:, i * 2 * HD : (i + 1) * 2 * HD] = both[0:KW]


def finish(recv, width, scale):
    count = recv.shape[0]
    vmem = pl.BlockSpec(memory_space=pltpu.VMEM)
    return pl.pallas_call(
        lambda *refs: finish_kernel(*refs, scale=scale),
        in_specs=[vmem],
        out_shape=[
            jax.ShapeDtypeStruct((HD // count, width), F32),
            jax.ShapeDtypeStruct((KW, width), F32),
        ],
        compiler_params=params(),
        name="finish",
    )(recv)


def exchange(blocks, step):
    pairs = lambda k: [(d, d ^ (step * k)) for d in range(FAST * SLOW)]
    moved = [
        local_memory(lax.ppermute(block, "dp", pairs(k))) for k, block in enumerate(blocks) if k
    ]
    return [blocks[0]] + moved


def local(frames, cotangent, w_qkv, w_out, w_conv, lengths):
    seq_count = lax.axis_size("seq")
    data_count = lax.axis_size("dp")
    rows, width = frames.shape[1:]
    first = lax.axis_index("seq") * rows
    grad_scale = 1.0 / math.sqrt(data_count * rows * seq_count)
    position = lax.axis_index("dp")
    fast = position % FAST
    slow = position // FAST
    place = [fast, slow, fast % 2, fast // 2]
    scalars = jnp.stack([lengths[0], first, jnp.zeros((), jnp.int32)] + place)
    x = frames[0]
    g = cotangent[0]

    forward = [(i, i + 1) for i in range(seq_count - 1)]
    backward = [(i + 1, i) for i in range(seq_count - 1)]
    low = lax.ppermute(jnp.concatenate([x[-HALO:], g[-HALO:]], axis=0), "seq", forward)
    high = lax.ppermute(jnp.concatenate([x[:HALO], g[:HALO]], axis=0), "seq", backward)
    x_side = jnp.concatenate([low[:HALO], high[:HALO]], axis=0)
    g_side = jnp.concatenate([low[HALO:], high[HALO:]], axis=0)

    normed, send = project(x, w_qkv)
    heads = lax.all_to_all(send, "seq", 0, 0, tiled=True)
    heads_near = local_memory(heads)
    normed_all = lax.all_gather(normed, "seq", axis=0, tiled=True)
    send, out, lse = attend(scalars, heads_near)
    att = local_memory(lax.all_to_all(send, "seq", 0, 0, tiled=True))
    output, res_grad, rounded, send = middle(scalars, att, x, x_side, g, g_side, w_out, w_conv)
    back = lax.all_to_all(send, "seq", 0, 0, tiled=True)
    back, outer = lax.optimization_barrier((back, out_part(scalars, att, rounded)))
    outer = exchange(fold_core(scalars, exchange(outer, 1)), FAST)
    send = attend_back(scalars, heads, local_memory(back), out, lse)
    joined = lax.all_to_all(send, "seq", 0, 0, tiled=True)
    parts = exchange(gradient_parts(scalars, send, back, normed_all), 1)
    outer = exchange(fold_out(scalars, outer), 2)
    parts = exchange(fold_fast(scalars, parts), FAST)
    qkv, send = fold_slow(parts, outer, seq_count, grad_scale)
    input_grad = input_gradient(joined, w_qkv, x, res_grad)
    recv = lax.all_to_all(send, "seq", 0, 0, tiled=True)
    out_total, taps_total = finish(local_memory(recv), width, grad_scale)
    return (
        output[None],
        input_grad[None],
        qkv.reshape(width // data_count, 3, HD),
        out_total,
        taps_total,
    )


def solution(mesh):
    placed = (P("dp", "seq", None), P("dp", "seq", None), P(), P(), P(), P("dp"))
    return jax.shard_map(
        local,
        mesh=mesh,
        in_specs=placed,
        out_specs=(
            P("dp", "seq", None),
            P("dp", "seq", None),
            P("dp", None, "seq"),
            P(("dp", "seq"), None),
            P(),
        ),
        check_vma=False,
    )
```

```python
import math

import jax
import jax.numpy as jnp
from jax import lax
from jax.experimental import pallas as pl
from jax.experimental.pallas import tpu as pltpu
from jax.sharding import PartitionSpec as P

HEADS = 16
KW = 31
HD = 64
HALO = 32
QB = 256
KB = 256
F32 = jnp.float32
BF16 = jnp.bfloat16
LIMIT = 56 * 1024 * 1024
CUT = 96
FAST = 4
SLOW = 4
TAPS = SLOW * CUT
OUT = 8 * HD


def dot(a, b, ca=1, cb=0):
    return lax.dot_general(a, b, (((ca,), (cb,)), ((), ())), preferred_element_type=F32)


def normalize(rows):
    center = rows - jnp.mean(rows, axis=-1, keepdims=True)
    scale = lax.rsqrt(jnp.mean(center * center, axis=-1, keepdims=True) + 1e-05)
    return center * scale, scale


def normalize_back(unit, scale, upstream):
    return scale * (
        upstream
        - jnp.mean(upstream, axis=-1, keepdims=True)
        - unit * jnp.mean(upstream * unit, axis=-1, keepdims=True)
    )


def params(**kw):
    return pltpu.CompilerParams(vmem_limit_bytes=LIMIT, **kw)


def cost(flops, moved, expos=0):
    return pl.CostEstimate(flops=flops, bytes_accessed=moved, transcendentals=expos)


def local_memory(array):
    return pltpu.with_memory_space_constraint(array, pltpu.VMEM)


def whole(shape):
    return pl.BlockSpec(shape, lambda *_: (0,) * len(shape))


def halves(exact):
    top = exact.astype(BF16)
    rest = (exact - top.astype(F32)).astype(BF16)
    return jnp.concatenate([top, rest], axis=1)


def joined_halves(pair):
    return pair[:, : pair.shape[1] // 2] + pair[:, pair.shape[1] // 2 :]


SMEM = pl.BlockSpec(memory_space=pltpu.SMEM)


def project_kernel(frames_ref, weight_ref, normed_ref, send_ref):
    @pl.when(pl.program_id(0) == 0)
    def _():
        unit, _ = normalize(frames_ref[...].astype(F32))
        normed_ref[...] = unit.astype(BF16)

    part = dot(normed_ref[...], weight_ref[...]).astype(BF16)
    send_ref[...] = part.T.reshape(send_ref.shape)


def project(frames, w_qkv):
    rows, width = frames.shape
    cols = 512
    per = cols // HD
    groups = HEADS // per
    return pl.pallas_call(
        project_kernel,
        grid=(3 * groups,),
        in_specs=[whole(frames.shape), pl.BlockSpec((width, cols), lambda j: (0, j))],
        out_specs=[
            whole(frames.shape),
            pl.BlockSpec((per, HD, rows), lambda j: (j % groups, j // groups, 0)),
        ],
        out_shape=[
            jax.ShapeDtypeStruct(frames.shape, BF16),
            jax.ShapeDtypeStruct((HEADS, 3 * HD, rows), BF16),
        ],
        compiler_params=params(),
        name="project",
    )(frames, w_qkv)


def load_heads(length, heads_ref, query, keys, count, rows):
    extra = lax.broadcasted_iota(jnp.int32, (HD, rows), 0)
    frame = lax.broadcasted_iota(jnp.int32, (HD, rows), 1)
    for i in range(count):
        cols = slice(i * rows, (i + 1) * rows)
        query[0:HD, cols] = (heads_ref[i, 0:HD, :].astype(F32) * 0.125).astype(BF16)
        query[HD : 2 * HD, cols] = jnp.where(extra == 0, 1.0, 0.0).astype(BF16)
        masked = jnp.logical_and(extra == 0, frame + i * rows >= length)
        mask = jnp.where(masked, -1e30, 0.0).astype(BF16)
        joined = jnp.concatenate([heads_ref[i, HD : 2 * HD, :], mask], axis=0)
        keys[cols, :] = joined.T


def attend_kernel(
    scalars, heads_ref, send_ref, out_ref, lse_ref, query, keys, value, scores
):
    count, _, rows = heads_ref.shape
    total = count * rows
    load_heads(scalars[0], heads_ref, query, keys, count, rows)
    for i in range(count):
        value[:, i * rows : (i + 1) * rows] = heads_ref[i, 2 * HD : 3 * HD, :]

    def one_block(block, carry):
        cols = pl.ds(pl.multiple_of(block * QB, QB), QB)
        query_cols = query[:, cols]
        peak = None
        for k in range(total // KB):
            part = dot(keys[k * KB : (k + 1) * KB, :], query_cols)
            scores[k * KB : (k + 1) * KB, :] = part
            top = jnp.max(part.reshape(KB // 8, 8, QB), axis=0)
            peak = top if peak is None else jnp.maximum(peak, top)
        peak = jnp.max(peak, axis=0, keepdims=True)
        total_row = jnp.zeros((8, QB), F32)
        acc = jnp.zeros((HD, QB), F32)
        for k in range(total // KB):
            expo = jnp.exp(scores[k * KB : (k + 1) * KB, :] - peak)
            total_row = total_row + jnp.sum(expo.reshape(KB // 8, 8, QB), axis=0)
            acc = acc + dot(value[:, k * KB : (k + 1) * KB], expo.astype(BF16))
        total_row = jnp.sum(total_row, axis=0, keepdims=True)
        out_ref[:, cols] = acc / total_row
        lse_ref[:, cols] = peak + jnp.log(total_row)
        return carry

    lax.fori_loop(0, total // QB, one_block, 0)
    none = jnp.zeros((HD, HALO), F32)
    for i in range(count):
        send_ref[i, 0:HD, :] = out_ref[:, i * rows : (i + 1) * rows].astype(BF16)
        low = out_ref[:, i * rows - HALO : i * rows] if i else none
        high = out_ref[:, (i + 1) * rows : (i + 1) * rows + HALO] if i < count - 1 else none
        sides = jnp.concatenate([low, high], axis=1)
        packed = jnp.concatenate([sides[0 : HD // 2], sides[HD // 2 :]], axis=1)
        send_ref[i, HD : HD + HD // 2, :] = packed.astype(BF16)


def attend(scalars, heads):
    count, _, rows = heads.shape
    total = count * rows
    return pl.pallas_call(
        attend_kernel,
        in_specs=[SMEM, pl.BlockSpec(memory_space=pltpu.VMEM)],
        out_shape=[
            jax.ShapeDtypeStruct((count, HD + HD // 2, rows), BF16),
            jax.ShapeDtypeStruct((HD, total), F32),
            jax.ShapeDtypeStruct((1, total), F32),
        ],
        scratch_shapes=[
            pltpu.VMEM((2 * HD, total), BF16),
            pltpu.VMEM((total, 2 * HD), BF16),
            pltpu.VMEM((HD, total), BF16),
            pltpu.VMEM((total, QB), F32),
        ],
        compiler_params=params(),
        cost_estimate=cost(2 * 2 * total * total * 256, heads.size * 2, total * total),
        name="attend",
    )(scalars, heads)


def middle_kernel(
    scalars,
    att_ref,
    frames_ref,
    frames_side,
    grads_ref,
    grads_side,
    w_out_ref,
    w_conv_ref,
    output_ref,
    res_grad_ref,
    send_ref,
    pack_one,
    pack_two,
    pack_three,
    pack_four,
    taps_ref,
    conv_in,
    grad_all,
    residual,
    window,
    window_back,
    conv_grad,
):
    rows, width = frames_ref.shape
    heads = att_ref.shape[0]
    length = scalars[0]
    first = scalars[1]
    zero = scalars[2]
    half = HD // 2
    body = slice(HALO, HALO + rows)

    attended = att_ref[:, 0:HD, :].reshape(width, rows).T
    main = frames_ref[...].astype(F32) + dot(attended, w_out_ref[...])
    packed = att_ref[:, HD : HD + half, :].reshape(heads * half, rows).T
    split_w = w_out_ref[...].reshape(heads, 2, half, width)
    side = dot(packed[0 : 2 * HALO], split_w[:, 0].reshape(heads * half, width))
    side = side + dot(packed[2 * HALO :], split_w[:, 1].reshape(heads * half, width))
    side = frames_side[...].astype(F32) + side

    def keep_of(count, start):
        frame = lax.broadcasted_iota(jnp.int32, (count, 1), 0) + start
        return jnp.where(jnp.logical_and(frame >= 0, frame < length), 1.0, 0.0)

    main = main.astype(BF16).astype(F32)
    residual[...] = main
    unit, scale = normalize(main)
    keep = keep_of(rows, first)
    conv_in[body, :] = (unit * keep).astype(BF16).astype(F32)
    unit_side, _ = normalize(side.astype(BF16).astype(F32))
    low = unit_side[0:HALO] * keep_of(HALO, first - HALO)
    high = unit_side[HALO:] * keep_of(HALO, first + rows)
    conv_in[0:HALO, :] = low.astype(BF16).astype(F32)
    conv_in[HALO + rows :, :] = high.astype(BF16).astype(F32)
    grad_all[0:HALO, :] = grads_side[0:HALO, :].astype(F32)
    grad_all[body, :] = grads_ref[...].astype(F32)
    grad_all[HALO + rows :, :] = grads_side[HALO:, :].astype(F32)

    reach = rows + HALO
    edge = HALO // 2

    def one_chunk(chunk, carry):
        lanes = pl.ds(pl.multiple_of(chunk * 128, 128), 128)
        window[...] = conv_in[:, lanes]
        acc = jnp.zeros((reach, 128), F32)
        for j in range(KW):
            acc = acc + w_conv_ref[j : j + 1, lanes] * window[pl.ds(zero + (1 + j), reach), :]
        gate = jax.nn.sigmoid(acc)
        back = grad_all[edge : edge + reach, lanes] * (gate + acc * gate * (1.0 - gate))
        window_back[...] = back
        gated = acc[edge : edge + rows] * gate[edge : edge + rows]
        output_ref[:, lanes] = (residual[:, lanes] + gated).astype(BF16)
        own = window_back[edge : edge + rows, :]
        acc = jnp.zeros((rows, 128), F32)
        for j in range(KW):
            acc = acc + w_conv_ref[j : j + 1, lanes] * window_back[
                pl.ds(zero + (KW - j), rows), :
            ]
            moved = window[pl.ds(zero + (edge + 1 + j), rows), :]
            taps_ref[j : j + 1, lanes] = jnp.sum(moved * own, axis=0, keepdims=True)
        taps_ref[KW : KW + 1, lanes] = jnp.zeros((1, 128), F32)
        conv_grad[:, lanes] = acc
        return carry

    lax.fori_loop(0, width // 128, one_chunk, 0)
    res_grad = grads_ref[...].astype(F32) + normalize_back(unit, scale, conv_grad[...] * keep)
    res_grad_ref[...] = res_grad
    rounded = res_grad.astype(BF16)
    for k, pack_ref in enumerate((pack_one, pack_two, pack_three, pack_four)):
        pack_ref[:, 0:width] = rounded
        picked = [att_ref[FAST * i + (scalars[3] ^ k), 0:HD, :] for i in range(SLOW)]
        pack_ref[:, width:] = jnp.concatenate(picked, axis=0).T
    back = dot(w_out_ref[...], rounded, 1, 1).astype(BF16)
    send_ref[:, 0:HD, :] = back.reshape(heads, HD, rows)
    for h in range(heads):
        send_ref[h, HD:, :] = halves(taps_ref[:, h * HD : (h + 1) * HD])


def middle(scalars, att, frames, frames_side, grads, grads_side, w_out, w_conv):
    rows, width = frames.shape
    vmem = pl.BlockSpec(memory_space=pltpu.VMEM)
    return pl.pallas_call(
        middle_kernel,
        in_specs=[SMEM] + [vmem] * 7,
        out_shape=[
            jax.ShapeDtypeStruct((rows, width), BF16),
            jax.ShapeDtypeStruct((rows, width), F32),
            jax.ShapeDtypeStruct((HEADS, HD + KW + 1, rows), BF16),
        ]
        + [jax.ShapeDtypeStruct((rows, width + SLOW * HD), BF16)] * FAST,
        scratch_shapes=[
            pltpu.VMEM((KW + 1, width), F32),
            pltpu.VMEM((rows + 2 * HALO, width), F32),
            pltpu.VMEM((rows + 2 * HALO, width), F32),
            pltpu.VMEM((rows, width), F32),
            pltpu.VMEM((rows + 2 * HALO, 128), F32),
            pltpu.VMEM((rows + HALO, 128), F32),
            pltpu.VMEM((rows, width), F32),
        ],
        compiler_params=params(),
        name="middle",
    )(scalars, att, frames, frames_side, grads, grads_side, w_out, w_conv)


def attend_back_kernel(
    scalars, heads_ref, grads_ref, out_ref, lse_ref, send_ref,
    query, keys, value_t, grad_t, query_rows, grad_rows, query_grad, probs, score_grads,
):
    count, _, rows = heads_ref.shape
    total = count * rows
    load_heads(scalars[0], heads_ref, query, keys, count, rows)
    for i in range(count):
        cols = slice(i * rows, (i + 1) * rows)
        block = grads_ref[i, 0:HD, :]
        grad_t[:, cols] = block
        both = jnp.concatenate([query[0:HD, cols], block], axis=0).T
        query_rows[cols, :] = both[:, 0:HD]
        grad_rows[cols, :] = both[:, HD:]
        value_t[cols, :] = heads_ref[i, 2 * HD : 3 * HD, :].T
    query_grad[...] = jnp.zeros_like(query_grad)
    lse = lse_ref[...]
    delta = jnp.sum(grad_t[...].astype(F32) * out_ref[...], axis=0, keepdims=True)

    def one_block(block, carry):
        span = pl.ds(pl.multiple_of(block * KB, KB), KB)
        key_rows = keys[span, :]
        value_rows = value_t[span, :]
        for q in range(total // QB):
            cols = slice(q * QB, (q + 1) * QB)
            prob = jnp.exp(dot(key_rows, query[:, cols]) - lse[:, cols])
            prob_grad = dot(value_rows, grad_t[:, cols])
            probs[:, cols] = prob.astype(BF16)
            score_grads[:, cols] = (prob * (prob_grad - delta[:, cols])).astype(BF16)
        key_grad = dot(score_grads[...], query_rows[...])
        value_grad = dot(probs[...], grad_rows[...])
        key_cols = key_rows[:, 0:HD].T
        query_grad[...] += dot(key_cols, score_grads[...])
        joined = jnp.concatenate([key_grad, value_grad], axis=1).T.astype(BF16)
        for i in range(KB // rows):
            send_ref[block * (KB // rows) + i, HD : 3 * HD, :] = joined[:, i * rows : (i + 1) * rows]
        return carry

    lax.fori_loop(0, total // KB, one_block, 0)
    for i in range(count):
        cols = slice(i * rows, (i + 1) * rows)
        send_ref[i, 0:HD, :] = (query_grad[:, cols] * 0.125).astype(BF16)


def attend_back(scalars, heads, grads, out, lse):
    count, _, rows = heads.shape
    total = count * rows
    vmem = pl.BlockSpec(memory_space=pltpu.VMEM)
    return pl.pallas_call(
        attend_back_kernel,
        in_specs=[SMEM] + [vmem] * 4,
        out_shape=jax.ShapeDtypeStruct(heads.shape, BF16),
        scratch_shapes=[
            pltpu.VMEM((2 * HD, total), BF16),
            pltpu.VMEM((total, 2 * HD), BF16),
            pltpu.VMEM((total, HD), BF16),
            pltpu.VMEM((HD, total), BF16),
            pltpu.VMEM((total, HD), BF16),
            pltpu.VMEM((total, HD), BF16),
            pltpu.VMEM((HD, total), F32),
            pltpu.VMEM((KB, total), BF16),
            pltpu.VMEM((KB, total), BF16),
        ],
        compiler_params=params(),
        cost_estimate=cost(5 * 2 * total * total * 256, heads.size * 4, total * total),
        name="attend_back",
    )(scalars, heads, grads, out, lse)


def input_grad_kernel(joined_ref, weight_ref, frames_ref, res_grad_ref, out_ref, joined, grads):
    step = pl.program_id(0)
    heads = joined_ref.shape[0]

    @pl.when(step == 0)
    def _():
        for h in range(heads):
            for t in range(3):
                row = (t * heads + h) * HD
                joined[row : row + HD, :] = joined_ref[h, t * HD : (t + 1) * HD, :]

    block = weight_ref.shape[0]
    start = pl.multiple_of(step * block, block)
    grads[pl.ds(start, block), :] = dot(weight_ref[...], joined[...])

    @pl.when(step == pl.num_programs(0) - 1)
    def _():
        unit, scale = normalize(frames_ref[...].astype(F32))
        back = normalize_back(unit, scale, grads[...].T)
        out_ref[...] = (res_grad_ref[...] + back).astype(BF16)


def input_gradient(joined, w_qkv, frames, res_grad):
    rows, width = frames.shape
    block = 256
    return pl.pallas_call(
        input_grad_kernel,
        grid=(width // block,),
        in_specs=[
            pl.BlockSpec(memory_space=pltpu.VMEM),
            pl.BlockSpec((block, w_qkv.shape[1]), lambda j: (j, 0)),
            whole(frames.shape),
            whole(frames.shape),
        ],
        out_specs=whole(frames.shape),
        out_shape=jax.ShapeDtypeStruct(frames.shape, BF16),
        scratch_shapes=[
            pltpu.VMEM((w_qkv.shape[1], rows), BF16),
            pltpu.VMEM((width, rows), F32),
        ],
        compiler_params=params(),
        name="input_gradient",
    )(local_memory(joined), w_qkv, frames, res_grad)


def out_part_kernel(scalars, one, two, three, four, *rest):
    send_refs, part = rest[:SLOW], rest[SLOW]
    width = send_refs[0].shape[0] // HD * 128
    packs = (one, two, three, four)
    left = jnp.concatenate([ref[:, width:] for ref in packs], axis=0)
    right = jnp.concatenate([ref[:, 0:width] for ref in packs], axis=0)
    part[...] = dot(left.T, right)
    for k, send_ref in enumerate(send_refs):
        rows = pl.ds(pl.multiple_of((scalars[4] ^ k) * HD, HD), HD)
        for c in range(width // 128):
            send_ref[c * HD : (c + 1) * HD, :] = part[rows, c * 128 : (c + 1) * 128].astype(BF16)


def out_part(scalars, packs):
    rows, wide = packs[0].shape
    vmem = pl.BlockSpec(memory_space=pltpu.VMEM)
    return pl.pallas_call(
        out_part_kernel,
        in_specs=[SMEM] + [vmem] * 4,
        out_shape=[jax.ShapeDtypeStruct((OUT, 128), BF16)] * SLOW,
        scratch_shapes=[pltpu.VMEM((SLOW * HD, wide - SLOW * HD), F32)],
        compiler_params=params(),
        name="out_part",
    )(scalars, *packs)


def parts_kernel(scalars, grads_ref, back_ref, normed_ref, *rest):
    send_refs, columns, pieces = rest[:FAST], rest[FAST], rest[FAST + 1]
    count, wide, rows = grads_ref.shape
    slow = pl.program_id(0)

    @pl.when(slow == 0)
    def _():
        taps = jnp.zeros((KW + 1, rows), F32)
        for i in range(count):
            columns[:, i * rows : (i + 1) * rows] = grads_ref[i]
            taps = taps + back_ref[i, HD:, :].astype(F32)
        pair = halves(joined_halves(taps))
        for send_ref in send_refs:
            send_ref[TAPS:, :] = pair

    part = dot(columns[...], normed_ref[...])
    each = part.shape[1] // FAST
    for i in range(FAST):
        piece = part[:, i * each : (i + 1) * each]
        pieces[i] = jnp.concatenate([piece[0:CUT], piece[CUT:]], axis=1).astype(BF16)
    for k, send_ref in enumerate(send_refs):
        send_ref[pl.ds(pl.multiple_of(slow * CUT, CUT), CUT), :] = pieces[scalars[3] ^ k]


def gradient_parts(scalars, grads, back, normed_all):
    count, wide, rows = grads.shape
    total, width = normed_all.shape
    return pl.pallas_call(
        parts_kernel,
        grid=(SLOW,),
        in_specs=[
            SMEM,
            whole(grads.shape),
            whole(back.shape),
            pl.BlockSpec((total, width // SLOW), lambda j: (0, j)),
        ],
        out_specs=[whole((TAPS + KW + 1, 128))] * FAST,
        out_shape=[jax.ShapeDtypeStruct((TAPS + KW + 1, 128), BF16)] * FAST,
        scratch_shapes=[pltpu.VMEM((wide, total), BF16), pltpu.VMEM((FAST, CUT, 128), BF16)],
        compiler_params=params(),
        cost_estimate=cost(2 * 256 * total * width, total * width * 2),
        name="gradient_parts",
    )(scalars, grads, back, normed_all)


def sum_four(own, one, two, three):
    return (own.astype(F32) + one.astype(F32)) + (two.astype(F32) + three.astype(F32))


def fold_fast_kernel(scalars, one, two, three, four, *rest):
    send_refs, pieces = rest[:SLOW], rest[SLOW]
    total = sum_four(one[...], two[...], three[...], four[...])
    pair = halves(joined_halves(total[TAPS:]))
    for i in range(SLOW):
        pieces[i] = total[i * CUT : (i + 1) * CUT].astype(BF16)
    for k, send_ref in enumerate(send_refs):
        send_ref[0:CUT, :] = pieces[scalars[4] ^ k]
        send_ref[CUT:, :] = pair


def fold_fast(scalars, blocks):
    vmem = pl.BlockSpec(memory_space=pltpu.VMEM)
    return pl.pallas_call(
        fold_fast_kernel,
        in_specs=[SMEM] + [vmem] * 4,
        out_shape=[jax.ShapeDtypeStruct((CUT + KW + 1, 128), BF16)] * SLOW,
        scratch_shapes=[pltpu.VMEM((SLOW, CUT, 128), BF16)],
        compiler_params=params(),
        name="fold_fast",
    )(scalars, *blocks)


def fold_slow_kernel(*refs, scale):
    qkv_ref, send_ref = refs[8:]
    total = sum_four(*(ref[...] for ref in refs[0:4]))
    model_rows = (total[0:CUT] * scale).T
    qkv_ref[:, 0:CUT] = model_rows[0:HD]
    qkv_ref[:, CUT:] = model_rows[HD:]
    pair = halves(joined_halves(total[CUT:]))
    outer = sum_four(*(ref[...] for ref in refs[4:8]))
    count = send_ref.shape[0]
    each = HD // count
    for i in range(count):
        pieces = [outer[c * HD + i * each : c * HD + (i + 1) * each] for c in range(OUT // HD)]
        send_ref[i, 0 : OUT // count, :] = jnp.concatenate(pieces, axis=0).astype(BF16)
        send_ref[i, OUT // count :, :] = pair


def fold_slow(blocks, out_blocks, seq_count, scale):
    vmem = pl.BlockSpec(memory_space=pltpu.VMEM)
    return pl.pallas_call(
        lambda *refs: fold_slow_kernel(*refs, scale=scale),
        in_specs=[vmem] * 8,
        out_shape=[
            jax.ShapeDtypeStruct((HD, 3 * HD), F32),
            jax.ShapeDtypeStruct((seq_count, OUT // seq_count + KW + 1, 128), BF16),
        ],
        compiler_params=params(),
        name="fold_slow",
    )(*blocks, *out_blocks)


def finish_kernel(recv_ref, out_ref, taps_ref, *, scale):
    count = recv_ref.shape[0]
    each = out_ref.shape[0]
    wide = OUT // count
    total = recv_ref[0, 0:wide, :].astype(F32)
    for i in range(1, count):
        total = total + recv_ref[i, 0:wide, :].astype(F32)
    total = total * scale
    for c in range(OUT // HD):
        out_ref[:, c * 128 : (c + 1) * 128] = total[c * each : (c + 1) * each]
    for i in range(count // 2):
        both = [joined_halves(recv_ref[2 * i + k, wide:, :].astype(F32)) for k in range(2)]
        both = jnp.concatenate(both, axis=1) * scale
        taps_ref[:, i * 2 * HD : (i + 1) * 2 * HD] = both[0:KW]


def finish(recv, width, scale):
    count = recv.shape[0]
    vmem = pl.BlockSpec(memory_space=pltpu.VMEM)
    return pl.pallas_call(
        lambda *refs: finish_kernel(*refs, scale=scale),
        in_specs=[vmem],
        out_shape=[
            jax.ShapeDtypeStruct((HD // count, width), F32),
            jax.ShapeDtypeStruct((KW, width), F32),
        ],
        compiler_params=params(),
        name="finish",
    )(recv)


def exchange(blocks, step):
    pairs = lambda k: [(d, d ^ (step * k)) for d in range(FAST * SLOW)]
    moved = [
        local_memory(lax.ppermute(block, "dp", pairs(k))) for k, block in enumerate(blocks) if k
    ]
    return [blocks[0]] + moved


def local(frames, cotangent, w_qkv, w_out, w_conv, lengths):
    seq_count = lax.axis_size("seq")
    data_count = lax.axis_size("dp")
    rows, width = frames.shape[1:]
    first = lax.axis_index("seq") * rows
    grad_scale = 1.0 / math.sqrt(data_count * rows * seq_count)
    position = lax.axis_index("dp")
    fast = position % FAST
    slow = position // FAST
    place = [fast, slow]
    scalars = jnp.stack([lengths[0], first, jnp.zeros((), jnp.int32)] + place)
    x = frames[0]
    g = cotangent[0]

    forward = [(i, i + 1) for i in range(seq_count - 1)]
    backward = [(i + 1, i) for i in range(seq_count - 1)]
    low = lax.ppermute(jnp.concatenate([x[-HALO:], g[-HALO:]], axis=0), "seq", forward)
    high = lax.ppermute(jnp.concatenate([x[:HALO], g[:HALO]], axis=0), "seq", backward)
    x_side = jnp.concatenate([low[:HALO], high[:HALO]], axis=0)
    g_side = jnp.concatenate([low[HALO:], high[HALO:]], axis=0)

    normed, send = project(x, w_qkv)
    heads = lax.all_to_all(send, "seq", 0, 0, tiled=True)
    heads_near = local_memory(heads)
    normed_all = lax.all_gather(normed, "seq", axis=0, tiled=True)
    send, out, lse = attend(scalars, heads_near)
    att = local_memory(lax.all_to_all(send, "seq", 0, 0, tiled=True))
    output, res_grad, send, *packs = middle(scalars, att, x, x_side, g, g_side, w_out, w_conv)
    back = lax.all_to_all(send, "seq", 0, 0, tiled=True)
    back, packs = lax.optimization_barrier((back, exchange(packs, 1)))
    send = attend_back(scalars, heads, local_memory(back), out, lse)
    joined = lax.all_to_all(send, "seq", 0, 0, tiled=True)
    parts = exchange(gradient_parts(scalars, send, back, normed_all), 1)
    outer = exchange(out_part(scalars, packs), FAST)
    parts = exchange(fold_fast(scalars, parts), FAST)
    qkv, send = fold_slow(parts, outer, seq_count, grad_scale)
    input_grad = input_gradient(joined, w_qkv, x, res_grad)
    recv = lax.all_to_all(send, "seq", 0, 0, tiled=True)
    out_total, taps_total = finish(local_memory(recv), width, grad_scale)
    return (
        output[None],
        input_grad[None],
        qkv.reshape(width // data_count, 3, HD),
        out_total,
        taps_total,
    )


def solution(mesh):
    placed = (P("dp", "seq", None), P("dp", "seq", None), P(), P(), P(), P("dp"))
    return jax.shard_map(
        local,
        mesh=mesh,
        in_specs=placed,
        out_specs=(
            P("dp", "seq", None),
            P("dp", "seq", None),
            P("dp", None, "seq"),
            P(("dp", "seq"), None),
            P(),
        ),
        check_vma=False,
    )
```

```python
import math

import jax
import jax.numpy as jnp
from jax import lax
from jax.experimental import pallas as pl
from jax.experimental.pallas import tpu as pltpu
from jax.sharding import PartitionSpec as P

HEADS = 16
KW = 31
HD = 64
HALO = 32
QB = 256
KB = 256
F32 = jnp.float32
BF16 = jnp.bfloat16
LIMIT = 56 * 1024 * 1024
CUT = 96
FAST = 4
SLOW = 4
TAPS = SLOW * CUT
PARTS = TAPS + KW + 1
OUT = 8 * HD


def dot(a, b, ca=1, cb=0):
    return lax.dot_general(a, b, (((ca,), (cb,)), ((), ())), preferred_element_type=F32)


def normalize(rows):
    center = rows - jnp.mean(rows, axis=-1, keepdims=True)
    scale = lax.rsqrt(jnp.mean(center * center, axis=-1, keepdims=True) + 1e-05)
    return center * scale, scale


def normalize_back(unit, scale, upstream):
    return scale * (
        upstream
        - jnp.mean(upstream, axis=-1, keepdims=True)
        - unit * jnp.mean(upstream * unit, axis=-1, keepdims=True)
    )


def params(**kw):
    return pltpu.CompilerParams(vmem_limit_bytes=LIMIT, **kw)


def cost(flops, moved, expos=0):
    return pl.CostEstimate(flops=flops, bytes_accessed=moved, transcendentals=expos)


def local_memory(array):
    return pltpu.with_memory_space_constraint(array, pltpu.VMEM)


def whole(shape):
    return pl.BlockSpec(shape, lambda *_: (0,) * len(shape))


def halves(exact):
    top = exact.astype(BF16)
    rest = (exact - top.astype(F32)).astype(BF16)
    return jnp.concatenate([top, rest], axis=1)


def joined_halves(pair):
    return pair[:, : pair.shape[1] // 2] + pair[:, pair.shape[1] // 2 :]


SMEM = pl.BlockSpec(memory_space=pltpu.SMEM)


def project_kernel(frames_ref, weight_ref, normed_ref, send_ref):
    @pl.when(pl.program_id(0) == 0)
    def _():
        unit, _ = normalize(frames_ref[...].astype(F32))
        normed_ref[...] = unit.astype(BF16)

    part = dot(normed_ref[...], weight_ref[...]).astype(BF16)
    send_ref[...] = part.T.reshape(send_ref.shape)


def project(frames, w_qkv):
    rows, width = frames.shape
    cols = 512
    per = cols // HD
    groups = HEADS // per
    return pl.pallas_call(
        project_kernel,
        grid=(3 * groups,),
        in_specs=[whole(frames.shape), pl.BlockSpec((width, cols), lambda j: (0, j))],
        out_specs=[
            whole(frames.shape),
            pl.BlockSpec((per, HD, rows), lambda j: (j % groups, j // groups, 0)),
        ],
        out_shape=[
            jax.ShapeDtypeStruct(frames.shape, BF16),
            jax.ShapeDtypeStruct((HEADS, 3 * HD, rows), BF16),
        ],
        compiler_params=params(),
        name="project",
    )(frames, w_qkv)


def load_heads(length, heads_ref, query, keys, count, rows):
    extra = lax.broadcasted_iota(jnp.int32, (HD, rows), 0)
    frame = lax.broadcasted_iota(jnp.int32, (HD, rows), 1)
    for i in range(count):
        cols = slice(i * rows, (i + 1) * rows)
        query[0:HD, cols] = (heads_ref[i, 0:HD, :].astype(F32) * 0.125).astype(BF16)
        query[HD : 2 * HD, cols] = jnp.where(extra == 0, 1.0, 0.0).astype(BF16)
        masked = jnp.logical_and(extra == 0, frame + i * rows >= length)
        mask = jnp.where(masked, -1e30, 0.0).astype(BF16)
        joined = jnp.concatenate([heads_ref[i, HD : 2 * HD, :], mask], axis=0)
        keys[cols, :] = joined.T


def attend_kernel(
    scalars, heads_ref, send_ref, out_ref, lse_ref, query, keys, value, scores
):
    count, _, rows = heads_ref.shape
    total = count * rows
    load_heads(scalars[0], heads_ref, query, keys, count, rows)
    for i in range(count):
        value[:, i * rows : (i + 1) * rows] = heads_ref[i, 2 * HD : 3 * HD, :]

    def one_block(block, carry):
        cols = pl.ds(pl.multiple_of(block * QB, QB), QB)
        query_cols = query[:, cols]
        peak = None
        for k in range(total // KB):
            part = dot(keys[k * KB : (k + 1) * KB, :], query_cols)
            scores[k * KB : (k + 1) * KB, :] = part
            top = jnp.max(part.reshape(KB // 8, 8, QB), axis=0)
            peak = top if peak is None else jnp.maximum(peak, top)
        peak = jnp.max(peak, axis=0, keepdims=True)
        total_row = jnp.zeros((8, QB), F32)
        acc = jnp.zeros((HD, QB), F32)
        for k in range(total // KB):
            expo = jnp.exp(scores[k * KB : (k + 1) * KB, :] - peak)
            total_row = total_row + jnp.sum(expo.reshape(KB // 8, 8, QB), axis=0)
            acc = acc + dot(value[:, k * KB : (k + 1) * KB], expo.astype(BF16))
        total_row = jnp.sum(total_row, axis=0, keepdims=True)
        out_ref[:, cols] = acc / total_row
        lse_ref[:, cols] = peak + jnp.log(total_row)
        return carry

    lax.fori_loop(0, total // QB, one_block, 0)
    none = jnp.zeros((HD, HALO), F32)
    for i in range(count):
        send_ref[i, 0:HD, :] = out_ref[:, i * rows : (i + 1) * rows].astype(BF16)
        low = out_ref[:, i * rows - HALO : i * rows] if i else none
        high = out_ref[:, (i + 1) * rows : (i + 1) * rows + HALO] if i < count - 1 else none
        sides = jnp.concatenate([low, high], axis=1)
        packed = jnp.concatenate([sides[0 : HD // 2], sides[HD // 2 :]], axis=1)
        send_ref[i, HD : HD + HD // 2, :] = packed.astype(BF16)


def attend(scalars, heads):
    count, _, rows = heads.shape
    total = count * rows
    return pl.pallas_call(
        attend_kernel,
        in_specs=[SMEM, pl.BlockSpec(memory_space=pltpu.VMEM)],
        out_shape=[
            jax.ShapeDtypeStruct((count, HD + HD // 2, rows), BF16),
            jax.ShapeDtypeStruct((HD, total), F32),
            jax.ShapeDtypeStruct((1, total), F32),
        ],
        scratch_shapes=[
            pltpu.VMEM((2 * HD, total), BF16),
            pltpu.VMEM((total, 2 * HD), BF16),
            pltpu.VMEM((HD, total), BF16),
            pltpu.VMEM((total, QB), F32),
        ],
        compiler_params=params(),
        cost_estimate=cost(2 * 2 * total * total * 256, heads.size * 2, total * total),
        name="attend",
    )(scalars, heads)


def middle_kernel(
    scalars,
    att_ref,
    frames_ref,
    frames_side,
    grads_ref,
    grads_side,
    w_out_ref,
    w_conv_ref,
    output_ref,
    res_grad_ref,
    send_ref,
    pack_one,
    pack_two,
    pack_three,
    pack_four,
    taps_ref,
    conv_in,
    grad_all,
    residual,
    window,
    window_back,
    conv_grad,
):
    rows, width = frames_ref.shape
    heads = att_ref.shape[0]
    length = scalars[0]
    first = scalars[1]
    zero = scalars[2]
    half = HD // 2
    body = slice(HALO, HALO + rows)

    attended = att_ref[:, 0:HD, :].reshape(width, rows).T
    main = frames_ref[...].astype(F32) + dot(attended, w_out_ref[...])
    packed = att_ref[:, HD : HD + half, :].reshape(heads * half, rows).T
    split_w = w_out_ref[...].reshape(heads, 2, half, width)
    side = dot(packed[0 : 2 * HALO], split_w[:, 0].reshape(heads * half, width))
    side = side + dot(packed[2 * HALO :], split_w[:, 1].reshape(heads * half, width))
    side = frames_side[...].astype(F32) + side

    def keep_of(count, start):
        frame = lax.broadcasted_iota(jnp.int32, (count, 1), 0) + start
        return jnp.where(jnp.logical_and(frame >= 0, frame < length), 1.0, 0.0)

    main = main.astype(BF16).astype(F32)
    residual[...] = main
    unit, scale = normalize(main)
    keep = keep_of(rows, first)
    conv_in[body, :] = (unit * keep).astype(BF16).astype(F32)
    unit_side, _ = normalize(side.astype(BF16).astype(F32))
    low = unit_side[0:HALO] * keep_of(HALO, first - HALO)
    high = unit_side[HALO:] * keep_of(HALO, first + rows)
    conv_in[0:HALO, :] = low.astype(BF16).astype(F32)
    conv_in[HALO + rows :, :] = high.astype(BF16).astype(F32)
    grad_all[0:HALO, :] = grads_side[0:HALO, :].astype(F32)
    grad_all[body, :] = grads_ref[...].astype(F32)
    grad_all[HALO + rows :, :] = grads_side[HALO:, :].astype(F32)

    reach = rows + HALO
    edge = HALO // 2

    def one_chunk(chunk, carry):
        lanes = pl.ds(pl.multiple_of(chunk * 128, 128), 128)
        window[...] = conv_in[:, lanes]
        acc = jnp.zeros((reach, 128), F32)
        for j in range(KW):
            acc = acc + w_conv_ref[j : j + 1, lanes] * window[pl.ds(zero + (1 + j), reach), :]
        gate = jax.nn.sigmoid(acc)
        back = grad_all[edge : edge + reach, lanes] * (gate + acc * gate * (1.0 - gate))
        window_back[...] = back
        gated = acc[edge : edge + rows] * gate[edge : edge + rows]
        output_ref[:, lanes] = (residual[:, lanes] + gated).astype(BF16)
        own = window_back[edge : edge + rows, :]
        acc = jnp.zeros((rows, 128), F32)
        for j in range(KW):
            acc = acc + w_conv_ref[j : j + 1, lanes] * window_back[
                pl.ds(zero + (KW - j), rows), :
            ]
            moved = window[pl.ds(zero + (edge + 1 + j), rows), :]
            taps_ref[j : j + 1, lanes] = jnp.sum(moved * own, axis=0, keepdims=True)
        taps_ref[KW : KW + 1, lanes] = jnp.zeros((1, 128), F32)
        conv_grad[:, lanes] = acc
        return carry

    lax.fori_loop(0, width // 128, one_chunk, 0)
    res_grad = grads_ref[...].astype(F32) + normalize_back(unit, scale, conv_grad[...] * keep)
    res_grad_ref[...] = res_grad
    rounded = res_grad.astype(BF16)
    for k, pack_ref in enumerate((pack_one, pack_two, pack_three, pack_four)):
        pack_ref[:, 0:width] = rounded
        first_head = pl.multiple_of((scalars[4] ^ k) * FAST, FAST)
        picked = att_ref[pl.ds(first_head, FAST), 0:HD, :]
        pack_ref[:, width:] = picked.reshape(FAST * HD, rows).T
    back = dot(w_out_ref[...], rounded, 1, 1).astype(BF16)
    send_ref[:, 0:HD, :] = back.reshape(heads, HD, rows)
    for h in range(heads):
        send_ref[h, HD:, :] = halves(taps_ref[:, h * HD : (h + 1) * HD])


def middle(scalars, att, frames, frames_side, grads, grads_side, w_out, w_conv):
    rows, width = frames.shape
    vmem = pl.BlockSpec(memory_space=pltpu.VMEM)
    return pl.pallas_call(
        middle_kernel,
        in_specs=[SMEM] + [vmem] * 7,
        out_shape=[
            jax.ShapeDtypeStruct((rows, width), BF16),
            jax.ShapeDtypeStruct((rows, width), F32),
            jax.ShapeDtypeStruct((HEADS, HD + KW + 1, rows), BF16),
        ]
        + [jax.ShapeDtypeStruct((rows, width + FAST * HD), BF16)] * SLOW,
        scratch_shapes=[
            pltpu.VMEM((KW + 1, width), F32),
            pltpu.VMEM((rows + 2 * HALO, width), F32),
            pltpu.VMEM((rows + 2 * HALO, width), F32),
            pltpu.VMEM((rows, width), F32),
            pltpu.VMEM((rows + 2 * HALO, 128), F32),
            pltpu.VMEM((rows + HALO, 128), F32),
            pltpu.VMEM((rows, width), F32),
        ],
        compiler_params=params(),
        name="middle",
    )(scalars, att, frames, frames_side, grads, grads_side, w_out, w_conv)


def attend_back_kernel(
    scalars, heads_ref, grads_ref, out_ref, lse_ref, send_ref,
    query, keys, value_t, grad_t, query_rows, grad_rows, query_grad, probs, score_grads,
):
    count, _, rows = heads_ref.shape
    total = count * rows
    load_heads(scalars[0], heads_ref, query, keys, count, rows)
    for i in range(count):
        cols = slice(i * rows, (i + 1) * rows)
        block = grads_ref[i, 0:HD, :]
        grad_t[:, cols] = block
        both = jnp.concatenate([query[0:HD, cols], block], axis=0).T
        query_rows[cols, :] = both[:, 0:HD]
        grad_rows[cols, :] = both[:, HD:]
        value_t[cols, :] = heads_ref[i, 2 * HD : 3 * HD, :].T
    query_grad[...] = jnp.zeros_like(query_grad)
    lse = lse_ref[...]
    delta = jnp.sum(grad_t[...].astype(F32) * out_ref[...], axis=0, keepdims=True)

    def one_block(block, carry):
        span = pl.ds(pl.multiple_of(block * KB, KB), KB)
        key_rows = keys[span, :]
        value_rows = value_t[span, :]
        for q in range(total // QB):
            cols = slice(q * QB, (q + 1) * QB)
            prob = jnp.exp(dot(key_rows, query[:, cols]) - lse[:, cols])
            prob_grad = dot(value_rows, grad_t[:, cols])
            probs[:, cols] = prob.astype(BF16)
            score_grads[:, cols] = (prob * (prob_grad - delta[:, cols])).astype(BF16)
        key_grad = dot(score_grads[...], query_rows[...])
        value_grad = dot(probs[...], grad_rows[...])
        key_cols = key_rows[:, 0:HD].T
        query_grad[...] += dot(key_cols, score_grads[...])
        joined = jnp.concatenate([key_grad, value_grad], axis=1).T.astype(BF16)
        for i in range(KB // rows):
            send_ref[block * (KB // rows) + i, HD : 3 * HD, :] = joined[:, i * rows : (i + 1) * rows]
        return carry

    lax.fori_loop(0, total // KB, one_block, 0)
    for i in range(count):
        cols = slice(i * rows, (i + 1) * rows)
        send_ref[i, 0:HD, :] = (query_grad[:, cols] * 0.125).astype(BF16)


def attend_back(scalars, heads, grads, out, lse):
    count, _, rows = heads.shape
    total = count * rows
    vmem = pl.BlockSpec(memory_space=pltpu.VMEM)
    return pl.pallas_call(
        attend_back_kernel,
        in_specs=[SMEM] + [vmem] * 4,
        out_shape=jax.ShapeDtypeStruct(heads.shape, BF16),
        scratch_shapes=[
            pltpu.VMEM((2 * HD, total), BF16),
            pltpu.VMEM((total, 2 * HD), BF16),
            pltpu.VMEM((total, HD), BF16),
            pltpu.VMEM((HD, total), BF16),
            pltpu.VMEM((total, HD), BF16),
            pltpu.VMEM((total, HD), BF16),
            pltpu.VMEM((HD, total), F32),
            pltpu.VMEM((KB, total), BF16),
            pltpu.VMEM((KB, total), BF16),
        ],
        compiler_params=params(),
        cost_estimate=cost(5 * 2 * total * total * 256, heads.size * 4, total * total),
        name="attend_back",
    )(scalars, heads, grads, out, lse)


def input_grad_kernel(joined_ref, weight_ref, frames_ref, res_grad_ref, out_ref, joined, grads):
    step = pl.program_id(0)
    heads = joined_ref.shape[0]

    @pl.when(step == 0)
    def _():
        for h in range(heads):
            for t in range(3):
                row = (t * heads + h) * HD
                joined[row : row + HD, :] = joined_ref[h, t * HD : (t + 1) * HD, :]

    block = weight_ref.shape[0]
    start = pl.multiple_of(step * block, block)
    grads[pl.ds(start, block), :] = dot(weight_ref[...], joined[...])

    @pl.when(step == pl.num_programs(0) - 1)
    def _():
        unit, scale = normalize(frames_ref[...].astype(F32))
        back = normalize_back(unit, scale, grads[...].T)
        out_ref[...] = (res_grad_ref[...] + back).astype(BF16)


def input_gradient(joined, w_qkv, frames, res_grad):
    rows, width = frames.shape
    block = 256
    return pl.pallas_call(
        input_grad_kernel,
        grid=(width // block,),
        in_specs=[
            pl.BlockSpec(memory_space=pltpu.VMEM),
            pl.BlockSpec((block, w_qkv.shape[1]), lambda j: (j, 0)),
            whole(frames.shape),
            whole(frames.shape),
        ],
        out_specs=whole(frames.shape),
        out_shape=jax.ShapeDtypeStruct(frames.shape, BF16),
        scratch_shapes=[
            pltpu.VMEM((w_qkv.shape[1], rows), BF16),
            pltpu.VMEM((width, rows), F32),
        ],
        compiler_params=params(),
        name="input_gradient",
    )(local_memory(joined), w_qkv, frames, res_grad)


def parts_kernel(scalars, grads_ref, back_ref, normed_ref, one, two, three, four, *rest):
    send_refs, columns, pieces, left, outer = rest[:FAST], *rest[FAST:]
    packs = (one, two, three, four)
    count, wide, rows = grads_ref.shape
    width = one.shape[1] - FAST * HD
    step = pl.program_id(0)

    @pl.when(step == 0)
    def _():
        taps = jnp.zeros((KW + 1, rows), F32)
        for i in range(count):
            columns[:, i * rows : (i + 1) * rows] = grads_ref[i]
            taps = taps + back_ref[i, HD:, :].astype(F32)
        pair = halves(joined_halves(taps))
        for send_ref in send_refs:
            send_ref[TAPS:PARTS, :] = pair
        left[...] = jnp.concatenate([ref[:, width:] for ref in packs], axis=0).T

    part = dot(columns[...], normed_ref[...])
    each = part.shape[1] // FAST
    for i in range(FAST):
        piece = part[:, i * each : (i + 1) * each]
        pieces[i] = jnp.concatenate([piece[0:CUT], piece[CUT:]], axis=1).astype(BF16)
    block = width // SLOW
    lanes = pl.ds(pl.multiple_of(step * block, block), block)
    outer[...] = dot(left[...], jnp.concatenate([ref[:, lanes] for ref in packs], axis=0))
    for k, send_ref in enumerate(send_refs):
        send_ref[pl.ds(pl.multiple_of(step * CUT, CUT), CUT), :] = pieces[scalars[3] ^ k]
        own = pl.ds(pl.multiple_of((scalars[3] ^ k) * HD, HD), HD)
        for c in range(block // 128):
            at = pl.multiple_of(PARTS + (step * (block // 128) + c) * HD, 32)
            send_ref[pl.ds(at, HD), :] = outer[own, c * 128 : (c + 1) * 128].astype(BF16)


def gradient_parts(scalars, grads, back, normed_all, packs):
    count, wide, rows = grads.shape
    total, width = normed_all.shape
    vmem = pl.BlockSpec(memory_space=pltpu.VMEM)
    return pl.pallas_call(
        parts_kernel,
        grid=(SLOW,),
        in_specs=[
            SMEM,
            vmem,
            vmem,
            pl.BlockSpec((total, width // SLOW), lambda j: (0, j)),
        ]
        + [vmem] * SLOW,
        out_specs=[whole((PARTS + OUT, 128))] * FAST,
        out_shape=[jax.ShapeDtypeStruct((PARTS + OUT, 128), BF16)] * FAST,
        scratch_shapes=[
            pltpu.VMEM((wide, total), BF16),
            pltpu.VMEM((FAST, CUT, 128), BF16),
            pltpu.VMEM((FAST * HD, SLOW * rows), BF16),
            pltpu.VMEM((FAST * HD, width // SLOW), F32),
        ],
        compiler_params=params(),
        name="gradient_parts",
    )(scalars, grads, back, normed_all, *packs)


def sum_four(own, one, two, three):
    return (own.astype(F32) + one.astype(F32)) + (two.astype(F32) + three.astype(F32))


def fold_fast_kernel(scalars, one, two, three, four, *rest):
    send_refs, outer_ref, pieces = rest[:SLOW], *rest[SLOW:]
    total = sum_four(one[...], two[...], three[...], four[...])
    outer_ref[...] = total[PARTS:]
    pair = halves(joined_halves(total[TAPS:PARTS]))
    for i in range(SLOW):
        pieces[i] = total[i * CUT : (i + 1) * CUT].astype(BF16)
    for k, send_ref in enumerate(send_refs):
        send_ref[0:CUT, :] = pieces[scalars[4] ^ k]
        send_ref[CUT:, :] = pair


def fold_fast(scalars, blocks):
    vmem = pl.BlockSpec(memory_space=pltpu.VMEM)
    return pl.pallas_call(
        fold_fast_kernel,
        in_specs=[SMEM] + [vmem] * 4,
        out_shape=[jax.ShapeDtypeStruct((CUT + KW + 1, 128), BF16)] * SLOW
        + [jax.ShapeDtypeStruct((OUT, 128), F32)],
        scratch_shapes=[pltpu.VMEM((SLOW, CUT, 128), BF16)],
        compiler_params=params(),
        name="fold_fast",
    )(scalars, *blocks)


def fold_slow_kernel(*refs, scale):
    qkv_ref, send_ref = refs[5:]
    total = sum_four(*(ref[...] for ref in refs[0:4]))
    model_rows = (total[0:CUT] * scale).T
    qkv_ref[:, 0:CUT] = model_rows[0:HD]
    qkv_ref[:, CUT:] = model_rows[HD:]
    pair = halves(joined_halves(total[CUT:]))
    outer = refs[4][...]
    count = send_ref.shape[0]
    each = HD // count
    for i in range(count):
        pieces = [outer[c * HD + i * each : c * HD + (i + 1) * each] for c in range(OUT // HD)]
        send_ref[i, 0 : OUT // count, :] = jnp.concatenate(pieces, axis=0).astype(BF16)
        send_ref[i, OUT // count :, :] = pair


def fold_slow(blocks, outer, seq_count, scale):
    vmem = pl.BlockSpec(memory_space=pltpu.VMEM)
    return pl.pallas_call(
        lambda *refs: fold_slow_kernel(*refs, scale=scale),
        in_specs=[vmem] * 5,
        out_shape=[
            jax.ShapeDtypeStruct((HD, 3 * HD), F32),
            jax.ShapeDtypeStruct((seq_count, OUT // seq_count + KW + 1, 128), BF16),
        ],
        compiler_params=params(),
        name="fold_slow",
    )(*blocks, outer)


def finish_kernel(recv_ref, out_ref, taps_ref, *, scale):
    count = recv_ref.shape[0]
    each = out_ref.shape[0]
    wide = OUT // count
    total = recv_ref[0, 0:wide, :].astype(F32)
    for i in range(1, count):
        total = total + recv_ref[i, 0:wide, :].astype(F32)
    total = total * scale
    for c in range(OUT // HD):
        out_ref[:, c * 128 : (c + 1) * 128] = total[c * each : (c + 1) * each]
    for i in range(count // 2):
        both = [joined_halves(recv_ref[2 * i + k, wide:, :].astype(F32)) for k in range(2)]
        both = jnp.concatenate(both, axis=1) * scale
        taps_ref[:, i * 2 * HD : (i + 1) * 2 * HD] = both[0:KW]


def finish(recv, width, scale):
    count = recv.shape[0]
    vmem = pl.BlockSpec(memory_space=pltpu.VMEM)
    return pl.pallas_call(
        lambda *refs: finish_kernel(*refs, scale=scale),
        in_specs=[vmem],
        out_shape=[
            jax.ShapeDtypeStruct((HD // count, width), F32),
            jax.ShapeDtypeStruct((KW, width), F32),
        ],
        compiler_params=params(),
        name="finish",
    )(recv)


def exchange(blocks, step):
    pairs = lambda k: [(d, d ^ (step * k)) for d in range(FAST * SLOW)]
    moved = [
        local_memory(lax.ppermute(block, "dp", pairs(k))) for k, block in enumerate(blocks) if k
    ]
    return [blocks[0]] + moved


def local(frames, cotangent, w_qkv, w_out, w_conv, lengths):
    seq_count = lax.axis_size("seq")
    data_count = lax.axis_size("dp")
    rows, width = frames.shape[1:]
    first = lax.axis_index("seq") * rows
    grad_scale = 1.0 / math.sqrt(data_count * rows * seq_count)
    position = lax.axis_index("dp")
    fast = position % FAST
    slow = position // FAST
    place = [fast, slow]
    scalars = jnp.stack([lengths[0], first, jnp.zeros((), jnp.int32)] + place)
    x = frames[0]
    g = cotangent[0]

    forward = [(i, i + 1) for i in range(seq_count - 1)]
    backward = [(i + 1, i) for i in range(seq_count - 1)]
    low = lax.ppermute(jnp.concatenate([x[-HALO:], g[-HALO:]], axis=0), "seq", forward)
    high = lax.ppermute(jnp.concatenate([x[:HALO], g[:HALO]], axis=0), "seq", backward)
    x_side = jnp.concatenate([low[:HALO], high[:HALO]], axis=0)
    g_side = jnp.concatenate([low[HALO:], high[HALO:]], axis=0)

    normed, send = project(x, w_qkv)
    heads = lax.all_to_all(send, "seq", 0, 0, tiled=True)
    heads_near = local_memory(heads)
    normed_all = lax.all_gather(normed, "seq", axis=0, tiled=True)
    send, out, lse = attend(scalars, heads_near)
    att = local_memory(lax.all_to_all(send, "seq", 0, 0, tiled=True))
    output, res_grad, send, *packs = middle(scalars, att, x, x_side, g, g_side, w_out, w_conv)
    back = lax.all_to_all(send, "seq", 0, 0, tiled=True)
    back, packs = lax.optimization_barrier((back, exchange(packs, FAST)))
    send = attend_back(scalars, heads, local_memory(back), out, lse)
    joined = lax.all_to_all(send, "seq", 0, 0, tiled=True)
    parts = exchange(gradient_parts(scalars, send, back, normed_all, packs), 1)
    *parts, outer = fold_fast(scalars, parts)
    parts = exchange(parts, FAST)
    qkv, send = fold_slow(parts, outer, seq_count, grad_scale)
    input_grad = input_gradient(joined, w_qkv, x, res_grad)
    recv = lax.all_to_all(send, "seq", 0, 0, tiled=True)
    out_total, taps_total = finish(local_memory(recv), width, grad_scale)
    return (
        output[None],
        input_grad[None],
        qkv.reshape(width // data_count, 3, HD),
        out_total,
        taps_total,
    )


def solution(mesh):
    placed = (P("dp", "seq", None), P("dp", "seq", None), P(), P(), P(), P("dp"))
    return jax.shard_map(
        local,
        mesh=mesh,
        in_specs=placed,
        out_specs=(
            P("dp", "seq", None),
            P("dp", "seq", None),
            P("dp", None, "seq"),
            P(("dp", "seq"), None),
            P(),
        ),
        check_vma=False,
    )
```

```python
import math

import jax
import jax.numpy as jnp
from jax import lax
from jax.experimental import pallas as pl
from jax.experimental.pallas import tpu as pltpu
from jax.sharding import PartitionSpec as P

HEADS = 16
KW = 31
HD = 64
HALO = 32
QB = 256
KB = 256
F32 = jnp.float32
BF16 = jnp.bfloat16
LIMIT = 56 * 1024 * 1024
CUT = 96
FAST = 4
SLOW = 4
TAPS = SLOW * CUT
OUT = 8 * HD


def dot(a, b, ca=1, cb=0):
    return lax.dot_general(a, b, (((ca,), (cb,)), ((), ())), preferred_element_type=F32)


def normalize(rows):
    center = rows - jnp.mean(rows, axis=-1, keepdims=True)
    scale = lax.rsqrt(jnp.mean(center * center, axis=-1, keepdims=True) + 1e-05)
    return center * scale, scale


def normalize_back(unit, scale, upstream):
    return scale * (
        upstream
        - jnp.mean(upstream, axis=-1, keepdims=True)
        - unit * jnp.mean(upstream * unit, axis=-1, keepdims=True)
    )


def params(**kw):
    return pltpu.CompilerParams(vmem_limit_bytes=LIMIT, **kw)


def cost(flops, moved, expos=0):
    return pl.CostEstimate(flops=flops, bytes_accessed=moved, transcendentals=expos)


def local_memory(array):
    return pltpu.with_memory_space_constraint(array, pltpu.VMEM)


def whole(shape):
    return pl.BlockSpec(shape, lambda *_: (0,) * len(shape))


def halves(exact):
    top = exact.astype(BF16)
    rest = (exact - top.astype(F32)).astype(BF16)
    return jnp.concatenate([top, rest], axis=1)


def joined_halves(pair):
    return pair[:, : pair.shape[1] // 2] + pair[:, pair.shape[1] // 2 :]


SMEM = pl.BlockSpec(memory_space=pltpu.SMEM)


def project_kernel(frames_ref, weight_ref, normed_ref, send_ref):
    @pl.when(pl.program_id(0) == 0)
    def _():
        unit, _ = normalize(frames_ref[...].astype(F32))
        normed_ref[...] = unit.astype(BF16)

    part = dot(normed_ref[...], weight_ref[...]).astype(BF16)
    send_ref[...] = part.T.reshape(send_ref.shape)


def project(frames, w_qkv):
    rows, width = frames.shape
    cols = 512
    per = cols // HD
    groups = HEADS // per
    return pl.pallas_call(
        project_kernel,
        grid=(3 * groups,),
        in_specs=[whole(frames.shape), pl.BlockSpec((width, cols), lambda j: (0, j))],
        out_specs=[
            whole(frames.shape),
            pl.BlockSpec((per, HD, rows), lambda j: (j % groups, j // groups, 0)),
        ],
        out_shape=[
            jax.ShapeDtypeStruct(frames.shape, BF16),
            jax.ShapeDtypeStruct((HEADS, 3 * HD, rows), BF16),
        ],
        compiler_params=params(),
        name="project",
    )(frames, w_qkv)


def load_heads(length, heads_ref, query, keys, count, rows):
    extra = lax.broadcasted_iota(jnp.int32, (HD, rows), 0)
    frame = lax.broadcasted_iota(jnp.int32, (HD, rows), 1)
    for i in range(count):
        cols = slice(i * rows, (i + 1) * rows)
        query[0:HD, cols] = (heads_ref[i, 0:HD, :].astype(F32) * 0.125).astype(BF16)
        query[HD : 2 * HD, cols] = jnp.where(extra == 0, 1.0, 0.0).astype(BF16)
        masked = jnp.logical_and(extra == 0, frame + i * rows >= length)
        mask = jnp.where(masked, -1e30, 0.0).astype(BF16)
        joined = jnp.concatenate([heads_ref[i, HD : 2 * HD, :], mask], axis=0)
        keys[cols, :] = joined.T


def attend_kernel(
    scalars, heads_ref, send_ref, out_ref, lse_ref, query, keys, value, scores
):
    count, _, rows = heads_ref.shape
    total = count * rows
    load_heads(scalars[0], heads_ref, query, keys, count, rows)
    for i in range(count):
        value[:, i * rows : (i + 1) * rows] = heads_ref[i, 2 * HD : 3 * HD, :]

    def one_block(block, carry):
        cols = pl.ds(pl.multiple_of(block * QB, QB), QB)
        query_cols = query[:, cols]
        peak = None
        for k in range(total // KB):
            part = dot(keys[k * KB : (k + 1) * KB, :], query_cols)
            scores[k * KB : (k + 1) * KB, :] = part
            top = jnp.max(part.reshape(KB // 8, 8, QB), axis=0)
            peak = top if peak is None else jnp.maximum(peak, top)
        peak = jnp.max(peak, axis=0, keepdims=True)
        total_row = jnp.zeros((8, QB), F32)
        acc = jnp.zeros((HD, QB), F32)
        for k in range(total // KB):
            expo = jnp.exp(scores[k * KB : (k + 1) * KB, :] - peak)
            total_row = total_row + jnp.sum(expo.reshape(KB // 8, 8, QB), axis=0)
            acc = acc + dot(value[:, k * KB : (k + 1) * KB], expo.astype(BF16))
        total_row = jnp.sum(total_row, axis=0, keepdims=True)
        out_ref[:, cols] = acc / total_row
        lse_ref[:, cols] = peak + jnp.log(total_row)
        return carry

    lax.fori_loop(0, total // QB, one_block, 0)
    none = jnp.zeros((HD, HALO), F32)
    for i in range(count):
        send_ref[i, 0:HD, :] = out_ref[:, i * rows : (i + 1) * rows].astype(BF16)
        low = out_ref[:, i * rows - HALO : i * rows] if i else none
        high = out_ref[:, (i + 1) * rows : (i + 1) * rows + HALO] if i < count - 1 else none
        sides = jnp.concatenate([low, high], axis=1)
        packed = jnp.concatenate([sides[0 : HD // 2], sides[HD // 2 :]], axis=1)
        send_ref[i, HD : HD + HD // 2, :] = packed.astype(BF16)


def attend(scalars, heads):
    count, _, rows = heads.shape
    total = count * rows
    return pl.pallas_call(
        attend_kernel,
        in_specs=[SMEM, pl.BlockSpec(memory_space=pltpu.VMEM)],
        out_shape=[
            jax.ShapeDtypeStruct((count, HD + HD // 2, rows), BF16),
            jax.ShapeDtypeStruct((HD, total), F32),
            jax.ShapeDtypeStruct((1, total), F32),
        ],
        scratch_shapes=[
            pltpu.VMEM((2 * HD, total), BF16),
            pltpu.VMEM((total, 2 * HD), BF16),
            pltpu.VMEM((HD, total), BF16),
            pltpu.VMEM((total, QB), F32),
        ],
        compiler_params=params(),
        cost_estimate=cost(2 * 2 * total * total * 256, heads.size * 2, total * total),
        name="attend",
    )(scalars, heads)


def middle_kernel(
    scalars,
    att_ref,
    frames_ref,
    frames_side,
    grads_ref,
    grads_side,
    w_out_ref,
    w_conv_ref,
    output_ref,
    res_grad_ref,
    send_ref,
    pack_ref,
    taps_ref,
    conv_in,
    grad_all,
    residual,
    window,
    window_back,
    conv_grad,
):
    rows, width = frames_ref.shape
    heads = att_ref.shape[0]
    length = scalars[0]
    first = scalars[1]
    zero = scalars[2]
    half = HD // 2
    body = slice(HALO, HALO + rows)

    attended = att_ref[:, 0:HD, :].reshape(width, rows).T
    main = frames_ref[...].astype(F32) + dot(attended, w_out_ref[...])
    packed = att_ref[:, HD : HD + half, :].reshape(heads * half, rows).T
    split_w = w_out_ref[...].reshape(heads, 2, half, width)
    side = dot(packed[0 : 2 * HALO], split_w[:, 0].reshape(heads * half, width))
    side = side + dot(packed[2 * HALO :], split_w[:, 1].reshape(heads * half, width))
    side = frames_side[...].astype(F32) + side

    def keep_of(count, start):
        frame = lax.broadcasted_iota(jnp.int32, (count, 1), 0) + start
        return jnp.where(jnp.logical_and(frame >= 0, frame < length), 1.0, 0.0)

    main = main.astype(BF16).astype(F32)
    residual[...] = main
    unit, scale = normalize(main)
    keep = keep_of(rows, first)
    conv_in[body, :] = (unit * keep).astype(BF16).astype(F32)
    unit_side, _ = normalize(side.astype(BF16).astype(F32))
    low = unit_side[0:HALO] * keep_of(HALO, first - HALO)
    high = unit_side[HALO:] * keep_of(HALO, first + rows)
    conv_in[0:HALO, :] = low.astype(BF16).astype(F32)
    conv_in[HALO + rows :, :] = high.astype(BF16).astype(F32)
    grad_all[0:HALO, :] = grads_side[0:HALO, :].astype(F32)
    grad_all[body, :] = grads_ref[...].astype(F32)
    grad_all[HALO + rows :, :] = grads_side[HALO:, :].astype(F32)

    reach = rows + HALO
    edge = HALO // 2

    def one_chunk(chunk, carry):
        lanes = pl.ds(pl.multiple_of(chunk * 128, 128), 128)
        window[...] = conv_in[:, lanes]
        acc = jnp.zeros((reach, 128), F32)
        for j in range(KW):
            acc = acc + w_conv_ref[j : j + 1, lanes] * window[pl.ds(zero + (1 + j), reach), :]
        gate = jax.nn.sigmoid(acc)
        back = grad_all[edge : edge + reach, lanes] * (gate + acc * gate * (1.0 - gate))
        window_back[...] = back
        gated = acc[edge : edge + rows] * gate[edge : edge + rows]
        output_ref[:, lanes] = (residual[:, lanes] + gated).astype(BF16)
        own = window_back[edge : edge + rows, :]
        acc = jnp.zeros((rows, 128), F32)
        for j in range(KW):
            acc = acc + w_conv_ref[j : j + 1, lanes] * window_back[
                pl.ds(zero + (KW - j), rows), :
            ]
            moved = window[pl.ds(zero + (edge + 1 + j), rows), :]
            taps_ref[j : j + 1, lanes] = jnp.sum(moved * own, axis=0, keepdims=True)
        taps_ref[KW : KW + 1, lanes] = jnp.zeros((1, 128), F32)
        conv_grad[:, lanes] = acc
        return carry

    lax.fori_loop(0, width // 128, one_chunk, 0)
    res_grad = grads_ref[...].astype(F32) + normalize_back(unit, scale, conv_grad[...] * keep)
    res_grad_ref[...] = res_grad
    rounded = res_grad.astype(BF16)
    pack_ref[:, 0:width] = rounded
    pack_ref[:, width:] = attended
    back = dot(w_out_ref[...], rounded, 1, 1).astype(BF16)
    send_ref[:, 0:HD, :] = back.reshape(heads, HD, rows)
    for h in range(heads):
        send_ref[h, HD:, :] = halves(taps_ref[:, h * HD : (h + 1) * HD])


def middle(scalars, att, frames, frames_side, grads, grads_side, w_out, w_conv):
    rows, width = frames.shape
    vmem = pl.BlockSpec(memory_space=pltpu.VMEM)
    return pl.pallas_call(
        middle_kernel,
        in_specs=[SMEM] + [vmem] * 7,
        out_shape=[
            jax.ShapeDtypeStruct((rows, width), BF16),
            jax.ShapeDtypeStruct((rows, width), F32),
            jax.ShapeDtypeStruct((HEADS, HD + KW + 1, rows), BF16),
            jax.ShapeDtypeStruct((rows, 2 * width), BF16),
        ],
        scratch_shapes=[
            pltpu.VMEM((KW + 1, width), F32),
            pltpu.VMEM((rows + 2 * HALO, width), F32),
            pltpu.VMEM((rows + 2 * HALO, width), F32),
            pltpu.VMEM((rows, width), F32),
            pltpu.VMEM((rows + 2 * HALO, 128), F32),
            pltpu.VMEM((rows + HALO, 128), F32),
            pltpu.VMEM((rows, width), F32),
        ],
        compiler_params=params(),
        name="middle",
    )(scalars, att, frames, frames_side, grads, grads_side, w_out, w_conv)


def attend_back_kernel(
    scalars, heads_ref, grads_ref, out_ref, lse_ref, send_ref,
    query, keys, value_t, grad_t, query_rows, grad_rows, query_grad, probs, score_grads,
):
    count, _, rows = heads_ref.shape
    total = count * rows
    load_heads(scalars[0], heads_ref, query, keys, count, rows)
    for i in range(count):
        cols = slice(i * rows, (i + 1) * rows)
        block = grads_ref[i, 0:HD, :]
        grad_t[:, cols] = block
        both = jnp.concatenate([query[0:HD, cols], block], axis=0).T
        query_rows[cols, :] = both[:, 0:HD]
        grad_rows[cols, :] = both[:, HD:]
        value_t[cols, :] = heads_ref[i, 2 * HD : 3 * HD, :].T
    query_grad[...] = jnp.zeros_like(query_grad)
    lse = lse_ref[...]
    delta = jnp.sum(grad_t[...].astype(F32) * out_ref[...], axis=0, keepdims=True)

    def one_block(block, carry):
        span = pl.ds(pl.multiple_of(block * KB, KB), KB)
        key_rows = keys[span, :]
        value_rows = value_t[span, :]
        for q in range(total // QB):
            cols = slice(q * QB, (q + 1) * QB)
            prob = jnp.exp(dot(key_rows, query[:, cols]) - lse[:, cols])
            prob_grad = dot(value_rows, grad_t[:, cols])
            probs[:, cols] = prob.astype(BF16)
            score_grads[:, cols] = (prob * (prob_grad - delta[:, cols])).astype(BF16)
        key_grad = dot(score_grads[...], query_rows[...])
        value_grad = dot(probs[...], grad_rows[...])
        key_cols = key_rows[:, 0:HD].T
        query_grad[...] += dot(key_cols, score_grads[...])
        joined = jnp.concatenate([key_grad, value_grad], axis=1).T.astype(BF16)
        for i in range(KB // rows):
            send_ref[block * (KB // rows) + i, HD : 3 * HD, :] = joined[:, i * rows : (i + 1) * rows]
        return carry

    lax.fori_loop(0, total // KB, one_block, 0)
    for i in range(count):
        cols = slice(i * rows, (i + 1) * rows)
        send_ref[i, 0:HD, :] = (query_grad[:, cols] * 0.125).astype(BF16)


def attend_back(scalars, heads, grads, out, lse):
    count, _, rows = heads.shape
    total = count * rows
    vmem = pl.BlockSpec(memory_space=pltpu.VMEM)
    return pl.pallas_call(
        attend_back_kernel,
        in_specs=[SMEM] + [vmem] * 4,
        out_shape=jax.ShapeDtypeStruct(heads.shape, BF16),
        scratch_shapes=[
            pltpu.VMEM((2 * HD, total), BF16),
            pltpu.VMEM((total, 2 * HD), BF16),
            pltpu.VMEM((total, HD), BF16),
            pltpu.VMEM((HD, total), BF16),
            pltpu.VMEM((total, HD), BF16),
            pltpu.VMEM((total, HD), BF16),
            pltpu.VMEM((HD, total), F32),
            pltpu.VMEM((KB, total), BF16),
            pltpu.VMEM((KB, total), BF16),
        ],
        compiler_params=params(),
        cost_estimate=cost(5 * 2 * total * total * 256, heads.size * 4, total * total),
        name="attend_back",
    )(scalars, heads, grads, out, lse)


def input_grad_kernel(joined_ref, weight_ref, frames_ref, res_grad_ref, out_ref, joined, grads):
    step = pl.program_id(0)
    heads = joined_ref.shape[0]

    @pl.when(step == 0)
    def _():
        for h in range(heads):
            for t in range(3):
                row = (t * heads + h) * HD
                joined[row : row + HD, :] = joined_ref[h, t * HD : (t + 1) * HD, :]

    block = weight_ref.shape[0]
    start = pl.multiple_of(step * block, block)
    grads[pl.ds(start, block), :] = dot(weight_ref[...], joined[...])

    @pl.when(step == pl.num_programs(0) - 1)
    def _():
        unit, scale = normalize(frames_ref[...].astype(F32))
        back = normalize_back(unit, scale, grads[...].T)
        out_ref[...] = (res_grad_ref[...] + back).astype(BF16)


def input_gradient(joined, w_qkv, frames, res_grad):
    rows, width = frames.shape
    block = 256
    return pl.pallas_call(
        input_grad_kernel,
        grid=(width // block,),
        in_specs=[
            pl.BlockSpec(memory_space=pltpu.VMEM),
            pl.BlockSpec((block, w_qkv.shape[1]), lambda j: (j, 0)),
            whole(frames.shape),
            whole(frames.shape),
        ],
        out_specs=whole(frames.shape),
        out_shape=jax.ShapeDtypeStruct(frames.shape, BF16),
        scratch_shapes=[
            pltpu.VMEM((w_qkv.shape[1], rows), BF16),
            pltpu.VMEM((width, rows), F32),
        ],
        compiler_params=params(),
        name="input_gradient",
    )(local_memory(joined), w_qkv, frames, res_grad)


def out_part_kernel(scalars, pack_ref, *rest):
    send_refs, part = rest[:FAST], rest[FAST]
    width = pack_ref.shape[1] // 2
    block = FAST * HD
    first = pl.multiple_of(width + scalars[4] * block, block)
    part[...] = dot(pack_ref[:, pl.ds(first, block)].T, pack_ref[:, 0:width])
    for k, send_ref in enumerate(send_refs):
        rows = pl.ds(pl.multiple_of((scalars[3] ^ k) * HD, HD), HD)
        for c in range(width // 128):
            send_ref[c * HD : (c + 1) * HD, :] = part[rows, c * 128 : (c + 1) * 128].astype(BF16)


def out_part(scalars, packs):
    width = packs.shape[1] // 2
    vmem = pl.BlockSpec(memory_space=pltpu.VMEM)
    return pl.pallas_call(
        out_part_kernel,
        in_specs=[SMEM, vmem],
        out_shape=[jax.ShapeDtypeStruct((OUT, 128), BF16)] * FAST,
        scratch_shapes=[pltpu.VMEM((FAST * HD, width), F32)],
        compiler_params=params(),
        name="out_part",
    )(scalars, packs)


def parts_kernel(scalars, grads_ref, back_ref, normed_ref, *rest):
    send_refs, columns, pieces = rest[:FAST], rest[FAST], rest[FAST + 1]
    count, wide, rows = grads_ref.shape
    slow = pl.program_id(0)

    @pl.when(slow == 0)
    def _():
        taps = jnp.zeros((KW + 1, rows), F32)
        for i in range(count):
            columns[:, i * rows : (i + 1) * rows] = grads_ref[i]
            taps = taps + back_ref[i, HD:, :].astype(F32)
        pair = halves(joined_halves(taps))
        for send_ref in send_refs:
            send_ref[TAPS:, :] = pair

    part = dot(columns[...], normed_ref[...])
    each = part.shape[1] // FAST
    for i in range(FAST):
        piece = part[:, i * each : (i + 1) * each]
        pieces[i] = jnp.concatenate([piece[0:CUT], piece[CUT:]], axis=1).astype(BF16)
    for k, send_ref in enumerate(send_refs):
        send_ref[pl.ds(pl.multiple_of(slow * CUT, CUT), CUT), :] = pieces[scalars[3] ^ k]


def gradient_parts(scalars, grads, back, normed_all):
    count, wide, rows = grads.shape
    total, width = normed_all.shape
    return pl.pallas_call(
        parts_kernel,
        grid=(SLOW,),
        in_specs=[
            SMEM,
            whole(grads.shape),
            whole(back.shape),
            pl.BlockSpec((total, width // SLOW), lambda j: (0, j)),
        ],
        out_specs=[whole((TAPS + KW + 1, 128))] * FAST,
        out_shape=[jax.ShapeDtypeStruct((TAPS + KW + 1, 128), BF16)] * FAST,
        scratch_shapes=[pltpu.VMEM((wide, total), BF16), pltpu.VMEM((FAST, CUT, 128), BF16)],
        compiler_params=params(),
        cost_estimate=cost(2 * 256 * total * width, total * width * 2),
        name="gradient_parts",
    )(scalars, grads, back, normed_all)


def sum_four(own, one, two, three):
    return (own.astype(F32) + one.astype(F32)) + (two.astype(F32) + three.astype(F32))


def fold_fast_kernel(scalars, one, two, three, four, *rest):
    send_refs, pieces = rest[:SLOW], rest[SLOW]
    total = sum_four(one[...], two[...], three[...], four[...])
    pair = halves(joined_halves(total[TAPS:]))
    for i in range(SLOW):
        pieces[i] = total[i * CUT : (i + 1) * CUT].astype(BF16)
    for k, send_ref in enumerate(send_refs):
        send_ref[0:CUT, :] = pieces[scalars[4] ^ k]
        send_ref[CUT:, :] = pair


def fold_fast(scalars, blocks):
    vmem = pl.BlockSpec(memory_space=pltpu.VMEM)
    return pl.pallas_call(
        fold_fast_kernel,
        in_specs=[SMEM] + [vmem] * 4,
        out_shape=[jax.ShapeDtypeStruct((CUT + KW + 1, 128), BF16)] * SLOW,
        scratch_shapes=[pltpu.VMEM((SLOW, CUT, 128), BF16)],
        compiler_params=params(),
        name="fold_fast",
    )(scalars, *blocks)


def fold_slow_kernel(*refs, scale):
    qkv_ref, send_ref = refs[8:]
    total = sum_four(*(ref[...] for ref in refs[0:4]))
    model_rows = (total[0:CUT] * scale).T
    qkv_ref[:, 0:CUT] = model_rows[0:HD]
    qkv_ref[:, CUT:] = model_rows[HD:]
    pair = halves(joined_halves(total[CUT:]))
    outer = sum_four(*(ref[...] for ref in refs[4:8]))
    count = send_ref.shape[0]
    each = HD // count
    for i in range(count):
        pieces = [outer[c * HD + i * each : c * HD + (i + 1) * each] for c in range(OUT // HD)]
        send_ref[i, 0 : OUT // count, :] = jnp.concatenate(pieces, axis=0).astype(BF16)
        send_ref[i, OUT // count :, :] = pair


def fold_slow(blocks, out_blocks, seq_count, scale):
    vmem = pl.BlockSpec(memory_space=pltpu.VMEM)
    return pl.pallas_call(
        lambda *refs: fold_slow_kernel(*refs, scale=scale),
        in_specs=[vmem] * 8,
        out_shape=[
            jax.ShapeDtypeStruct((HD, 3 * HD), F32),
            jax.ShapeDtypeStruct((seq_count, OUT // seq_count + KW + 1, 128), BF16),
        ],
        compiler_params=params(),
        name="fold_slow",
    )(*blocks, *out_blocks)


def finish_kernel(recv_ref, out_ref, taps_ref, *, scale):
    count = recv_ref.shape[0]
    each = out_ref.shape[0]
    wide = OUT // count
    total = recv_ref[0, 0:wide, :].astype(F32)
    for i in range(1, count):
        total = total + recv_ref[i, 0:wide, :].astype(F32)
    total = total * scale
    for c in range(OUT // HD):
        out_ref[:, c * 128 : (c + 1) * 128] = total[c * each : (c + 1) * each]
    for i in range(count // 2):
        both = [joined_halves(recv_ref[2 * i + k, wide:, :].astype(F32)) for k in range(2)]
        both = jnp.concatenate(both, axis=1) * scale
        taps_ref[:, i * 2 * HD : (i + 1) * 2 * HD] = both[0:KW]


def finish(recv, width, scale):
    count = recv.shape[0]
    vmem = pl.BlockSpec(memory_space=pltpu.VMEM)
    return pl.pallas_call(
        lambda *refs: finish_kernel(*refs, scale=scale),
        in_specs=[vmem],
        out_shape=[
            jax.ShapeDtypeStruct((HD // count, width), F32),
            jax.ShapeDtypeStruct((KW, width), F32),
        ],
        compiler_params=params(),
        name="finish",
    )(recv)


def exchange(blocks, step):
    pairs = lambda k: [(d, d ^ (step * k)) for d in range(FAST * SLOW)]
    moved = [
        local_memory(lax.ppermute(block, "dp", pairs(k))) for k, block in enumerate(blocks) if k
    ]
    return [blocks[0]] + moved


def local(frames, cotangent, w_qkv, w_out, w_conv, lengths):
    seq_count = lax.axis_size("seq")
    data_count = lax.axis_size("dp")
    rows, width = frames.shape[1:]
    first = lax.axis_index("seq") * rows
    grad_scale = 1.0 / math.sqrt(data_count * rows * seq_count)
    position = lax.axis_index("dp")
    fast = position % FAST
    slow = position // FAST
    place = [fast, slow]
    scalars = jnp.stack([lengths[0], first, jnp.zeros((), jnp.int32)] + place)
    x = frames[0]
    g = cotangent[0]

    forward = [(i, i + 1) for i in range(seq_count - 1)]
    backward = [(i + 1, i) for i in range(seq_count - 1)]
    low = lax.ppermute(jnp.concatenate([x[-HALO:], g[-HALO:]], axis=0), "seq", forward)
    high = lax.ppermute(jnp.concatenate([x[:HALO], g[:HALO]], axis=0), "seq", backward)
    x_side = jnp.concatenate([low[:HALO], high[:HALO]], axis=0)
    g_side = jnp.concatenate([low[HALO:], high[HALO:]], axis=0)

    normed, send = project(x, w_qkv)
    heads = lax.all_to_all(send, "seq", 0, 0, tiled=True)
    heads_near = local_memory(heads)
    normed_all = lax.all_gather(normed, "seq", axis=0, tiled=True)
    send, out, lse = attend(scalars, heads_near)
    att = local_memory(lax.all_to_all(send, "seq", 0, 0, tiled=True))
    output, res_grad, send, pack = middle(scalars, att, x, x_side, g, g_side, w_out, w_conv)
    back = lax.all_to_all(send, "seq", 0, 0, tiled=True)
    far = [[FAST * i + j for i in range(SLOW)] for j in range(FAST)]
    packs = lax.all_gather(pack, "dp", axis=0, axis_index_groups=far, tiled=True)
    send = attend_back(scalars, heads, local_memory(back), out, lse)
    joined = lax.all_to_all(send, "seq", 0, 0, tiled=True)
    parts = exchange(gradient_parts(scalars, send, back, normed_all), 1)
    outer = exchange(out_part(scalars, packs), 1)
    parts = exchange(fold_fast(scalars, parts), FAST)
    qkv, send = fold_slow(parts, outer, seq_count, grad_scale)
    input_grad = input_gradient(joined, w_qkv, x, res_grad)
    recv = lax.all_to_all(send, "seq", 0, 0, tiled=True)
    out_total, taps_total = finish(local_memory(recv), width, grad_scale)
    return (
        output[None],
        input_grad[None],
        qkv.reshape(width // data_count, 3, HD),
        out_total,
        taps_total,
    )


def solution(mesh):
    placed = (P("dp", "seq", None), P("dp", "seq", None), P(), P(), P(), P("dp"))
    return jax.shard_map(
        local,
        mesh=mesh,
        in_specs=placed,
        out_specs=(
            P("dp", "seq", None),
            P("dp", "seq", None),
            P("dp", None, "seq"),
            P(("dp", "seq"), None),
            P(),
        ),
        check_vma=False,
    )
```

```python
import math

import jax
import jax.numpy as jnp
from jax import lax
from jax.experimental import pallas as pl
from jax.experimental.pallas import tpu as pltpu
from jax.sharding import PartitionSpec as P

HEADS = 16
KW = 31
HD = 64
HALO = 32
QB = 256
KB = 256
F32 = jnp.float32
BF16 = jnp.bfloat16
LIMIT = 56 * 1024 * 1024
CUT = 96
FAST = 4
SLOW = 4
TAPS = SLOW * CUT
OUT = 8 * HD


def dot(a, b, ca=1, cb=0):
    return lax.dot_general(a, b, (((ca,), (cb,)), ((), ())), preferred_element_type=F32)


def normalize(rows):
    center = rows - jnp.mean(rows, axis=-1, keepdims=True)
    scale = lax.rsqrt(jnp.mean(center * center, axis=-1, keepdims=True) + 1e-05)
    return center * scale, scale


def normalize_back(unit, scale, upstream):
    return scale * (
        upstream
        - jnp.mean(upstream, axis=-1, keepdims=True)
        - unit * jnp.mean(upstream * unit, axis=-1, keepdims=True)
    )


def params(**kw):
    return pltpu.CompilerParams(vmem_limit_bytes=LIMIT, **kw)


def cost(flops, moved, expos=0):
    return pl.CostEstimate(flops=flops, bytes_accessed=moved, transcendentals=expos)


def local_memory(array):
    return pltpu.with_memory_space_constraint(array, pltpu.VMEM)


def whole(shape):
    return pl.BlockSpec(shape, lambda *_: (0,) * len(shape))


def halves(exact):
    top = exact.astype(BF16)
    rest = (exact - top.astype(F32)).astype(BF16)
    return jnp.concatenate([top, rest], axis=1)


def joined_halves(pair):
    return pair[:, : pair.shape[1] // 2] + pair[:, pair.shape[1] // 2 :]


SMEM = pl.BlockSpec(memory_space=pltpu.SMEM)


def project_kernel(frames_ref, weight_ref, normed_ref, send_ref):
    @pl.when(pl.program_id(0) == 0)
    def _():
        unit, _ = normalize(frames_ref[...].astype(F32))
        normed_ref[...] = unit.astype(BF16)

    part = dot(normed_ref[...], weight_ref[...]).astype(BF16)
    send_ref[...] = part.T.reshape(send_ref.shape)


def project(frames, w_qkv):
    rows, width = frames.shape
    cols = 512
    per = cols // HD
    groups = HEADS // per
    return pl.pallas_call(
        project_kernel,
        grid=(3 * groups,),
        in_specs=[whole(frames.shape), pl.BlockSpec((width, cols), lambda j: (0, j))],
        out_specs=[
            whole(frames.shape),
            pl.BlockSpec((per, HD, rows), lambda j: (j % groups, j // groups, 0)),
        ],
        out_shape=[
            jax.ShapeDtypeStruct(frames.shape, BF16),
            jax.ShapeDtypeStruct((HEADS, 3 * HD, rows), BF16),
        ],
        compiler_params=params(),
        name="project",
    )(frames, w_qkv)


def load_heads(length, heads_ref, query, keys, count, rows):
    extra = lax.broadcasted_iota(jnp.int32, (HD, rows), 0)
    frame = lax.broadcasted_iota(jnp.int32, (HD, rows), 1)
    for i in range(count):
        cols = slice(i * rows, (i + 1) * rows)
        query[0:HD, cols] = (heads_ref[i, 0:HD, :].astype(F32) * 0.125).astype(BF16)
        query[HD : 2 * HD, cols] = jnp.where(extra == 0, 1.0, 0.0).astype(BF16)
        masked = jnp.logical_and(extra == 0, frame + i * rows >= length)
        mask = jnp.where(masked, -1e30, 0.0).astype(BF16)
        joined = jnp.concatenate([heads_ref[i, HD : 2 * HD, :], mask], axis=0)
        keys[cols, :] = joined.T


def attend_kernel(
    scalars, heads_ref, send_ref, out_ref, lse_ref, query, keys, value, scores
):
    count, _, rows = heads_ref.shape
    total = count * rows
    load_heads(scalars[0], heads_ref, query, keys, count, rows)
    for i in range(count):
        value[:, i * rows : (i + 1) * rows] = heads_ref[i, 2 * HD : 3 * HD, :]

    def one_block(block, carry):
        cols = pl.ds(pl.multiple_of(block * QB, QB), QB)
        query_cols = query[:, cols]
        peak = None
        for k in range(total // KB):
            part = dot(keys[k * KB : (k + 1) * KB, :], query_cols)
            scores[k * KB : (k + 1) * KB, :] = part
            top = jnp.max(part.reshape(KB // 8, 8, QB), axis=0)
            peak = top if peak is None else jnp.maximum(peak, top)
        peak = jnp.max(peak, axis=0, keepdims=True)
        total_row = jnp.zeros((8, QB), F32)
        acc = jnp.zeros((HD, QB), F32)
        for k in range(total // KB):
            expo = jnp.exp(scores[k * KB : (k + 1) * KB, :] - peak)
            total_row = total_row + jnp.sum(expo.reshape(KB // 8, 8, QB), axis=0)
            acc = acc + dot(value[:, k * KB : (k + 1) * KB], expo.astype(BF16))
        total_row = jnp.sum(total_row, axis=0, keepdims=True)
        out_ref[:, cols] = acc / total_row
        lse_ref[:, cols] = peak + jnp.log(total_row)
        return carry

    lax.fori_loop(0, total // QB, one_block, 0)
    none = jnp.zeros((HD, HALO), F32)
    for i in range(count):
        send_ref[i, 0:HD, :] = out_ref[:, i * rows : (i + 1) * rows].astype(BF16)
        low = out_ref[:, i * rows - HALO : i * rows] if i else none
        high = out_ref[:, (i + 1) * rows : (i + 1) * rows + HALO] if i < count - 1 else none
        sides = jnp.concatenate([low, high], axis=1)
        packed = jnp.concatenate([sides[0 : HD // 2], sides[HD // 2 :]], axis=1)
        send_ref[i, HD : HD + HD // 2, :] = packed.astype(BF16)


def attend(scalars, heads):
    count, _, rows = heads.shape
    total = count * rows
    return pl.pallas_call(
        attend_kernel,
        in_specs=[SMEM, pl.BlockSpec(memory_space=pltpu.VMEM)],
        out_shape=[
            jax.ShapeDtypeStruct((count, HD + HD // 2, rows), BF16),
            jax.ShapeDtypeStruct((HD, total), F32),
            jax.ShapeDtypeStruct((1, total), F32),
        ],
        scratch_shapes=[
            pltpu.VMEM((2 * HD, total), BF16),
            pltpu.VMEM((total, 2 * HD), BF16),
            pltpu.VMEM((HD, total), BF16),
            pltpu.VMEM((total, QB), F32),
        ],
        compiler_params=params(),
        cost_estimate=cost(2 * 2 * total * total * 256, heads.size * 2, total * total),
        name="attend",
    )(scalars, heads)


def middle_kernel(
    scalars,
    att_ref,
    frames_ref,
    frames_side,
    grads_ref,
    grads_side,
    w_out_ref,
    w_conv_ref,
    output_ref,
    res_grad_ref,
    send_ref,
    pack_ref,
    taps_ref,
    conv_in,
    grad_all,
    residual,
    window,
    window_back,
    conv_grad,
):
    rows, width = frames_ref.shape
    heads = att_ref.shape[0]
    length = scalars[0]
    first = scalars[1]
    zero = scalars[2]
    half = HD // 2
    body = slice(HALO, HALO + rows)

    attended = att_ref[:, 0:HD, :].reshape(width, rows).T
    main = frames_ref[...].astype(F32) + dot(attended, w_out_ref[...])
    packed = att_ref[:, HD : HD + half, :].reshape(heads * half, rows).T
    split_w = w_out_ref[...].reshape(heads, 2, half, width)
    side = dot(packed[0 : 2 * HALO], split_w[:, 0].reshape(heads * half, width))
    side = side + dot(packed[2 * HALO :], split_w[:, 1].reshape(heads * half, width))
    side = frames_side[...].astype(F32) + side

    def keep_of(count, start):
        frame = lax.broadcasted_iota(jnp.int32, (count, 1), 0) + start
        return jnp.where(jnp.logical_and(frame >= 0, frame < length), 1.0, 0.0)

    main = main.astype(BF16).astype(F32)
    residual[...] = main
    unit, scale = normalize(main)
    keep = keep_of(rows, first)
    conv_in[body, :] = (unit * keep).astype(BF16).astype(F32)
    unit_side, _ = normalize(side.astype(BF16).astype(F32))
    low = unit_side[0:HALO] * keep_of(HALO, first - HALO)
    high = unit_side[HALO:] * keep_of(HALO, first + rows)
    conv_in[0:HALO, :] = low.astype(BF16).astype(F32)
    conv_in[HALO + rows :, :] = high.astype(BF16).astype(F32)
    grad_all[0:HALO, :] = grads_side[0:HALO, :].astype(F32)
    grad_all[body, :] = grads_ref[...].astype(F32)
    grad_all[HALO + rows :, :] = grads_side[HALO:, :].astype(F32)

    reach = rows + HALO
    edge = HALO // 2

    def one_chunk(chunk, carry):
        lanes = pl.ds(pl.multiple_of(chunk * 128, 128), 128)
        window[...] = conv_in[:, lanes]
        acc = jnp.zeros((reach, 128), F32)
        for j in range(KW):
            acc = acc + w_conv_ref[j : j + 1, lanes] * window[pl.ds(zero + (1 + j), reach), :]
        gate = jax.nn.sigmoid(acc)
        back = grad_all[edge : edge + reach, lanes] * (gate + acc * gate * (1.0 - gate))
        window_back[...] = back
        gated = acc[edge : edge + rows] * gate[edge : edge + rows]
        output_ref[:, lanes] = (residual[:, lanes] + gated).astype(BF16)
        own = window_back[edge : edge + rows, :]
        acc = jnp.zeros((rows, 128), F32)
        for j in range(KW):
            acc = acc + w_conv_ref[j : j + 1, lanes] * window_back[
                pl.ds(zero + (KW - j), rows), :
            ]
            moved = window[pl.ds(zero + (edge + 1 + j), rows), :]
            taps_ref[j : j + 1, lanes] = jnp.sum(moved * own, axis=0, keepdims=True)
        taps_ref[KW : KW + 1, lanes] = jnp.zeros((1, 128), F32)
        conv_grad[:, lanes] = acc
        return carry

    lax.fori_loop(0, width // 128, one_chunk, 0)
    res_grad = grads_ref[...].astype(F32) + normalize_back(unit, scale, conv_grad[...] * keep)
    res_grad_ref[...] = res_grad
    rounded = res_grad.astype(BF16)
    pack_ref[:, 0:width] = rounded
    pack_ref[:, width:] = attended
    back = dot(w_out_ref[...], rounded, 1, 1).astype(BF16)
    send_ref[:, 0:HD, :] = back.reshape(heads, HD, rows)
    for h in range(heads):
        own = taps_ref[:, h * HD : (h + 1) * HD]
        middle_row = (KW + 1) // 2
        own = jnp.concatenate([own[0:middle_row], own[middle_row:]], axis=1)
        send_ref[h, HD:, :] = own.astype(BF16)


def middle(scalars, att, frames, frames_side, grads, grads_side, w_out, w_conv):
    rows, width = frames.shape
    vmem = pl.BlockSpec(memory_space=pltpu.VMEM)
    return pl.pallas_call(
        middle_kernel,
        in_specs=[SMEM] + [vmem] * 7,
        out_shape=[
            jax.ShapeDtypeStruct((rows, width), BF16),
            jax.ShapeDtypeStruct((rows, width), F32),
            jax.ShapeDtypeStruct((HEADS, HD + (KW + 1) // 2, rows), BF16),
            jax.ShapeDtypeStruct((rows, 2 * width), BF16),
        ],
        scratch_shapes=[
            pltpu.VMEM((KW + 1, width), F32),
            pltpu.VMEM((rows + 2 * HALO, width), F32),
            pltpu.VMEM((rows + 2 * HALO, width), F32),
            pltpu.VMEM((rows, width), F32),
            pltpu.VMEM((rows + 2 * HALO, 128), F32),
            pltpu.VMEM((rows + HALO, 128), F32),
            pltpu.VMEM((rows, width), F32),
        ],
        compiler_params=params(),
        name="middle",
    )(scalars, att, frames, frames_side, grads, grads_side, w_out, w_conv)


def attend_back_kernel(
    scalars, heads_ref, grads_ref, out_ref, lse_ref, send_ref,
    query, keys, value_t, grad_t, query_rows, grad_rows, query_grad, probs, score_grads,
):
    count, _, rows = heads_ref.shape
    total = count * rows
    load_heads(scalars[0], heads_ref, query, keys, count, rows)
    for i in range(count):
        cols = slice(i * rows, (i + 1) * rows)
        block = grads_ref[i, 0:HD, :]
        grad_t[:, cols] = block
        both = jnp.concatenate([query[0:HD, cols], block], axis=0).T
        query_rows[cols, :] = both[:, 0:HD]
        grad_rows[cols, :] = both[:, HD:]
        value_t[cols, :] = heads_ref[i, 2 * HD : 3 * HD, :].T
    query_grad[...] = jnp.zeros_like(query_grad)
    lse = lse_ref[...]
    delta = jnp.sum(grad_t[...].astype(F32) * out_ref[...], axis=0, keepdims=True)

    def one_block(block, carry):
        span = pl.ds(pl.multiple_of(block * KB, KB), KB)
        key_rows = keys[span, :]
        value_rows = value_t[span, :]
        for q in range(total // QB):
            cols = slice(q * QB, (q + 1) * QB)
            prob = jnp.exp(dot(key_rows, query[:, cols]) - lse[:, cols])
            prob_grad = dot(value_rows, grad_t[:, cols])
            probs[:, cols] = prob.astype(BF16)
            score_grads[:, cols] = (prob * (prob_grad - delta[:, cols])).astype(BF16)
        key_grad = dot(score_grads[...], query_rows[...])
        value_grad = dot(probs[...], grad_rows[...])
        key_cols = key_rows[:, 0:HD].T
        query_grad[...] += dot(key_cols, score_grads[...])
        joined = jnp.concatenate([key_grad, value_grad], axis=1).T.astype(BF16)
        for i in range(KB // rows):
            send_ref[block * (KB // rows) + i, HD : 3 * HD, :] = joined[:, i * rows : (i + 1) * rows]
        return carry

    lax.fori_loop(0, total // KB, one_block, 0)
    for i in range(count):
        cols = slice(i * rows, (i + 1) * rows)
        send_ref[i, 0:HD, :] = (query_grad[:, cols] * 0.125).astype(BF16)


def attend_back(scalars, heads, grads, out, lse):
    count, _, rows = heads.shape
    total = count * rows
    vmem = pl.BlockSpec(memory_space=pltpu.VMEM)
    return pl.pallas_call(
        attend_back_kernel,
        in_specs=[SMEM] + [vmem] * 4,
        out_shape=jax.ShapeDtypeStruct(heads.shape, BF16),
        scratch_shapes=[
            pltpu.VMEM((2 * HD, total), BF16),
            pltpu.VMEM((total, 2 * HD), BF16),
            pltpu.VMEM((total, HD), BF16),
            pltpu.VMEM((HD, total), BF16),
            pltpu.VMEM((total, HD), BF16),
            pltpu.VMEM((total, HD), BF16),
            pltpu.VMEM((HD, total), F32),
            pltpu.VMEM((KB, total), BF16),
            pltpu.VMEM((KB, total), BF16),
        ],
        compiler_params=params(),
        cost_estimate=cost(5 * 2 * total * total * 256, heads.size * 4, total * total),
        name="attend_back",
    )(scalars, heads, grads, out, lse)


def input_grad_kernel(joined_ref, weight_ref, frames_ref, res_grad_ref, out_ref, joined, grads):
    step = pl.program_id(0)
    heads = joined_ref.shape[0]

    @pl.when(step == 0)
    def _():
        for h in range(heads):
            for t in range(3):
                row = (t * heads + h) * HD
                joined[row : row + HD, :] = joined_ref[h, t * HD : (t + 1) * HD, :]

    block = weight_ref.shape[0]
    start = pl.multiple_of(step * block, block)
    grads[pl.ds(start, block), :] = dot(weight_ref[...], joined[...])

    @pl.when(step == pl.num_programs(0) - 1)
    def _():
        unit, scale = normalize(frames_ref[...].astype(F32))
        back = normalize_back(unit, scale, grads[...].T)
        out_ref[...] = (res_grad_ref[...] + back).astype(BF16)


def input_gradient(joined, w_qkv, frames, res_grad):
    rows, width = frames.shape
    block = 256
    return pl.pallas_call(
        input_grad_kernel,
        grid=(width // block,),
        in_specs=[
            pl.BlockSpec(memory_space=pltpu.VMEM),
            pl.BlockSpec((block, w_qkv.shape[1]), lambda j: (j, 0)),
            whole(frames.shape),
            whole(frames.shape),
        ],
        out_specs=whole(frames.shape),
        out_shape=jax.ShapeDtypeStruct(frames.shape, BF16),
        scratch_shapes=[
            pltpu.VMEM((w_qkv.shape[1], rows), BF16),
            pltpu.VMEM((width, rows), F32),
        ],
        compiler_params=params(),
        name="input_gradient",
    )(local_memory(joined), w_qkv, frames, res_grad)


def out_part_kernel(scalars, pack_ref, *rest):
    send_refs, part = rest[:FAST], rest[FAST]
    width = pack_ref.shape[1] // 2
    block = FAST * HD
    first = pl.multiple_of(width + scalars[4] * block, block)
    part[...] = dot(pack_ref[:, pl.ds(first, block)].T, pack_ref[:, 0:width])
    for k, send_ref in enumerate(send_refs):
        rows = pl.ds(pl.multiple_of((scalars[3] ^ k) * HD, HD), HD)
        for c in range(width // 128):
            send_ref[c * HD : (c + 1) * HD, :] = part[rows, c * 128 : (c + 1) * 128].astype(BF16)


def out_part(scalars, packs):
    width = packs.shape[1] // 2
    vmem = pl.BlockSpec(memory_space=pltpu.VMEM)
    return pl.pallas_call(
        out_part_kernel,
        in_specs=[SMEM, vmem],
        out_shape=[jax.ShapeDtypeStruct((OUT, 128), BF16)] * FAST,
        scratch_shapes=[pltpu.VMEM((FAST * HD, width), F32)],
        compiler_params=params(),
        name="out_part",
    )(scalars, packs)


def parts_kernel(scalars, grads_ref, back_ref, normed_ref, *rest):
    send_refs, columns, pieces = rest[:FAST], rest[FAST], rest[FAST + 1]
    count, wide, rows = grads_ref.shape
    slow = pl.program_id(0)

    @pl.when(slow == 0)
    def _():
        taps = jnp.zeros(((KW + 1) // 2, rows), F32)
        for i in range(count):
            columns[:, i * rows : (i + 1) * rows] = grads_ref[i]
            taps = taps + back_ref[i, HD:, :].astype(F32)
        pair = halves(jnp.concatenate([taps[:, 0:HD], taps[:, HD:]], axis=0))
        for send_ref in send_refs:
            send_ref[TAPS:, :] = pair

    part = dot(columns[...], normed_ref[...])
    each = part.shape[1] // FAST
    for i in range(FAST):
        piece = part[:, i * each : (i + 1) * each]
        pieces[i] = jnp.concatenate([piece[0:CUT], piece[CUT:]], axis=1).astype(BF16)
    for k, send_ref in enumerate(send_refs):
        send_ref[pl.ds(pl.multiple_of(slow * CUT, CUT), CUT), :] = pieces[scalars[3] ^ k]


def gradient_parts(scalars, grads, back, normed_all):
    count, wide, rows = grads.shape
    total, width = normed_all.shape
    return pl.pallas_call(
        parts_kernel,
        grid=(SLOW,),
        in_specs=[
            SMEM,
            whole(grads.shape),
            whole(back.shape),
            pl.BlockSpec((total, width // SLOW), lambda j: (0, j)),
        ],
        out_specs=[whole((TAPS + KW + 1, 128))] * FAST,
        out_shape=[jax.ShapeDtypeStruct((TAPS + KW + 1, 128), BF16)] * FAST,
        scratch_shapes=[pltpu.VMEM((wide, total), BF16), pltpu.VMEM((FAST, CUT, 128), BF16)],
        compiler_params=params(),
        cost_estimate=cost(2 * 256 * total * width, total * width * 2),
        name="gradient_parts",
    )(scalars, grads, back, normed_all)


def sum_four(own, one, two, three):
    return (own.astype(F32) + one.astype(F32)) + (two.astype(F32) + three.astype(F32))


def fold_fast_kernel(scalars, one, two, three, four, *rest):
    send_refs, pieces = rest[:SLOW], rest[SLOW]
    total = sum_four(one[...], two[...], three[...], four[...])
    pair = halves(joined_halves(total[TAPS:]))
    for i in range(SLOW):
        pieces[i] = total[i * CUT : (i + 1) * CUT].astype(BF16)
    for k, send_ref in enumerate(send_refs):
        send_ref[0:CUT, :] = pieces[scalars[4] ^ k]
        send_ref[CUT:, :] = pair


def fold_fast(scalars, blocks):
    vmem = pl.BlockSpec(memory_space=pltpu.VMEM)
    return pl.pallas_call(
        fold_fast_kernel,
        in_specs=[SMEM] + [vmem] * 4,
        out_shape=[jax.ShapeDtypeStruct((CUT + KW + 1, 128), BF16)] * SLOW,
        scratch_shapes=[pltpu.VMEM((SLOW, CUT, 128), BF16)],
        compiler_params=params(),
        name="fold_fast",
    )(scalars, *blocks)


def fold_slow_kernel(*refs, scale):
    qkv_ref, send_ref = refs[8:]
    total = sum_four(*(ref[...] for ref in refs[0:4]))
    model_rows = (total[0:CUT] * scale).T
    qkv_ref[:, 0:CUT] = model_rows[0:HD]
    qkv_ref[:, CUT:] = model_rows[HD:]
    pair = halves(joined_halves(total[CUT:]))
    outer = sum_four(*(ref[...] for ref in refs[4:8]))
    count = send_ref.shape[0]
    each = HD // count
    for i in range(count):
        pieces = [outer[c * HD + i * each : c * HD + (i + 1) * each] for c in range(OUT // HD)]
        send_ref[i, 0 : OUT // count, :] = jnp.concatenate(pieces, axis=0).astype(BF16)
        send_ref[i, OUT // count :, :] = pair


def fold_slow(blocks, out_blocks, seq_count, scale):
    vmem = pl.BlockSpec(memory_space=pltpu.VMEM)
    return pl.pallas_call(
        lambda *refs: fold_slow_kernel(*refs, scale=scale),
        in_specs=[vmem] * 8,
        out_shape=[
            jax.ShapeDtypeStruct((HD, 3 * HD), F32),
            jax.ShapeDtypeStruct((seq_count, OUT // seq_count + KW + 1, 128), BF16),
        ],
        compiler_params=params(),
        name="fold_slow",
    )(*blocks, *out_blocks)


def finish_kernel(recv_ref, out_ref, taps_ref, *, scale):
    count = recv_ref.shape[0]
    each = out_ref.shape[0]
    wide = OUT // count
    total = recv_ref[0, 0:wide, :].astype(F32)
    for i in range(1, count):
        total = total + recv_ref[i, 0:wide, :].astype(F32)
    total = total * scale
    for c in range(OUT // HD):
        out_ref[:, c * 128 : (c + 1) * 128] = total[c * each : (c + 1) * each]
    for i in range(count // 2):
        both = [joined_halves(recv_ref[2 * i + k, wide:, :].astype(F32)) for k in range(2)]
        both = jnp.concatenate(both, axis=1) * scale
        taps_ref[:, i * 2 * HD : (i + 1) * 2 * HD] = both[0:KW]


def finish(recv, width, scale):
    count = recv.shape[0]
    vmem = pl.BlockSpec(memory_space=pltpu.VMEM)
    return pl.pallas_call(
        lambda *refs: finish_kernel(*refs, scale=scale),
        in_specs=[vmem],
        out_shape=[
            jax.ShapeDtypeStruct((HD // count, width), F32),
            jax.ShapeDtypeStruct((KW, width), F32),
        ],
        compiler_params=params(),
        name="finish",
    )(recv)


def exchange(blocks, step):
    pairs = lambda k: [(d, d ^ (step * k)) for d in range(FAST * SLOW)]
    moved = [
        local_memory(lax.ppermute(block, "dp", pairs(k))) for k, block in enumerate(blocks) if k
    ]
    return [blocks[0]] + moved


def local(frames, cotangent, w_qkv, w_out, w_conv, lengths):
    seq_count = lax.axis_size("seq")
    data_count = lax.axis_size("dp")
    rows, width = frames.shape[1:]
    first = lax.axis_index("seq") * rows
    grad_scale = 1.0 / math.sqrt(data_count * rows * seq_count)
    position = lax.axis_index("dp")
    fast = position % FAST
    slow = position // FAST
    place = [fast, slow]
    scalars = jnp.stack([lengths[0], first, jnp.zeros((), jnp.int32)] + place)
    x = frames[0]
    g = cotangent[0]

    forward = [(i, i + 1) for i in range(seq_count - 1)]
    backward = [(i + 1, i) for i in range(seq_count - 1)]
    low = lax.ppermute(jnp.concatenate([x[-HALO:], g[-HALO:]], axis=0), "seq", forward)
    high = lax.ppermute(jnp.concatenate([x[:HALO], g[:HALO]], axis=0), "seq", backward)
    x_side = jnp.concatenate([low[:HALO], high[:HALO]], axis=0)
    g_side = jnp.concatenate([low[HALO:], high[HALO:]], axis=0)

    normed, send = project(x, w_qkv)
    heads = lax.all_to_all(send, "seq", 0, 0, tiled=True)
    heads_near = local_memory(heads)
    normed_all = lax.all_gather(normed, "seq", axis=0, tiled=True)
    send, out, lse = attend(scalars, heads_near)
    att = local_memory(lax.all_to_all(send, "seq", 0, 0, tiled=True))
    output, res_grad, send, pack = middle(scalars, att, x, x_side, g, g_side, w_out, w_conv)
    back = lax.all_to_all(send, "seq", 0, 0, tiled=True)
    far = [[FAST * i + j for i in range(SLOW)] for j in range(FAST)]
    packs = lax.all_gather(pack, "dp", axis=0, axis_index_groups=far, tiled=True)
    send = attend_back(scalars, heads, local_memory(back), out, lse)
    joined = lax.all_to_all(send, "seq", 0, 0, tiled=True)
    parts = exchange(gradient_parts(scalars, send, back, normed_all), 1)
    parts, packs = lax.optimization_barrier((fold_fast(scalars, parts), packs))
    parts = exchange(parts, FAST)
    outer = exchange(out_part(scalars, packs), 1)
    qkv, send = fold_slow(parts, outer, seq_count, grad_scale)
    input_grad = input_gradient(joined, w_qkv, x, res_grad)
    recv = lax.all_to_all(send, "seq", 0, 0, tiled=True)
    out_total, taps_total = finish(local_memory(recv), width, grad_scale)
    return (
        output[None],
        input_grad[None],
        qkv.reshape(width // data_count, 3, HD),
        out_total,
        taps_total,
    )


def solution(mesh):
    placed = (P("dp", "seq", None), P("dp", "seq", None), P(), P(), P(), P("dp"))
    return jax.shard_map(
        local,
        mesh=mesh,
        in_specs=placed,
        out_specs=(
            P("dp", "seq", None),
            P("dp", "seq", None),
            P("dp", None, "seq"),
            P(("dp", "seq"), None),
            P(),
        ),
        check_vma=False,
    )
```

```python
import math

import jax
import jax.numpy as jnp
from jax import lax
from jax.experimental import pallas as pl
from jax.experimental.pallas import tpu as pltpu
from jax.sharding import PartitionSpec as P

HEADS = 16
KW = 31
HD = 64
HALO = 32
QB = 256
KB = 256
F32 = jnp.float32
BF16 = jnp.bfloat16
LIMIT = 56 * 1024 * 1024
CUT = 96
FAST = 4
SLOW = 4
TAPS = FAST * CUT
LAST = CUT + KW + 1
OUT = 8 * HD


def dot(a, b, ca=1, cb=0):
    return lax.dot_general(a, b, (((ca,), (cb,)), ((), ())), preferred_element_type=F32)


def normalize(rows):
    center = rows - jnp.mean(rows, axis=-1, keepdims=True)
    scale = lax.rsqrt(jnp.mean(center * center, axis=-1, keepdims=True) + 1e-05)
    return center * scale, scale


def normalize_back(unit, scale, upstream):
    return scale * (
        upstream
        - jnp.mean(upstream, axis=-1, keepdims=True)
        - unit * jnp.mean(upstream * unit, axis=-1, keepdims=True)
    )


def params(**kw):
    return pltpu.CompilerParams(vmem_limit_bytes=LIMIT, **kw)


def cost(flops, moved, expos=0):
    return pl.CostEstimate(flops=flops, bytes_accessed=moved, transcendentals=expos)


def local_memory(array):
    return pltpu.with_memory_space_constraint(array, pltpu.VMEM)


def whole(shape):
    return pl.BlockSpec(shape, lambda *_: (0,) * len(shape))


def halves(exact):
    top = exact.astype(BF16)
    rest = (exact - top.astype(F32)).astype(BF16)
    return jnp.concatenate([top, rest], axis=1)


def joined_halves(pair):
    return pair[:, : pair.shape[1] // 2] + pair[:, pair.shape[1] // 2 :]


SMEM = pl.BlockSpec(memory_space=pltpu.SMEM)


def project_kernel(frames_ref, weight_ref, normed_ref, send_ref):
    @pl.when(pl.program_id(0) == 0)
    def _():
        unit, _ = normalize(frames_ref[...].astype(F32))
        normed_ref[...] = unit.astype(BF16)

    part = dot(normed_ref[...], weight_ref[...]).astype(BF16)
    send_ref[...] = part.T.reshape(send_ref.shape)


def project(frames, w_qkv):
    rows, width = frames.shape
    cols = 512
    per = cols // HD
    groups = HEADS // per
    return pl.pallas_call(
        project_kernel,
        grid=(3 * groups,),
        in_specs=[whole(frames.shape), pl.BlockSpec((width, cols), lambda j: (0, j))],
        out_specs=[
            whole(frames.shape),
            pl.BlockSpec((per, HD, rows), lambda j: (j % groups, j // groups, 0)),
        ],
        out_shape=[
            jax.ShapeDtypeStruct(frames.shape, BF16),
            jax.ShapeDtypeStruct((HEADS, 3 * HD, rows), BF16),
        ],
        compiler_params=params(),
        name="project",
    )(frames, w_qkv)


def load_heads(length, heads_ref, query, keys, count, rows):
    extra = lax.broadcasted_iota(jnp.int32, (HD, rows), 0)
    frame = lax.broadcasted_iota(jnp.int32, (HD, rows), 1)
    for i in range(count):
        cols = slice(i * rows, (i + 1) * rows)
        query[0:HD, cols] = (heads_ref[i, 0:HD, :].astype(F32) * 0.125).astype(BF16)
        query[HD : 2 * HD, cols] = jnp.where(extra == 0, 1.0, 0.0).astype(BF16)
        masked = jnp.logical_and(extra == 0, frame + i * rows >= length)
        mask = jnp.where(masked, -1e30, 0.0).astype(BF16)
        joined = jnp.concatenate([heads_ref[i, HD : 2 * HD, :], mask], axis=0)
        keys[cols, :] = joined.T


def attend_kernel(
    scalars, heads_ref, send_ref, out_ref, lse_ref, query, keys, value, scores
):
    count, _, rows = heads_ref.shape
    total = count * rows
    load_heads(scalars[0], heads_ref, query, keys, count, rows)
    for i in range(count):
        value[:, i * rows : (i + 1) * rows] = heads_ref[i, 2 * HD : 3 * HD, :]

    def one_block(block, carry):
        cols = pl.ds(pl.multiple_of(block * QB, QB), QB)
        query_cols = query[:, cols]
        peak = None
        for k in range(total // KB):
            part = dot(keys[k * KB : (k + 1) * KB, :], query_cols)
            scores[k * KB : (k + 1) * KB, :] = part
            top = jnp.max(part.reshape(KB // 8, 8, QB), axis=0)
            peak = top if peak is None else jnp.maximum(peak, top)
        peak = jnp.max(peak, axis=0, keepdims=True)
        total_row = jnp.zeros((8, QB), F32)
        acc = jnp.zeros((HD, QB), F32)
        for k in range(total // KB):
            expo = jnp.exp(scores[k * KB : (k + 1) * KB, :] - peak)
            total_row = total_row + jnp.sum(expo.reshape(KB // 8, 8, QB), axis=0)
            acc = acc + dot(value[:, k * KB : (k + 1) * KB], expo.astype(BF16))
        total_row = jnp.sum(total_row, axis=0, keepdims=True)
        out_ref[:, cols] = acc / total_row
        lse_ref[:, cols] = peak + jnp.log(total_row)
        return carry

    lax.fori_loop(0, total // QB, one_block, 0)
    none = jnp.zeros((HD, HALO), F32)
    for i in range(count):
        send_ref[i, 0:HD, :] = out_ref[:, i * rows : (i + 1) * rows].astype(BF16)
        low = out_ref[:, i * rows - HALO : i * rows] if i else none
        high = out_ref[:, (i + 1) * rows : (i + 1) * rows + HALO] if i < count - 1 else none
        sides = jnp.concatenate([low, high], axis=1)
        packed = jnp.concatenate([sides[0 : HD // 2], sides[HD // 2 :]], axis=1)
        send_ref[i, HD : HD + HD // 2, :] = packed.astype(BF16)


def attend(scalars, heads):
    count, _, rows = heads.shape
    total = count * rows
    return pl.pallas_call(
        attend_kernel,
        in_specs=[SMEM, pl.BlockSpec(memory_space=pltpu.VMEM)],
        out_shape=[
            jax.ShapeDtypeStruct((count, HD + HD // 2, rows), BF16),
            jax.ShapeDtypeStruct((HD, total), F32),
            jax.ShapeDtypeStruct((1, total), F32),
        ],
        scratch_shapes=[
            pltpu.VMEM((2 * HD, total), BF16),
            pltpu.VMEM((total, 2 * HD), BF16),
            pltpu.VMEM((HD, total), BF16),
            pltpu.VMEM((total, QB), F32),
        ],
        compiler_params=params(),
        cost_estimate=cost(2 * 2 * total * total * 256, heads.size * 2, total * total),
        name="attend",
    )(scalars, heads)


def middle_kernel(
    scalars,
    att_ref,
    frames_ref,
    frames_side,
    grads_ref,
    grads_side,
    w_out_ref,
    w_conv_ref,
    output_ref,
    res_grad_ref,
    send_ref,
    pack_ref,
    taps_ref,
    conv_in,
    grad_all,
    residual,
    window,
    window_back,
    conv_grad,
):
    rows, width = frames_ref.shape
    heads = att_ref.shape[0]
    length = scalars[0]
    first = scalars[1]
    zero = scalars[2]
    half = HD // 2
    body = slice(HALO, HALO + rows)

    attended = att_ref[:, 0:HD, :].reshape(width, rows).T
    main = frames_ref[...].astype(F32) + dot(attended, w_out_ref[...])
    packed = att_ref[:, HD : HD + half, :].reshape(heads * half, rows).T
    split_w = w_out_ref[...].reshape(heads, 2, half, width)
    side = dot(packed[0 : 2 * HALO], split_w[:, 0].reshape(heads * half, width))
    side = side + dot(packed[2 * HALO :], split_w[:, 1].reshape(heads * half, width))
    side = frames_side[...].astype(F32) + side

    def keep_of(count, start):
        frame = lax.broadcasted_iota(jnp.int32, (count, 1), 0) + start
        return jnp.where(jnp.logical_and(frame >= 0, frame < length), 1.0, 0.0)

    main = main.astype(BF16).astype(F32)
    residual[...] = main
    unit, scale = normalize(main)
    keep = keep_of(rows, first)
    conv_in[body, :] = (unit * keep).astype(BF16).astype(F32)
    unit_side, _ = normalize(side.astype(BF16).astype(F32))
    low = unit_side[0:HALO] * keep_of(HALO, first - HALO)
    high = unit_side[HALO:] * keep_of(HALO, first + rows)
    conv_in[0:HALO, :] = low.astype(BF16).astype(F32)
    conv_in[HALO + rows :, :] = high.astype(BF16).astype(F32)
    grad_all[0:HALO, :] = grads_side[0:HALO, :].astype(F32)
    grad_all[body, :] = grads_ref[...].astype(F32)
    grad_all[HALO + rows :, :] = grads_side[HALO:, :].astype(F32)

    reach = rows + HALO
    edge = HALO // 2

    def one_chunk(chunk, carry):
        lanes = pl.ds(pl.multiple_of(chunk * 128, 128), 128)
        window[...] = conv_in[:, lanes]
        acc = jnp.zeros((reach, 128), F32)
        for j in range(KW):
            acc = acc + w_conv_ref[j : j + 1, lanes] * window[pl.ds(zero + (1 + j), reach), :]
        gate = jax.nn.sigmoid(acc)
        back = grad_all[edge : edge + reach, lanes] * (gate + acc * gate * (1.0 - gate))
        window_back[...] = back
        gated = acc[edge : edge + rows] * gate[edge : edge + rows]
        output_ref[:, lanes] = (residual[:, lanes] + gated).astype(BF16)
        own = window_back[edge : edge + rows, :]
        acc = jnp.zeros((rows, 128), F32)
        for j in range(KW):
            acc = acc + w_conv_ref[j : j + 1, lanes] * window_back[
                pl.ds(zero + (KW - j), rows), :
            ]
            moved = window[pl.ds(zero + (edge + 1 + j), rows), :]
            taps_ref[j : j + 1, lanes] = jnp.sum(moved * own, axis=0, keepdims=True)
        taps_ref[KW : KW + 1, lanes] = jnp.zeros((1, 128), F32)
        conv_grad[:, lanes] = acc
        return carry

    lax.fori_loop(0, width // 128, one_chunk, 0)
    res_grad = grads_ref[...].astype(F32) + normalize_back(unit, scale, conv_grad[...] * keep)
    res_grad_ref[...] = res_grad
    rounded = res_grad.astype(BF16)
    pack_ref[:, 0:width] = rounded
    pack_ref[:, width:] = attended
    back = dot(w_out_ref[...], rounded, 1, 1).astype(BF16)
    send_ref[:, 0:HD, :] = back.reshape(heads, HD, rows)
    for h in range(heads):
        own = taps_ref[:, h * HD : (h + 1) * HD]
        middle_row = (KW + 1) // 2
        own = jnp.concatenate([own[0:middle_row], own[middle_row:]], axis=1)
        send_ref[h, HD:, :] = own.astype(BF16)


def middle(scalars, att, frames, frames_side, grads, grads_side, w_out, w_conv):
    rows, width = frames.shape
    vmem = pl.BlockSpec(memory_space=pltpu.VMEM)
    return pl.pallas_call(
        middle_kernel,
        in_specs=[SMEM] + [vmem] * 7,
        out_shape=[
            jax.ShapeDtypeStruct((rows, width), BF16),
            jax.ShapeDtypeStruct((rows, width), F32),
            jax.ShapeDtypeStruct((HEADS, HD + (KW + 1) // 2, rows), BF16),
            jax.ShapeDtypeStruct((rows, 2 * width), BF16),
        ],
        scratch_shapes=[
            pltpu.VMEM((KW + 1, width), F32),
            pltpu.VMEM((rows + 2 * HALO, width), F32),
            pltpu.VMEM((rows + 2 * HALO, width), F32),
            pltpu.VMEM((rows, width), F32),
            pltpu.VMEM((rows + 2 * HALO, 128), F32),
            pltpu.VMEM((rows + HALO, 128), F32),
            pltpu.VMEM((rows, width), F32),
        ],
        compiler_params=params(),
        name="middle",
    )(scalars, att, frames, frames_side, grads, grads_side, w_out, w_conv)


def attend_back_kernel(
    scalars, heads_ref, grads_ref, out_ref, lse_ref, send_ref,
    query, keys, value_t, grad_t, query_rows, grad_rows, query_grad, probs, score_grads,
):
    count, _, rows = heads_ref.shape
    total = count * rows
    load_heads(scalars[0], heads_ref, query, keys, count, rows)
    for i in range(count):
        cols = slice(i * rows, (i + 1) * rows)
        block = grads_ref[i, 0:HD, :]
        grad_t[:, cols] = block
        both = jnp.concatenate([query[0:HD, cols], block], axis=0).T
        query_rows[cols, :] = both[:, 0:HD]
        grad_rows[cols, :] = both[:, HD:]
        value_t[cols, :] = heads_ref[i, 2 * HD : 3 * HD, :].T
    query_grad[...] = jnp.zeros_like(query_grad)
    lse = lse_ref[...]
    delta = jnp.sum(grad_t[...].astype(F32) * out_ref[...], axis=0, keepdims=True)

    def one_block(block, carry):
        span = pl.ds(pl.multiple_of(block * KB, KB), KB)
        key_rows = keys[span, :]
        value_rows = value_t[span, :]
        for q in range(total // QB):
            cols = slice(q * QB, (q + 1) * QB)
            prob = jnp.exp(dot(key_rows, query[:, cols]) - lse[:, cols])
            prob_grad = dot(value_rows, grad_t[:, cols])
            probs[:, cols] = prob.astype(BF16)
            score_grads[:, cols] = (prob * (prob_grad - delta[:, cols])).astype(BF16)
        key_grad = dot(score_grads[...], query_rows[...])
        value_grad = dot(probs[...], grad_rows[...])
        key_cols = key_rows[:, 0:HD].T
        query_grad[...] += dot(key_cols, score_grads[...])
        joined = jnp.concatenate([key_grad, value_grad], axis=1).T.astype(BF16)
        for i in range(KB // rows):
            send_ref[block * (KB // rows) + i, HD : 3 * HD, :] = joined[:, i * rows : (i + 1) * rows]
        return carry

    lax.fori_loop(0, total // KB, one_block, 0)
    for i in range(count):
        cols = slice(i * rows, (i + 1) * rows)
        send_ref[i, 0:HD, :] = (query_grad[:, cols] * 0.125).astype(BF16)


def attend_back(scalars, heads, grads, out, lse):
    count, _, rows = heads.shape
    total = count * rows
    vmem = pl.BlockSpec(memory_space=pltpu.VMEM)
    return pl.pallas_call(
        attend_back_kernel,
        in_specs=[SMEM] + [vmem] * 4,
        out_shape=jax.ShapeDtypeStruct(heads.shape, BF16),
        scratch_shapes=[
            pltpu.VMEM((2 * HD, total), BF16),
            pltpu.VMEM((total, 2 * HD), BF16),
            pltpu.VMEM((total, HD), BF16),
            pltpu.VMEM((HD, total), BF16),
            pltpu.VMEM((total, HD), BF16),
            pltpu.VMEM((total, HD), BF16),
            pltpu.VMEM((HD, total), F32),
            pltpu.VMEM((KB, total), BF16),
            pltpu.VMEM((KB, total), BF16),
        ],
        compiler_params=params(),
        cost_estimate=cost(5 * 2 * total * total * 256, heads.size * 4, total * total),
        name="attend_back",
    )(scalars, heads, grads, out, lse)


def input_grad_kernel(joined_ref, weight_ref, frames_ref, res_grad_ref, out_ref, joined, grads):
    step = pl.program_id(0)
    heads = joined_ref.shape[0]

    @pl.when(step == 0)
    def _():
        for h in range(heads):
            for t in range(3):
                row = (t * heads + h) * HD
                joined[row : row + HD, :] = joined_ref[h, t * HD : (t + 1) * HD, :]

    block = weight_ref.shape[0]
    start = pl.multiple_of(step * block, block)
    grads[pl.ds(start, block), :] = dot(weight_ref[...], joined[...])

    @pl.when(step == pl.num_programs(0) - 1)
    def _():
        unit, scale = normalize(frames_ref[...].astype(F32))
        back = normalize_back(unit, scale, grads[...].T)
        out_ref[...] = (res_grad_ref[...] + back).astype(BF16)


def input_gradient(joined, w_qkv, frames, res_grad):
    rows, width = frames.shape
    block = 256
    return pl.pallas_call(
        input_grad_kernel,
        grid=(width // block,),
        in_specs=[
            pl.BlockSpec(memory_space=pltpu.VMEM),
            pl.BlockSpec((block, w_qkv.shape[1]), lambda j: (j, 0)),
            whole(frames.shape),
            whole(frames.shape),
        ],
        out_specs=whole(frames.shape),
        out_shape=jax.ShapeDtypeStruct(frames.shape, BF16),
        scratch_shapes=[
            pltpu.VMEM((w_qkv.shape[1], rows), BF16),
            pltpu.VMEM((width, rows), F32),
        ],
        compiler_params=params(),
        name="input_gradient",
    )(local_memory(joined), w_qkv, frames, res_grad)


def parts_kernel(scalars, grads_ref, back_ref, normed_ref, *rest):
    send_refs, columns = rest[:SLOW], rest[SLOW]
    count, wide, rows = grads_ref.shape

    @pl.when(pl.program_id(0) == 0)
    def _():
        taps = jnp.zeros(((KW + 1) // 2, rows), F32)
        for i in range(count):
            columns[:, i * rows : (i + 1) * rows] = grads_ref[i]
            taps = taps + back_ref[i, HD:, :].astype(F32)
        pair = halves(jnp.concatenate([taps[:, 0:HD], taps[:, HD:]], axis=0))
        for send_ref in send_refs:
            send_ref[TAPS:, :] = pair

    part = dot(columns[...], normed_ref[...])
    each = part.shape[1] // FAST
    pieces = []
    for i in range(FAST):
        piece = part[:, i * each : (i + 1) * each]
        pieces.append(jnp.concatenate([piece[0:CUT], piece[CUT:]], axis=1).astype(BF16))
    for k, send_ref in enumerate(send_refs):

        @pl.when(pl.program_id(0) == k)
        def _():
            for i, piece in enumerate(pieces):
                send_ref[i * CUT : (i + 1) * CUT, :] = piece


def gradient_parts(scalars, grads, back, normed_all):
    count, wide, rows = grads.shape
    total, width = normed_all.shape
    return pl.pallas_call(
        parts_kernel,
        grid_spec=pltpu.PrefetchScalarGridSpec(
            num_scalar_prefetch=1,
            grid=(SLOW,),
            in_specs=[
                pl.BlockSpec(grads.shape, lambda j, place: (0, 0, 0)),
                pl.BlockSpec(back.shape, lambda j, place: (0, 0, 0)),
                pl.BlockSpec((total, width // SLOW), lambda j, place: (0, place[4] ^ j)),
            ],
            out_specs=[pl.BlockSpec((TAPS + KW + 1, 128), lambda j, place: (0, 0))] * SLOW,
            scratch_shapes=[pltpu.VMEM((wide, total), BF16)],
        ),
        out_shape=[jax.ShapeDtypeStruct((TAPS + KW + 1, 128), BF16)] * SLOW,
        compiler_params=params(),
        name="gradient_parts",
    )(scalars, grads, back, normed_all)


def sum_four(own, one, two, three):
    return (own.astype(F32) + one.astype(F32)) + (two.astype(F32) + three.astype(F32))


def fold_first_kernel(scalars, one, two, three, four, pack_ref, *rest):
    send_refs, pieces, outer = rest[:FAST], *rest[FAST:]
    width = pack_ref.shape[1] // 2
    block = FAST * HD
    first = pl.multiple_of(width + scalars[4] * block, block)
    outer[...] = dot(pack_ref[:, pl.ds(first, block)].T, pack_ref[:, 0:width])
    total = sum_four(one[...], two[...], three[...], four[...])
    pair = halves(joined_halves(total[TAPS:]))
    for i in range(FAST):
        pieces[i] = total[i * CUT : (i + 1) * CUT].astype(BF16)
    for k, send_ref in enumerate(send_refs):
        send_ref[0:CUT, :] = pieces[scalars[3] ^ k]
        send_ref[CUT:LAST, :] = pair
        own = pl.ds(pl.multiple_of((scalars[3] ^ k) * HD, HD), HD)
        for c in range(width // 128):
            at = LAST + c * HD
            send_ref[at : at + HD, :] = outer[own, c * 128 : (c + 1) * 128].astype(BF16)


def fold_first(scalars, blocks, packs):
    vmem = pl.BlockSpec(memory_space=pltpu.VMEM)
    return pl.pallas_call(
        fold_first_kernel,
        in_specs=[SMEM] + [vmem] * 5,
        out_shape=[jax.ShapeDtypeStruct((LAST + OUT, 128), BF16)] * FAST,
        scratch_shapes=[
            pltpu.VMEM((FAST, CUT, 128), BF16),
            pltpu.VMEM((FAST * HD, packs.shape[1] // 2), F32),
        ],
        compiler_params=params(),
        name="fold_first",
    )(scalars, *blocks, packs)


def fold_last_kernel(*refs, scale):
    qkv_ref, send_ref = refs[4:]
    total = sum_four(*(ref[...] for ref in refs[0:4]))
    model_rows = (total[0:CUT] * scale).T
    qkv_ref[:, 0:CUT] = model_rows[0:HD]
    qkv_ref[:, CUT:] = model_rows[HD:]
    pair = halves(joined_halves(total[CUT:LAST]))
    outer = total[LAST:]
    count = send_ref.shape[0]
    each = HD // count
    for i in range(count):
        pieces = [outer[c * HD + i * each : c * HD + (i + 1) * each] for c in range(OUT // HD)]
        send_ref[i, 0 : OUT // count, :] = jnp.concatenate(pieces, axis=0).astype(BF16)
        send_ref[i, OUT // count :, :] = pair


def fold_last(blocks, seq_count, scale):
    vmem = pl.BlockSpec(memory_space=pltpu.VMEM)
    return pl.pallas_call(
        lambda *refs: fold_last_kernel(*refs, scale=scale),
        in_specs=[vmem] * 4,
        out_shape=[
            jax.ShapeDtypeStruct((HD, 3 * HD), F32),
            jax.ShapeDtypeStruct((seq_count, OUT // seq_count + KW + 1, 128), BF16),
        ],
        compiler_params=params(),
        name="fold_last",
    )(*blocks)


def finish_kernel(recv_ref, out_ref, taps_ref, *, scale):
    count = recv_ref.shape[0]
    each = out_ref.shape[0]
    wide = OUT // count
    total = recv_ref[0, 0:wide, :].astype(F32)
    for i in range(1, count):
        total = total + recv_ref[i, 0:wide, :].astype(F32)
    total = total * scale
    for c in range(OUT // HD):
        out_ref[:, c * 128 : (c + 1) * 128] = total[c * each : (c + 1) * each]
    for i in range(count // 2):
        both = [joined_halves(recv_ref[2 * i + k, wide:, :].astype(F32)) for k in range(2)]
        both = jnp.concatenate(both, axis=1) * scale
        taps_ref[:, i * 2 * HD : (i + 1) * 2 * HD] = both[0:KW]


def finish(recv, width, scale):
    count = recv.shape[0]
    vmem = pl.BlockSpec(memory_space=pltpu.VMEM)
    return pl.pallas_call(
        lambda *refs: finish_kernel(*refs, scale=scale),
        in_specs=[vmem],
        out_shape=[
            jax.ShapeDtypeStruct((HD // count, width), F32),
            jax.ShapeDtypeStruct((KW, width), F32),
        ],
        compiler_params=params(),
        name="finish",
    )(recv)


def exchange(blocks, step):
    pairs = lambda k: [(d, d ^ (step * k)) for d in range(FAST * SLOW)]
    moved = [
        local_memory(lax.ppermute(block, "dp", pairs(k))) for k, block in enumerate(blocks) if k
    ]
    return [blocks[0]] + moved


def local(frames, cotangent, w_qkv, w_out, w_conv, lengths):
    seq_count = lax.axis_size("seq")
    data_count = lax.axis_size("dp")
    rows, width = frames.shape[1:]
    first = lax.axis_index("seq") * rows
    grad_scale = 1.0 / math.sqrt(data_count * rows * seq_count)
    position = lax.axis_index("dp")
    fast = position % FAST
    slow = position // FAST
    place = [fast, slow]
    scalars = jnp.stack([lengths[0], first, jnp.zeros((), jnp.int32)] + place)
    x = frames[0]
    g = cotangent[0]

    forward = [(i, i + 1) for i in range(seq_count - 1)]
    backward = [(i + 1, i) for i in range(seq_count - 1)]
    low = lax.ppermute(jnp.concatenate([x[-HALO:], g[-HALO:]], axis=0), "seq", forward)
    high = lax.ppermute(jnp.concatenate([x[:HALO], g[:HALO]], axis=0), "seq", backward)
    x_side = jnp.concatenate([low[:HALO], high[:HALO]], axis=0)
    g_side = jnp.concatenate([low[HALO:], high[HALO:]], axis=0)

    normed, send = project(x, w_qkv)
    heads = lax.all_to_all(send, "seq", 0, 0, tiled=True)
    heads_near = local_memory(heads)
    normed_all = lax.all_gather(normed, "seq", axis=0, tiled=True)
    send, out, lse = attend(scalars, heads_near)
    att = local_memory(lax.all_to_all(send, "seq", 0, 0, tiled=True))
    output, res_grad, send, pack = middle(scalars, att, x, x_side, g, g_side, w_out, w_conv)
    back = lax.all_to_all(send, "seq", 0, 0, tiled=True)
    far = [[FAST * i + j for i in range(SLOW)] for j in range(FAST)]
    packs = lax.all_gather(pack, "dp", axis=0, axis_index_groups=far, tiled=True)
    send = attend_back(scalars, heads, local_memory(back), out, lse)
    joined = lax.all_to_all(send, "seq", 0, 0, tiled=True)
    parts = exchange(gradient_parts(scalars, send, back, normed_all), FAST)
    parts = exchange(fold_first(scalars, parts, packs), 1)
    qkv, send = fold_last(parts, seq_count, grad_scale)
    input_grad = input_gradient(joined, w_qkv, x, res_grad)
    recv = lax.all_to_all(send, "seq", 0, 0, tiled=True)
    out_total, taps_total = finish(local_memory(recv), width, grad_scale)
    return (
        output[None],
        input_grad[None],
        qkv.reshape(width // data_count, 3, HD),
        out_total,
        taps_total,
    )


def solution(mesh):
    placed = (P("dp", "seq", None), P("dp", "seq", None), P(), P(), P(), P("dp"))
    return jax.shard_map(
        local,
        mesh=mesh,
        in_specs=placed,
        out_specs=(
            P("dp", "seq", None),
            P("dp", "seq", None),
            P("dp", None, "seq"),
            P(("dp", "seq"), None),
            P(),
        ),
        check_vma=False,
    )
```

```python
import math

import jax
import jax.numpy as jnp
from jax import lax
from jax.experimental import pallas as pl
from jax.experimental.pallas import tpu as pltpu
from jax.sharding import PartitionSpec as P

HEADS = 16
KW = 31
HD = 64
HALO = 32
QUERIES = 512
KEYS = 256
QB = 256
KB = 512
F32 = jnp.float32
BF16 = jnp.bfloat16
LIMIT = 56 * 1024 * 1024
CUT = 96
FAST = 4
SLOW = 4
TAPS = FAST * CUT
LAST = CUT + KW + 1
OUT = 8 * HD


def dot(a, b, ca=1, cb=0):
    return lax.dot_general(a, b, (((ca,), (cb,)), ((), ())), preferred_element_type=F32)


def normalize(rows):
    center = rows - jnp.mean(rows, axis=-1, keepdims=True)
    scale = lax.rsqrt(jnp.mean(center * center, axis=-1, keepdims=True) + 1e-05)
    return center * scale, scale


def normalize_back(unit, scale, upstream):
    return scale * (
        upstream
        - jnp.mean(upstream, axis=-1, keepdims=True)
        - unit * jnp.mean(upstream * unit, axis=-1, keepdims=True)
    )


def params(**kw):
    return pltpu.CompilerParams(vmem_limit_bytes=LIMIT, **kw)


def cost(flops, moved, expos=0):
    return pl.CostEstimate(flops=flops, bytes_accessed=moved, transcendentals=expos)


def local_memory(array):
    return pltpu.with_memory_space_constraint(array, pltpu.VMEM)


def whole(shape):
    return pl.BlockSpec(shape, lambda *_: (0,) * len(shape))


def halves(exact):
    top = exact.astype(BF16)
    rest = (exact - top.astype(F32)).astype(BF16)
    return jnp.concatenate([top, rest], axis=1)


def joined_halves(pair):
    return pair[:, : pair.shape[1] // 2] + pair[:, pair.shape[1] // 2 :]


SMEM = pl.BlockSpec(memory_space=pltpu.SMEM)


def project_kernel(frames_ref, weight_ref, normed_ref, send_ref):
    @pl.when(pl.program_id(0) == 0)
    def _():
        unit, _ = normalize(frames_ref[...].astype(F32))
        normed_ref[...] = unit.astype(BF16)

    part = dot(normed_ref[...], weight_ref[...]).astype(BF16)
    send_ref[...] = part.T.reshape(send_ref.shape)


def project(frames, w_qkv):
    rows, width = frames.shape
    cols = 1024
    per = cols // HD
    groups = HEADS // per
    return pl.pallas_call(
        project_kernel,
        grid=(3 * groups,),
        in_specs=[whole(frames.shape), pl.BlockSpec((width, cols), lambda j: (0, j))],
        out_specs=[
            whole(frames.shape),
            pl.BlockSpec((per, HD, rows), lambda j: (j % groups, j // groups, 0)),
        ],
        out_shape=[
            jax.ShapeDtypeStruct(frames.shape, BF16),
            jax.ShapeDtypeStruct((HEADS, 3 * HD, rows), BF16),
        ],
        compiler_params=params(),
        name="project",
    )(frames, w_qkv)


def load_heads(length, heads_ref, query, keys, count, rows):
    extra = lax.broadcasted_iota(jnp.int32, (HD, rows), 0)
    frame = lax.broadcasted_iota(jnp.int32, (HD, rows), 1)
    for i in range(count):
        cols = slice(i * rows, (i + 1) * rows)
        query[0:HD, cols] = (heads_ref[i, 0:HD, :].astype(F32) * 0.125).astype(BF16)
        query[HD : 2 * HD, cols] = jnp.where(extra == 0, 1.0, 0.0).astype(BF16)
        masked = jnp.logical_and(extra == 0, frame + i * rows >= length)
        mask = jnp.where(masked, -1e30, 0.0).astype(BF16)
        joined = jnp.concatenate([heads_ref[i, HD : 2 * HD, :], mask], axis=0)
        keys[cols, :] = joined.T


def attend_kernel(
    scalars, heads_ref, send_ref, out_ref, lse_ref, query, keys, value, scores
):
    count, _, rows = heads_ref.shape
    total = count * rows
    load_heads(scalars[0], heads_ref, query, keys, count, rows)
    for i in range(count):
        value[:, i * rows : (i + 1) * rows] = heads_ref[i, 2 * HD : 3 * HD, :]

    def one_block(block, carry):
        cols = pl.ds(pl.multiple_of(block * QUERIES, QUERIES), QUERIES)
        query_cols = query[:, cols]
        peak = None
        for k in range(total // KEYS):
            part = dot(keys[k * KEYS : (k + 1) * KEYS, :], query_cols)
            scores[k * KEYS : (k + 1) * KEYS, :] = part
            top = jnp.max(part.reshape(KEYS // 8, 8, QUERIES), axis=0)
            peak = top if peak is None else jnp.maximum(peak, top)
        peak = jnp.max(peak, axis=0, keepdims=True)
        total_row = jnp.zeros((8, QUERIES), F32)
        acc = jnp.zeros((HD, QUERIES), F32)
        for k in range(total // KEYS):
            expo = jnp.exp(scores[k * KEYS : (k + 1) * KEYS, :] - peak)
            total_row = total_row + jnp.sum(expo.reshape(KEYS // 8, 8, QUERIES), axis=0)
            acc = acc + dot(value[:, k * KEYS : (k + 1) * KEYS], expo.astype(BF16))
        total_row = jnp.sum(total_row, axis=0, keepdims=True)
        out_ref[:, cols] = acc / total_row
        lse_ref[:, cols] = peak + jnp.log(total_row)
        return carry

    lax.fori_loop(0, total // QUERIES, one_block, 0, unroll=True)
    none = jnp.zeros((HD, HALO), F32)
    for i in range(count):
        send_ref[i, 0:HD, :] = out_ref[:, i * rows : (i + 1) * rows].astype(BF16)
        low = out_ref[:, i * rows - HALO : i * rows] if i else none
        high = out_ref[:, (i + 1) * rows : (i + 1) * rows + HALO] if i < count - 1 else none
        sides = jnp.concatenate([low, high], axis=1)
        packed = jnp.concatenate([sides[0 : HD // 2], sides[HD // 2 :]], axis=1)
        send_ref[i, HD : HD + HD // 2, :] = packed.astype(BF16)


def attend(scalars, heads):
    count, _, rows = heads.shape
    total = count * rows
    return pl.pallas_call(
        attend_kernel,
        in_specs=[SMEM, pl.BlockSpec(memory_space=pltpu.VMEM)],
        out_shape=[
            jax.ShapeDtypeStruct((count, HD + HD // 2, rows), BF16),
            jax.ShapeDtypeStruct((HD, total), F32),
            jax.ShapeDtypeStruct((1, total), F32),
        ],
        scratch_shapes=[
            pltpu.VMEM((2 * HD, total), BF16),
            pltpu.VMEM((total, 2 * HD), BF16),
            pltpu.VMEM((HD, total), BF16),
            pltpu.VMEM((total, QUERIES), F32),
        ],
        compiler_params=params(),
        cost_estimate=cost(2 * 2 * total * total * 256, heads.size * 2, total * total),
        name="attend",
    )(scalars, heads)


def middle_kernel(
    scalars,
    att_ref,
    frames_ref,
    frames_side,
    grads_ref,
    grads_side,
    w_out_ref,
    w_conv_ref,
    output_ref,
    res_grad_ref,
    send_ref,
    round_ref,
    pick_one,
    pick_two,
    pick_three,
    pick_four,
    taps_ref,
    conv_in,
    grad_all,
    residual,
    window,
    window_back,
    conv_grad,
):
    rows, width = frames_ref.shape
    heads = att_ref.shape[0]
    length = scalars[0]
    first = scalars[1]
    zero = scalars[2]
    half = HD // 2
    body = slice(HALO, HALO + rows)

    attended = att_ref[:, 0:HD, :].reshape(width, rows).T
    main = frames_ref[...].astype(F32) + dot(attended, w_out_ref[...])
    packed = att_ref[:, HD : HD + half, :].reshape(heads * half, rows).T
    split_w = w_out_ref[...].reshape(heads, 2, half, width)
    side = dot(packed[0 : 2 * HALO], split_w[:, 0].reshape(heads * half, width))
    side = side + dot(packed[2 * HALO :], split_w[:, 1].reshape(heads * half, width))
    side = frames_side[...].astype(F32) + side

    def keep_of(count, start):
        frame = lax.broadcasted_iota(jnp.int32, (count, 1), 0) + start
        return jnp.where(jnp.logical_and(frame >= 0, frame < length), 1.0, 0.0)

    main = main.astype(BF16).astype(F32)
    residual[...] = main
    unit, scale = normalize(main)
    keep = keep_of(rows, first)
    conv_in[body, :] = (unit * keep).astype(BF16).astype(F32)
    unit_side, _ = normalize(side.astype(BF16).astype(F32))
    low = unit_side[0:HALO] * keep_of(HALO, first - HALO)
    high = unit_side[HALO:] * keep_of(HALO, first + rows)
    conv_in[0:HALO, :] = low.astype(BF16).astype(F32)
    conv_in[HALO + rows :, :] = high.astype(BF16).astype(F32)
    grad_all[0:HALO, :] = grads_side[0:HALO, :].astype(F32)
    grad_all[body, :] = grads_ref[...].astype(F32)
    grad_all[HALO + rows :, :] = grads_side[HALO:, :].astype(F32)

    reach = rows + HALO
    edge = HALO // 2

    def one_chunk(chunk, carry):
        lanes = pl.ds(pl.multiple_of(chunk * 128, 128), 128)
        window[...] = conv_in[:, lanes]
        acc = jnp.zeros((reach, 128), F32)
        for j in range(KW):
            acc = acc + w_conv_ref[j : j + 1, lanes] * window[pl.ds(zero + (1 + j), reach), :]
        gate = jax.nn.sigmoid(acc)
        back = grad_all[edge : edge + reach, lanes] * (gate + acc * gate * (1.0 - gate))
        window_back[...] = back
        gated = acc[edge : edge + rows] * gate[edge : edge + rows]
        output_ref[:, lanes] = (residual[:, lanes] + gated).astype(BF16)
        own = window_back[edge : edge + rows, :]
        acc = jnp.zeros((rows, 128), F32)
        for j in range(KW):
            acc = acc + w_conv_ref[j : j + 1, lanes] * window_back[
                pl.ds(zero + (KW - j), rows), :
            ]
            moved = window[pl.ds(zero + (edge + 1 + j), rows), :]
            taps_ref[j : j + 1, lanes] = jnp.sum(moved * own, axis=0, keepdims=True)
        taps_ref[KW : KW + 1, lanes] = jnp.zeros((1, 128), F32)
        conv_grad[:, lanes] = acc
        return carry

    lax.fori_loop(0, width // 128, one_chunk, 0)
    res_grad = grads_ref[...].astype(F32) + normalize_back(unit, scale, conv_grad[...] * keep)
    res_grad_ref[...] = res_grad
    rounded = res_grad.astype(BF16)
    round_ref[...] = rounded
    for k, pick_ref in enumerate((pick_one, pick_two, pick_three, pick_four)):
        first_head = pl.multiple_of((scalars[4] ^ k) * FAST, FAST)
        pick_ref[...] = att_ref[pl.ds(first_head, FAST), 0:HD, :].reshape(FAST * HD, rows)
    back = dot(w_out_ref[...], rounded, 1, 1).astype(BF16)
    send_ref[:, 0:HD, :] = back.reshape(heads, HD, rows)
    for h in range(heads):
        own = taps_ref[:, h * HD : (h + 1) * HD]
        middle_row = (KW + 1) // 2
        own = jnp.concatenate([own[0:middle_row], own[middle_row:]], axis=1)
        send_ref[h, HD:, :] = own.astype(BF16)


def middle(scalars, att, frames, frames_side, grads, grads_side, w_out, w_conv):
    rows, width = frames.shape
    vmem = pl.BlockSpec(memory_space=pltpu.VMEM)
    return pl.pallas_call(
        middle_kernel,
        in_specs=[SMEM] + [vmem] * 7,
        out_shape=[
            jax.ShapeDtypeStruct((rows, width), BF16),
            jax.ShapeDtypeStruct((rows, width), F32),
            jax.ShapeDtypeStruct((HEADS, HD + (KW + 1) // 2, rows), BF16),
            jax.ShapeDtypeStruct((rows, width), BF16),
        ]
        + [jax.ShapeDtypeStruct((FAST * HD, rows), BF16)] * SLOW,
        scratch_shapes=[
            pltpu.VMEM((KW + 1, width), F32),
            pltpu.VMEM((rows + 2 * HALO, width), F32),
            pltpu.VMEM((rows + 2 * HALO, width), F32),
            pltpu.VMEM((rows, width), F32),
            pltpu.VMEM((rows + 2 * HALO, 128), F32),
            pltpu.VMEM((rows + HALO, 128), F32),
            pltpu.VMEM((rows, width), F32),
        ],
        compiler_params=params(),
        name="middle",
    )(scalars, att, frames, frames_side, grads, grads_side, w_out, w_conv)


def attend_back_kernel(
    scalars, heads_ref, grads_ref, out_ref, lse_ref, send_ref,
    query, keys, value_t, grad_t, query_rows, grad_rows, query_grad, probs, score_grads,
):
    count, _, rows = heads_ref.shape
    total = count * rows
    load_heads(scalars[0], heads_ref, query, keys, count, rows)
    for i in range(count):
        cols = slice(i * rows, (i + 1) * rows)
        block = grads_ref[i, 0:HD, :]
        grad_t[:, cols] = block
        both = jnp.concatenate([query[0:HD, cols], block], axis=0).T
        query_rows[cols, :] = both[:, 0:HD]
        grad_rows[cols, :] = both[:, HD:]
        value_t[cols, :] = heads_ref[i, 2 * HD : 3 * HD, :].T
    query_grad[...] = jnp.zeros_like(query_grad)
    lse = lse_ref[...]
    delta = jnp.sum(grad_t[...].astype(F32) * out_ref[...], axis=0, keepdims=True)

    def one_block(block, carry):
        span = pl.ds(pl.multiple_of(block * KB, KB), KB)
        key_rows = keys[span, :]
        value_rows = value_t[span, :]
        for q in range(total // QB):
            cols = slice(q * QB, (q + 1) * QB)
            prob = jnp.exp(dot(key_rows, query[:, cols]) - lse[:, cols])
            prob_grad = dot(value_rows, grad_t[:, cols])
            probs[:, cols] = prob.astype(BF16)
            score_grads[:, cols] = (prob * (prob_grad - delta[:, cols])).astype(BF16)
        key_grad = dot(score_grads[...], query_rows[...])
        value_grad = dot(probs[...], grad_rows[...])
        key_cols = key_rows[:, 0:HD].T
        query_grad[...] += dot(key_cols, score_grads[...])
        joined = jnp.concatenate([key_grad, value_grad], axis=1).T.astype(BF16)
        for i in range(KB // rows):
            send_ref[block * (KB // rows) + i, HD : 3 * HD, :] = joined[:, i * rows : (i + 1) * rows]
        return carry

    lax.fori_loop(0, total // KB, one_block, 0, unroll=True)
    for i in range(count):
        cols = slice(i * rows, (i + 1) * rows)
        send_ref[i, 0:HD, :] = (query_grad[:, cols] * 0.125).astype(BF16)


def attend_back(scalars, heads, grads, out, lse):
    count, _, rows = heads.shape
    total = count * rows
    vmem = pl.BlockSpec(memory_space=pltpu.VMEM)
    return pl.pallas_call(
        attend_back_kernel,
        in_specs=[SMEM] + [vmem] * 4,
        out_shape=jax.ShapeDtypeStruct(heads.shape, BF16),
        scratch_shapes=[
            pltpu.VMEM((2 * HD, total), BF16),
            pltpu.VMEM((total, 2 * HD), BF16),
            pltpu.VMEM((total, HD), BF16),
            pltpu.VMEM((HD, total), BF16),
            pltpu.VMEM((total, HD), BF16),
            pltpu.VMEM((total, HD), BF16),
            pltpu.VMEM((HD, total), F32),
            pltpu.VMEM((KB, total), BF16),
            pltpu.VMEM((KB, total), BF16),
        ],
        compiler_params=params(),
        cost_estimate=cost(5 * 2 * total * total * 256, heads.size * 4, total * total),
        name="attend_back",
    )(scalars, heads, grads, out, lse)


def input_grad_kernel(joined_ref, weight_ref, frames_ref, res_grad_ref, out_ref, joined, grads):
    step = pl.program_id(0)
    heads = joined_ref.shape[0]

    @pl.when(step == 0)
    def _():
        for h in range(heads):
            for t in range(3):
                row = (t * heads + h) * HD
                joined[row : row + HD, :] = joined_ref[h, t * HD : (t + 1) * HD, :]

    block = weight_ref.shape[0]
    start = pl.multiple_of(step * block, block)
    grads[pl.ds(start, block), :] = dot(weight_ref[...], joined[...])

    @pl.when(step == pl.num_programs(0) - 1)
    def _():
        unit, scale = normalize(frames_ref[...].astype(F32))
        back = normalize_back(unit, scale, grads[...].T)
        out_ref[...] = (res_grad_ref[...] + back).astype(BF16)


def input_gradient(joined, w_qkv, frames, res_grad):
    rows, width = frames.shape
    block = 512
    return pl.pallas_call(
        input_grad_kernel,
        grid=(width // block,),
        in_specs=[
            pl.BlockSpec(memory_space=pltpu.VMEM),
            pl.BlockSpec((block, w_qkv.shape[1]), lambda j: (j, 0)),
            whole(frames.shape),
            whole(frames.shape),
        ],
        out_specs=whole(frames.shape),
        out_shape=jax.ShapeDtypeStruct(frames.shape, BF16),
        scratch_shapes=[
            pltpu.VMEM((w_qkv.shape[1], rows), BF16),
            pltpu.VMEM((width, rows), F32),
        ],
        compiler_params=params(),
        name="input_gradient",
    )(local_memory(joined), w_qkv, frames, res_grad)


def parts_kernel(scalars, grads_ref, back_ref, normed_ref, *rest):
    send_refs, columns = rest[:SLOW], rest[SLOW]
    count, wide, rows = grads_ref.shape

    @pl.when(pl.program_id(0) == 0)
    def _():
        taps = jnp.zeros(((KW + 1) // 2, rows), F32)
        for i in range(count):
            columns[:, i * rows : (i + 1) * rows] = grads_ref[i]
            taps = taps + back_ref[i, HD:, :].astype(F32)
        pair = halves(jnp.concatenate([taps[:, 0:HD], taps[:, HD:]], axis=0))
        for send_ref in send_refs:
            send_ref[TAPS:, :] = pair

    part = dot(columns[...], normed_ref[...])
    each = part.shape[1] // FAST
    pieces = []
    for i in range(FAST):
        piece = part[:, i * each : (i + 1) * each]
        pieces.append(jnp.concatenate([piece[0:CUT], piece[CUT:]], axis=1).astype(BF16))
    for k, send_ref in enumerate(send_refs):

        @pl.when(pl.program_id(0) == k)
        def _():
            for i, piece in enumerate(pieces):
                send_ref[i * CUT : (i + 1) * CUT, :] = piece


def gradient_parts(scalars, grads, back, normed_all):
    count, wide, rows = grads.shape
    total, width = normed_all.shape
    return pl.pallas_call(
        parts_kernel,
        grid_spec=pltpu.PrefetchScalarGridSpec(
            num_scalar_prefetch=1,
            grid=(SLOW,),
            in_specs=[
                pl.BlockSpec(grads.shape, lambda j, place: (0, 0, 0)),
                pl.BlockSpec(back.shape, lambda j, place: (0, 0, 0)),
                pl.BlockSpec((total, width // SLOW), lambda j, place: (0, place[4] ^ j)),
            ],
            out_specs=[pl.BlockSpec((TAPS + KW + 1, 128), lambda j, place: (0, 0))] * SLOW,
            scratch_shapes=[pltpu.VMEM((wide, total), BF16)],
        ),
        out_shape=[jax.ShapeDtypeStruct((TAPS + KW + 1, 128), BF16)] * SLOW,
        compiler_params=params(),
        name="gradient_parts",
    )(scalars, grads, back, normed_all)


def sum_four(own, one, two, three):
    return (own.astype(F32) + one.astype(F32)) + (two.astype(F32) + three.astype(F32))


def fold_first_kernel(scalars, one, two, three, four, round_ref, *rest):
    picks, send_refs = rest[:SLOW], rest[SLOW : SLOW + FAST]
    pieces, outer = rest[SLOW + FAST :]
    width = round_ref.shape[1]
    rows = picks[0].shape[1]
    right = []
    for k in range(SLOW):
        first = pl.multiple_of((scalars[4] ^ k) * rows, rows)
        right.append(round_ref[pl.ds(first, rows), :])
    left = jnp.concatenate([ref[...] for ref in picks], axis=1)
    outer[...] = dot(left, jnp.concatenate(right, axis=0))
    total = sum_four(one[...], two[...], three[...], four[...])
    pair = halves(joined_halves(total[TAPS:]))
    for i in range(FAST):
        pieces[i] = total[i * CUT : (i + 1) * CUT].astype(BF16)
    for k, send_ref in enumerate(send_refs):
        send_ref[0:CUT, :] = pieces[scalars[3] ^ k]
        send_ref[CUT:LAST, :] = pair
        own = pl.ds(pl.multiple_of((scalars[3] ^ k) * HD, HD), HD)
        for c in range(width // 128):
            at = LAST + c * HD
            send_ref[at : at + HD, :] = outer[own, c * 128 : (c + 1) * 128].astype(BF16)


def fold_first(scalars, blocks, rounded_all, picks):
    vmem = pl.BlockSpec(memory_space=pltpu.VMEM)
    return pl.pallas_call(
        fold_first_kernel,
        in_specs=[SMEM] + [vmem] * (5 + SLOW),
        out_shape=[jax.ShapeDtypeStruct((LAST + OUT, 128), BF16)] * FAST,
        scratch_shapes=[
            pltpu.VMEM((FAST, CUT, 128), BF16),
            pltpu.VMEM((FAST * HD, rounded_all.shape[1]), F32),
        ],
        compiler_params=params(),
        name="fold_first",
    )(scalars, *blocks, rounded_all, *picks)


def fold_last_kernel(*refs, scale):
    qkv_ref, send_ref = refs[4:]
    total = sum_four(*(ref[...] for ref in refs[0:4]))
    model_rows = (total[0:CUT] * scale).T
    qkv_ref[:, 0:CUT] = model_rows[0:HD]
    qkv_ref[:, CUT:] = model_rows[HD:]
    pair = halves(joined_halves(total[CUT:LAST]))
    outer = total[LAST:]
    count = send_ref.shape[0]
    each = HD // count
    for i in range(count):
        pieces = [outer[c * HD + i * each : c * HD + (i + 1) * each] for c in range(OUT // HD)]
        send_ref[i, 0 : OUT // count, :] = jnp.concatenate(pieces, axis=0).astype(BF16)
        send_ref[i, OUT // count :, :] = pair


def fold_last(blocks, seq_count, scale):
    vmem = pl.BlockSpec(memory_space=pltpu.VMEM)
    return pl.pallas_call(
        lambda *refs: fold_last_kernel(*refs, scale=scale),
        in_specs=[vmem] * 4,
        out_shape=[
            jax.ShapeDtypeStruct((HD, 3 * HD), F32),
            jax.ShapeDtypeStruct((seq_count, OUT // seq_count + KW + 1, 128), BF16),
        ],
        compiler_params=params(),
        name="fold_last",
    )(*blocks)


def finish_kernel(recv_ref, out_ref, taps_ref, *, scale):
    count = recv_ref.shape[0]
    each = out_ref.shape[0]
    wide = OUT // count
    total = recv_ref[0, 0:wide, :].astype(F32)
    for i in range(1, count):
        total = total + recv_ref[i, 0:wide, :].astype(F32)
    total = total * scale
    for c in range(OUT // HD):
        out_ref[:, c * 128 : (c + 1) * 128] = total[c * each : (c + 1) * each]
    for i in range(count // 2):
        both = [joined_halves(recv_ref[2 * i + k, wide:, :].astype(F32)) for k in range(2)]
        both = jnp.concatenate(both, axis=1) * scale
        taps_ref[:, i * 2 * HD : (i + 1) * 2 * HD] = both[0:KW]


def finish(recv, width, scale):
    count = recv.shape[0]
    vmem = pl.BlockSpec(memory_space=pltpu.VMEM)
    return pl.pallas_call(
        lambda *refs: finish_kernel(*refs, scale=scale),
        in_specs=[vmem],
        out_shape=[
            jax.ShapeDtypeStruct((HD // count, width), F32),
            jax.ShapeDtypeStruct((KW, width), F32),
        ],
        compiler_params=params(),
        name="finish",
    )(recv)


def exchange(blocks, step):
    pairs = lambda k: [(d, d ^ (step * k)) for d in range(FAST * SLOW)]
    moved = [
        local_memory(lax.ppermute(block, "dp", pairs(k))) for k, block in enumerate(blocks) if k
    ]
    return [blocks[0]] + moved


def local(frames, cotangent, w_qkv, w_out, w_conv, lengths):
    seq_count = lax.axis_size("seq")
    data_count = lax.axis_size("dp")
    rows, width = frames.shape[1:]
    first = lax.axis_index("seq") * rows
    grad_scale = 1.0 / math.sqrt(data_count * rows * seq_count)
    position = lax.axis_index("dp")
    fast = position % FAST
    slow = position // FAST
    place = [fast, slow]
    scalars = jnp.stack([lengths[0], first, jnp.zeros((), jnp.int32)] + place)
    x = frames[0]
    g = cotangent[0]

    forward = [(i, i + 1) for i in range(seq_count - 1)]
    backward = [(i + 1, i) for i in range(seq_count - 1)]
    low = lax.ppermute(jnp.concatenate([x[-HALO:], g[-HALO:]], axis=0), "seq", forward)
    high = lax.ppermute(jnp.concatenate([x[:HALO], g[:HALO]], axis=0), "seq", backward)
    x_side = jnp.concatenate([low[:HALO], high[:HALO]], axis=0)
    g_side = jnp.concatenate([low[HALO:], high[HALO:]], axis=0)

    normed, send = project(x, w_qkv)
    heads = lax.all_to_all(send, "seq", 0, 0, tiled=True)
    heads_near = local_memory(heads)
    normed_all = lax.all_gather(normed, "seq", axis=0, tiled=True)
    send, out, lse = attend(scalars, heads_near)
    att = local_memory(lax.all_to_all(send, "seq", 0, 0, tiled=True))
    output, res_grad, send, rounded, *picks = middle(scalars, att, x, x_side, g, g_side, w_out, w_conv)
    back = lax.all_to_all(send, "seq", 0, 0, tiled=True)
    far = [[FAST * i + j for i in range(SLOW)] for j in range(FAST)]
    rounded_all = lax.all_gather(rounded, "dp", axis=0, axis_index_groups=far, tiled=True)
    back, picks = lax.optimization_barrier((back, exchange(picks, FAST)))
    send = attend_back(scalars, heads, local_memory(back), out, lse)
    joined = lax.all_to_all(send, "seq", 0, 0, tiled=True)
    parts = exchange(gradient_parts(scalars, send, back, normed_all), FAST)
    parts = exchange(fold_first(scalars, parts, rounded_all, picks), 1)
    qkv, send = fold_last(parts, seq_count, grad_scale)
    input_grad = input_gradient(joined, w_qkv, x, res_grad)
    recv = lax.all_to_all(send, "seq", 0, 0, tiled=True)
    out_total, taps_total = finish(local_memory(recv), width, grad_scale)
    return (
        output[None],
        input_grad[None],
        qkv.reshape(width // data_count, 3, HD),
        out_total,
        taps_total,
    )


def solution(mesh):
    placed = (P("dp", "seq", None), P("dp", "seq", None), P(), P(), P(), P("dp"))
    return jax.shard_map(
        local,
        mesh=mesh,
        in_specs=placed,
        out_specs=(
            P("dp", "seq", None),
            P("dp", "seq", None),
            P("dp", None, "seq"),
            P(("dp", "seq"), None),
            P(),
        ),
        check_vma=False,
    )
```

```python
import math

import jax
import jax.numpy as jnp
from jax import lax
from jax.experimental import pallas as pl
from jax.experimental.pallas import tpu as pltpu
from jax.sharding import PartitionSpec as P

HEADS = 16
KW = 31
HD = 64
HALO = 32
QUERIES = 512
KEYS = 256
QB = 256
KB = 512
F32 = jnp.float32
BF16 = jnp.bfloat16
LIMIT = 56 * 1024 * 1024
CUT = 96
FAST = 4
SLOW = 4
TAPS = FAST * CUT
LAST = CUT + KW + 1
OUT = 8 * HD


def dot(a, b, ca=1, cb=0):
    return lax.dot_general(a, b, (((ca,), (cb,)), ((), ())), preferred_element_type=F32)


def normalize(rows):
    center = rows - jnp.mean(rows, axis=-1, keepdims=True)
    scale = lax.rsqrt(jnp.mean(center * center, axis=-1, keepdims=True) + 1e-05)
    return center * scale, scale


def normalize_back(unit, scale, upstream):
    return scale * (
        upstream
        - jnp.mean(upstream, axis=-1, keepdims=True)
        - unit * jnp.mean(upstream * unit, axis=-1, keepdims=True)
    )


def params(**kw):
    return pltpu.CompilerParams(vmem_limit_bytes=LIMIT, **kw)


def cost(flops, moved, expos=0):
    return pl.CostEstimate(flops=flops, bytes_accessed=moved, transcendentals=expos)


def local_memory(array):
    return pltpu.with_memory_space_constraint(array, pltpu.VMEM)


def whole(shape):
    return pl.BlockSpec(shape, lambda *_: (0,) * len(shape))


def halves(exact):
    top = exact.astype(BF16)
    rest = (exact - top.astype(F32)).astype(BF16)
    return jnp.concatenate([top, rest], axis=1)


def joined_halves(pair):
    return pair[:, : pair.shape[1] // 2] + pair[:, pair.shape[1] // 2 :]


SMEM = pl.BlockSpec(memory_space=pltpu.SMEM)


def project_kernel(frames_ref, weight_ref, normed_ref, send_ref):
    @pl.when(pl.program_id(0) == 0)
    def _():
        unit, _ = normalize(frames_ref[...].astype(F32))
        normed_ref[...] = unit.astype(BF16)

    part = dot(normed_ref[...], weight_ref[...]).astype(BF16)
    send_ref[...] = part.T.reshape(send_ref.shape)


def project(frames, w_qkv):
    rows, width = frames.shape
    cols = 1024
    per = cols // HD
    groups = HEADS // per
    return pl.pallas_call(
        project_kernel,
        grid=(3 * groups,),
        in_specs=[whole(frames.shape), pl.BlockSpec((width, cols), lambda j: (0, j))],
        out_specs=[
            whole(frames.shape),
            pl.BlockSpec((per, HD, rows), lambda j: (j % groups, j // groups, 0)),
        ],
        out_shape=[
            jax.ShapeDtypeStruct(frames.shape, BF16),
            jax.ShapeDtypeStruct((HEADS, 3 * HD, rows), BF16),
        ],
        compiler_params=params(),
        name="project",
    )(frames, w_qkv)


def load_heads(length, heads_ref, query, keys, count, rows):
    extra = lax.broadcasted_iota(jnp.int32, (HD, rows), 0)
    frame = lax.broadcasted_iota(jnp.int32, (HD, rows), 1)
    for i in range(count):
        cols = slice(i * rows, (i + 1) * rows)
        query[0:HD, cols] = (heads_ref[i, 0:HD, :].astype(F32) * 0.125).astype(BF16)
        query[HD : 2 * HD, cols] = jnp.where(extra == 0, 1.0, 0.0).astype(BF16)
        masked = jnp.logical_and(extra == 0, frame + i * rows >= length)
        mask = jnp.where(masked, -1e30, 0.0).astype(BF16)
        joined = jnp.concatenate([heads_ref[i, HD : 2 * HD, :], mask], axis=0)
        keys[cols, :] = joined.T


def attend_kernel(
    scalars, heads_ref, send_ref, out_ref, lse_ref, query, keys, value, scores
):
    count, _, rows = heads_ref.shape
    total = count * rows
    load_heads(scalars[0], heads_ref, query, keys, count, rows)
    for i in range(count):
        value[:, i * rows : (i + 1) * rows] = heads_ref[i, 2 * HD : 3 * HD, :]

    def one_block(block, carry):
        cols = pl.ds(pl.multiple_of(block * QUERIES, QUERIES), QUERIES)
        query_cols = query[:, cols]
        peak = None
        for k in range(total // KEYS):
            part = dot(keys[k * KEYS : (k + 1) * KEYS, :], query_cols)
            scores[k * KEYS : (k + 1) * KEYS, :] = part
            top = jnp.max(part.reshape(KEYS // 8, 8, QUERIES), axis=0)
            peak = top if peak is None else jnp.maximum(peak, top)
        peak = jnp.max(peak, axis=0, keepdims=True)
        total_row = jnp.zeros((8, QUERIES), F32)
        acc = jnp.zeros((HD, QUERIES), F32)
        for k in range(total // KEYS):
            expo = jnp.exp(scores[k * KEYS : (k + 1) * KEYS, :] - peak)
            total_row = total_row + jnp.sum(expo.reshape(KEYS // 8, 8, QUERIES), axis=0)
            acc = acc + dot(value[:, k * KEYS : (k + 1) * KEYS], expo.astype(BF16))
        total_row = jnp.sum(total_row, axis=0, keepdims=True)
        out_ref[:, cols] = acc / total_row
        lse_ref[:, cols] = peak + jnp.log(total_row)
        return carry

    lax.fori_loop(0, total // QUERIES, one_block, 0, unroll=True)
    none = jnp.zeros((HD, HALO), F32)
    for i in range(count):
        send_ref[i, 0:HD, :] = out_ref[:, i * rows : (i + 1) * rows].astype(BF16)
        low = out_ref[:, i * rows - HALO : i * rows] if i else none
        high = out_ref[:, (i + 1) * rows : (i + 1) * rows + HALO] if i < count - 1 else none
        sides = jnp.concatenate([low, high], axis=1)
        packed = jnp.concatenate([sides[0 : HD // 2], sides[HD // 2 :]], axis=1)
        send_ref[i, HD : HD + HD // 2, :] = packed.astype(BF16)


def attend(scalars, heads):
    count, _, rows = heads.shape
    total = count * rows
    return pl.pallas_call(
        attend_kernel,
        in_specs=[SMEM, pl.BlockSpec(memory_space=pltpu.VMEM)],
        out_shape=[
            jax.ShapeDtypeStruct((count, HD + HD // 2, rows), BF16),
            jax.ShapeDtypeStruct((HD, total), F32),
            jax.ShapeDtypeStruct((1, total), F32),
        ],
        scratch_shapes=[
            pltpu.VMEM((2 * HD, total), BF16),
            pltpu.VMEM((total, 2 * HD), BF16),
            pltpu.VMEM((HD, total), BF16),
            pltpu.VMEM((total, QUERIES), F32),
        ],
        compiler_params=params(),
        cost_estimate=cost(2 * 2 * total * total * 256, heads.size * 2, total * total),
        name="attend",
    )(scalars, heads)


def middle_kernel(
    scalars,
    att_ref,
    frames_ref,
    grads_ref,
    low_ref,
    high_ref,
    w_out_ref,
    w_conv_ref,
    output_ref,
    res_grad_ref,
    send_ref,
    round_ref,
    pick_one,
    pick_two,
    pick_three,
    pick_four,
    taps_ref,
    conv_in,
    grad_all,
    residual,
    window,
    window_back,
    conv_grad,
):
    rows, width = frames_ref.shape
    heads = att_ref.shape[0]
    length = scalars[0]
    first = scalars[1]
    zero = scalars[2]
    half = HD // 2
    body = slice(HALO, HALO + rows)

    attended = att_ref[:, 0:HD, :].reshape(width, rows).T
    main = frames_ref[...].astype(F32) + dot(attended, w_out_ref[...])
    packed = att_ref[:, HD : HD + half, :].reshape(heads * half, rows).T
    split_w = w_out_ref[...].reshape(heads, 2, half, width)
    side = dot(packed[0 : 2 * HALO], split_w[:, 0].reshape(heads * half, width))
    side = side + dot(packed[2 * HALO :], split_w[:, 1].reshape(heads * half, width))
    side = jnp.concatenate([low_ref[0:HALO, :], high_ref[0:HALO, :]], axis=0).astype(F32) + side

    def keep_of(count, start):
        frame = lax.broadcasted_iota(jnp.int32, (count, 1), 0) + start
        return jnp.where(jnp.logical_and(frame >= 0, frame < length), 1.0, 0.0)

    main = main.astype(BF16).astype(F32)
    residual[...] = main
    unit, scale = normalize(main)
    keep = keep_of(rows, first)
    conv_in[body, :] = (unit * keep).astype(BF16).astype(F32)
    unit_side, _ = normalize(side.astype(BF16).astype(F32))
    low = unit_side[0:HALO] * keep_of(HALO, first - HALO)
    high = unit_side[HALO:] * keep_of(HALO, first + rows)
    conv_in[0:HALO, :] = low.astype(BF16).astype(F32)
    conv_in[HALO + rows :, :] = high.astype(BF16).astype(F32)
    reach = rows + HALO
    edge = HALO // 2
    grad_all[edge:HALO, :] = low_ref[HALO:, :].astype(F32)
    grad_all[body, :] = grads_ref[...].astype(F32)
    grad_all[HALO + rows : edge + reach, :] = high_ref[HALO:, :].astype(F32)

    def one_chunk(chunk, carry):
        lanes = pl.ds(pl.multiple_of(chunk * 128, 128), 128)
        window[...] = conv_in[:, lanes]
        acc = jnp.zeros((reach, 128), F32)
        for j in range(KW):
            acc = acc + w_conv_ref[j : j + 1, lanes] * window[pl.ds(zero + (1 + j), reach), :]
        gate = jax.nn.sigmoid(acc)
        back = grad_all[edge : edge + reach, lanes] * (gate + acc * gate * (1.0 - gate))
        window_back[...] = back
        gated = acc[edge : edge + rows] * gate[edge : edge + rows]
        output_ref[:, lanes] = (residual[:, lanes] + gated).astype(BF16)
        own = window_back[edge : edge + rows, :]
        acc = jnp.zeros((rows, 128), F32)
        for j in range(KW):
            acc = acc + w_conv_ref[j : j + 1, lanes] * window_back[
                pl.ds(zero + (KW - j), rows), :
            ]
            moved = window[pl.ds(zero + (edge + 1 + j), rows), :]
            taps_ref[j : j + 1, lanes] = jnp.sum(moved * own, axis=0, keepdims=True)
        taps_ref[KW : KW + 1, lanes] = jnp.zeros((1, 128), F32)
        conv_grad[:, lanes] = acc
        return carry

    lax.fori_loop(0, width // 128, one_chunk, 0)
    res_grad = grads_ref[...].astype(F32) + normalize_back(unit, scale, conv_grad[...] * keep)
    res_grad_ref[...] = res_grad
    rounded = res_grad.astype(BF16)
    round_ref[...] = rounded
    for k, pick_ref in enumerate((pick_one, pick_two, pick_three, pick_four)):
        first_head = pl.multiple_of((scalars[4] ^ k) * FAST, FAST)
        pick_ref[...] = att_ref[pl.ds(first_head, FAST), 0:HD, :].reshape(FAST * HD, rows)
    back = dot(w_out_ref[...], rounded, 1, 1).astype(BF16)
    send_ref[:, 0:HD, :] = back.reshape(heads, HD, rows)
    for h in range(heads):
        own = taps_ref[:, h * HD : (h + 1) * HD]
        middle_row = (KW + 1) // 2
        own = jnp.concatenate([own[0:middle_row], own[middle_row:]], axis=1)
        send_ref[h, HD:, :] = own.astype(BF16)


def middle(scalars, att, frames, grads, low, high, w_out, w_conv):
    rows, width = frames.shape
    vmem = pl.BlockSpec(memory_space=pltpu.VMEM)
    return pl.pallas_call(
        middle_kernel,
        in_specs=[SMEM] + [vmem] * 7,
        out_shape=[
            jax.ShapeDtypeStruct((rows, width), BF16),
            jax.ShapeDtypeStruct((rows, width), F32),
            jax.ShapeDtypeStruct((HEADS, HD + (KW + 1) // 2, rows), BF16),
            jax.ShapeDtypeStruct((rows, width), BF16),
        ]
        + [jax.ShapeDtypeStruct((FAST * HD, rows), BF16)] * SLOW,
        scratch_shapes=[
            pltpu.VMEM((KW + 1, width), F32),
            pltpu.VMEM((rows + 2 * HALO, width), F32),
            pltpu.VMEM((rows + 2 * HALO, width), F32),
            pltpu.VMEM((rows, width), F32),
            pltpu.VMEM((rows + 2 * HALO, 128), F32),
            pltpu.VMEM((rows + HALO, 128), F32),
            pltpu.VMEM((rows, width), F32),
        ],
        compiler_params=params(),
        name="middle",
    )(scalars, att, frames, grads, low, high, w_out, w_conv)


def attend_back_kernel(
    scalars, heads_ref, grads_ref, out_ref, lse_ref, send_ref,
    query, keys, value_t, grad_t, query_rows, grad_rows, query_grad, probs, score_grads,
):
    count, _, rows = heads_ref.shape
    total = count * rows
    load_heads(scalars[0], heads_ref, query, keys, count, rows)
    for i in range(count):
        cols = slice(i * rows, (i + 1) * rows)
        block = grads_ref[i, 0:HD, :]
        grad_t[:, cols] = block
        both = jnp.concatenate([query[0:HD, cols], block], axis=0).T
        query_rows[cols, :] = both[:, 0:HD]
        grad_rows[cols, :] = both[:, HD:]
        value_t[cols, :] = heads_ref[i, 2 * HD : 3 * HD, :].T
    query_grad[...] = jnp.zeros_like(query_grad)
    lse = lse_ref[...]
    delta = jnp.sum(grad_t[...].astype(F32) * out_ref[...], axis=0, keepdims=True)

    def one_block(block, carry):
        span = pl.ds(pl.multiple_of(block * KB, KB), KB)
        key_rows = keys[span, :]
        value_rows = value_t[span, :]
        for q in range(total // QB):
            cols = slice(q * QB, (q + 1) * QB)
            prob = jnp.exp(dot(key_rows, query[:, cols]) - lse[:, cols])
            prob_grad = dot(value_rows, grad_t[:, cols])
            probs[:, cols] = prob.astype(BF16)
            score_grads[:, cols] = (prob * (prob_grad - delta[:, cols])).astype(BF16)
        key_grad = dot(score_grads[...], query_rows[...])
        value_grad = dot(probs[...], grad_rows[...])
        key_cols = key_rows[:, 0:HD].T
        query_grad[...] += dot(key_cols, score_grads[...])
        joined = jnp.concatenate([key_grad, value_grad], axis=1).T.astype(BF16)
        for i in range(KB // rows):
            send_ref[block * (KB // rows) + i, HD : 3 * HD, :] = joined[:, i * rows : (i + 1) * rows]
        return carry

    lax.fori_loop(0, total // KB, one_block, 0, unroll=True)
    for i in range(count):
        cols = slice(i * rows, (i + 1) * rows)
        send_ref[i, 0:HD, :] = (query_grad[:, cols] * 0.125).astype(BF16)


def attend_back(scalars, heads, grads, out, lse):
    count, _, rows = heads.shape
    total = count * rows
    vmem = pl.BlockSpec(memory_space=pltpu.VMEM)
    return pl.pallas_call(
        attend_back_kernel,
        in_specs=[SMEM] + [vmem] * 4,
        out_shape=jax.ShapeDtypeStruct(heads.shape, BF16),
        scratch_shapes=[
            pltpu.VMEM((2 * HD, total), BF16),
            pltpu.VMEM((total, 2 * HD), BF16),
            pltpu.VMEM((total, HD), BF16),
            pltpu.VMEM((HD, total), BF16),
            pltpu.VMEM((total, HD), BF16),
            pltpu.VMEM((total, HD), BF16),
            pltpu.VMEM((HD, total), F32),
            pltpu.VMEM((KB, total), BF16),
            pltpu.VMEM((KB, total), BF16),
        ],
        compiler_params=params(),
        cost_estimate=cost(5 * 2 * total * total * 256, heads.size * 4, total * total),
        name="attend_back",
    )(scalars, heads, grads, out, lse)


def input_grad_kernel(joined_ref, weight_ref, frames_ref, res_grad_ref, out_ref, joined, grads):
    step = pl.program_id(0)
    heads = joined_ref.shape[0]

    @pl.when(step == 0)
    def _():
        for h in range(heads):
            for t in range(3):
                row = (t * heads + h) * HD
                joined[row : row + HD, :] = joined_ref[h, t * HD : (t + 1) * HD, :]

    block = weight_ref.shape[0]
    start = pl.multiple_of(step * block, block)
    grads[pl.ds(start, block), :] = dot(weight_ref[...], joined[...])

    @pl.when(step == pl.num_programs(0) - 1)
    def _():
        unit, scale = normalize(frames_ref[...].astype(F32))
        back = normalize_back(unit, scale, grads[...].T)
        out_ref[...] = (res_grad_ref[...] + back).astype(BF16)


def input_gradient(joined, w_qkv, frames, res_grad):
    rows, width = frames.shape
    block = 512
    return pl.pallas_call(
        input_grad_kernel,
        grid=(width // block,),
        in_specs=[
            pl.BlockSpec(memory_space=pltpu.VMEM),
            pl.BlockSpec((block, w_qkv.shape[1]), lambda j: (j, 0)),
            whole(frames.shape),
            whole(frames.shape),
        ],
        out_specs=whole(frames.shape),
        out_shape=jax.ShapeDtypeStruct(frames.shape, BF16),
        scratch_shapes=[
            pltpu.VMEM((w_qkv.shape[1], rows), BF16),
            pltpu.VMEM((width, rows), F32),
        ],
        compiler_params=params(),
        name="input_gradient",
    )(local_memory(joined), w_qkv, frames, res_grad)


def parts_kernel(scalars, grads_ref, back_ref, normed_ref, *rest):
    send_refs, columns = rest[:SLOW], rest[SLOW]
    count, wide, rows = grads_ref.shape

    @pl.when(pl.program_id(0) == 0)
    def _():
        taps = jnp.zeros(((KW + 1) // 2, rows), F32)
        for i in range(count):
            columns[:, i * rows : (i + 1) * rows] = grads_ref[i]
            taps = taps + back_ref[i, HD:, :].astype(F32)
        pair = halves(jnp.concatenate([taps[:, 0:HD], taps[:, HD:]], axis=0))
        for send_ref in send_refs:
            send_ref[TAPS:, :] = pair

    part = dot(columns[...], normed_ref[...])
    each = part.shape[1] // FAST
    pieces = []
    for i in range(FAST):
        piece = part[:, i * each : (i + 1) * each]
        pieces.append(jnp.concatenate([piece[0:CUT], piece[CUT:]], axis=1).astype(BF16))
    for k, send_ref in enumerate(send_refs):

        @pl.when(pl.program_id(0) == k)
        def _():
            for i, piece in enumerate(pieces):
                send_ref[i * CUT : (i + 1) * CUT, :] = piece


def gradient_parts(scalars, grads, back, normed_all):
    count, wide, rows = grads.shape
    total, width = normed_all.shape
    return pl.pallas_call(
        parts_kernel,
        grid_spec=pltpu.PrefetchScalarGridSpec(
            num_scalar_prefetch=1,
            grid=(SLOW,),
            in_specs=[
                pl.BlockSpec(grads.shape, lambda j, place: (0, 0, 0)),
                pl.BlockSpec(back.shape, lambda j, place: (0, 0, 0)),
                pl.BlockSpec((total, width // SLOW), lambda j, place: (0, place[4] ^ j)),
            ],
            out_specs=[pl.BlockSpec((TAPS + KW + 1, 128), lambda j, place: (0, 0))] * SLOW,
            scratch_shapes=[pltpu.VMEM((wide, total), BF16)],
        ),
        out_shape=[jax.ShapeDtypeStruct((TAPS + KW + 1, 128), BF16)] * SLOW,
        compiler_params=params(),
        name="gradient_parts",
    )(scalars, grads, back, normed_all)


def sum_four(own, one, two, three):
    return (own.astype(F32) + one.astype(F32)) + (two.astype(F32) + three.astype(F32))


def fold_first_kernel(scalars, one, two, three, four, round_ref, *rest):
    picks, send_refs = rest[:SLOW], rest[SLOW : SLOW + FAST]
    pieces, outer = rest[SLOW + FAST :]
    width = round_ref.shape[1]
    rows = picks[0].shape[1]
    right = []
    for k in range(SLOW):
        first = pl.multiple_of((scalars[4] ^ k) * rows, rows)
        right.append(round_ref[pl.ds(first, rows), :])
    left = jnp.concatenate([ref[...] for ref in picks], axis=1)
    outer[...] = dot(left, jnp.concatenate(right, axis=0))
    total = sum_four(one[...], two[...], three[...], four[...])
    pair = halves(joined_halves(total[TAPS:]))
    for i in range(FAST):
        pieces[i] = total[i * CUT : (i + 1) * CUT].astype(BF16)
    for k, send_ref in enumerate(send_refs):
        send_ref[0:CUT, :] = pieces[scalars[3] ^ k]
        send_ref[CUT:LAST, :] = pair
        own = pl.ds(pl.multiple_of((scalars[3] ^ k) * HD, HD), HD)
        for c in range(width // 128):
            at = LAST + c * HD
            send_ref[at : at + HD, :] = outer[own, c * 128 : (c + 1) * 128].astype(BF16)


def fold_first(scalars, blocks, rounded_all, picks):
    vmem = pl.BlockSpec(memory_space=pltpu.VMEM)
    return pl.pallas_call(
        fold_first_kernel,
        in_specs=[SMEM] + [vmem] * (5 + SLOW),
        out_shape=[jax.ShapeDtypeStruct((LAST + OUT, 128), BF16)] * FAST,
        scratch_shapes=[
            pltpu.VMEM((FAST, CUT, 128), BF16),
            pltpu.VMEM((FAST * HD, rounded_all.shape[1]), F32),
        ],
        compiler_params=params(),
        name="fold_first",
    )(scalars, *blocks, rounded_all, *picks)


def fold_last_kernel(*refs, scale):
    qkv_ref, send_ref = refs[4:]
    total = sum_four(*(ref[...] for ref in refs[0:4]))
    model_rows = (total[0:CUT] * scale).T
    qkv_ref[:, 0:CUT] = model_rows[0:HD]
    qkv_ref[:, CUT:] = model_rows[HD:]
    taps = joined_halves(total[CUT:LAST])
    half = (KW + 1) // 2
    pair = jnp.concatenate([taps[0:half], taps[half:]], axis=1).astype(BF16)
    outer = total[LAST:]
    count = send_ref.shape[0]
    each = HD // count
    for i in range(count):
        pieces = [outer[c * HD + i * each : c * HD + (i + 1) * each] for c in range(OUT // HD)]
        send_ref[i, 0 : OUT // count, :] = jnp.concatenate(pieces, axis=0).astype(BF16)
        send_ref[i, OUT // count :, :] = pair


def fold_last(blocks, seq_count, scale):
    vmem = pl.BlockSpec(memory_space=pltpu.VMEM)
    return pl.pallas_call(
        lambda *refs: fold_last_kernel(*refs, scale=scale),
        in_specs=[vmem] * 4,
        out_shape=[
            jax.ShapeDtypeStruct((HD, 3 * HD), F32),
            jax.ShapeDtypeStruct((seq_count, OUT // seq_count + (KW + 1) // 2, 128), BF16),
        ],
        compiler_params=params(),
        name="fold_last",
    )(*blocks)


def finish_kernel(recv_ref, out_ref, taps_ref, *, scale):
    count = recv_ref.shape[0]
    each = out_ref.shape[0]
    wide = OUT // count
    total = recv_ref[0, 0:wide, :].astype(F32)
    for i in range(1, count):
        total = total + recv_ref[i, 0:wide, :].astype(F32)
    total = total * scale
    for c in range(OUT // HD):
        out_ref[:, c * 128 : (c + 1) * 128] = total[c * each : (c + 1) * each]
    for i in range(count // 2):
        a = recv_ref[2 * i, wide:, :].astype(F32) * scale
        b = recv_ref[2 * i + 1, wide:, :].astype(F32) * scale
        lanes = slice(i * 2 * HD, (i + 1) * 2 * HD)
        half = (KW + 1) // 2
        taps_ref[0:half, lanes] = jnp.concatenate([a[:, 0:HD], b[:, 0:HD]], axis=1)
        upper = jnp.concatenate([a[:, HD:], b[:, HD:]], axis=1)
        taps_ref[half:KW, lanes] = upper[0 : KW - half]


def finish(recv, width, scale):
    count = recv.shape[0]
    vmem = pl.BlockSpec(memory_space=pltpu.VMEM)
    return pl.pallas_call(
        lambda *refs: finish_kernel(*refs, scale=scale),
        in_specs=[vmem],
        out_shape=[
            jax.ShapeDtypeStruct((HD // count, width), F32),
            jax.ShapeDtypeStruct((KW, width), F32),
        ],
        compiler_params=params(),
        name="finish",
    )(recv)


def exchange(blocks, step):
    pairs = lambda k: [(d, d ^ (step * k)) for d in range(FAST * SLOW)]
    moved = [
        local_memory(lax.ppermute(block, "dp", pairs(k))) for k, block in enumerate(blocks) if k
    ]
    return [blocks[0]] + moved


def local(frames, cotangent, w_qkv, w_out, w_conv, lengths):
    seq_count = lax.axis_size("seq")
    data_count = lax.axis_size("dp")
    rows, width = frames.shape[1:]
    first = lax.axis_index("seq") * rows
    grad_scale = 1.0 / math.sqrt(data_count * rows * seq_count)
    position = lax.axis_index("dp")
    fast = position % FAST
    slow = position // FAST
    place = [fast, slow]
    scalars = jnp.stack([lengths[0], first, jnp.zeros((), jnp.int32)] + place)
    x = frames[0]
    g = cotangent[0]

    forward = [(i, i + 1) for i in range(seq_count - 1)]
    backward = [(i + 1, i) for i in range(seq_count - 1)]
    edge = HALO // 2
    low = lax.ppermute(jnp.concatenate([x[-HALO:], g[-edge:]], axis=0), "seq", forward)
    high = lax.ppermute(jnp.concatenate([x[:HALO], g[:edge]], axis=0), "seq", backward)
    low, high = local_memory(low), local_memory(high)

    normed, send = project(x, w_qkv)
    heads = lax.all_to_all(send, "seq", 0, 0, tiled=True)
    heads_near = local_memory(heads)
    normed_all = lax.all_gather(normed, "seq", axis=0, tiled=True)
    send, out, lse = attend(scalars, heads_near)
    att = local_memory(lax.all_to_all(send, "seq", 0, 0, tiled=True))
    output, res_grad, send, rounded, *picks = middle(scalars, att, x, g, low, high, w_out, w_conv)
    back = lax.all_to_all(send, "seq", 0, 0, tiled=True)
    far = [[FAST * i + j for i in range(SLOW)] for j in range(FAST)]
    rounded_all = lax.all_gather(rounded, "dp", axis=0, axis_index_groups=far, tiled=True)
    back, picks = lax.optimization_barrier((back, exchange(picks, FAST)))
    send = attend_back(scalars, heads, local_memory(back), out, lse)
    joined = lax.all_to_all(send, "seq", 0, 0, tiled=True)
    parts = exchange(gradient_parts(scalars, send, back, normed_all), FAST)
    parts = exchange(fold_first(scalars, parts, rounded_all, picks), 1)
    qkv, send = fold_last(parts, seq_count, grad_scale)
    input_grad = input_gradient(joined, w_qkv, x, res_grad)
    recv = lax.all_to_all(send, "seq", 0, 0, tiled=True)
    out_total, taps_total = finish(local_memory(recv), width, grad_scale)
    return (
        output[None],
        input_grad[None],
        qkv.reshape(width // data_count, 3, HD),
        out_total,
        taps_total,
    )


def solution(mesh):
    placed = (P("dp", "seq", None), P("dp", "seq", None), P(), P(), P(), P("dp"))
    return jax.shard_map(
        local,
        mesh=mesh,
        in_specs=placed,
        out_specs=(
            P("dp", "seq", None),
            P("dp", "seq", None),
            P("dp", None, "seq"),
            P(("dp", "seq"), None),
            P(),
        ),
        check_vma=False,
    )
```

```python
import math

import jax
import jax.numpy as jnp
from jax import lax
from jax.experimental import pallas as pl
from jax.experimental.pallas import tpu as pltpu
from jax.sharding import PartitionSpec as P

HEADS = 16
KW = 31
HD = 64
HALO = 32
QUERIES = 512
KEYS = 256
QB = 256
KB = 512
F32 = jnp.float32
BF16 = jnp.bfloat16
LIMIT = 56 * 1024 * 1024
CUT = 96
FAST = 4
SLOW = 4
TAPS = FAST * CUT
LAST = CUT + KW + 1
OUT = 8 * HD


def dot(a, b, ca=1, cb=0):
    return lax.dot_general(a, b, (((ca,), (cb,)), ((), ())), preferred_element_type=F32)


def normalize(rows):
    center = rows - jnp.mean(rows, axis=-1, keepdims=True)
    scale = lax.rsqrt(jnp.mean(center * center, axis=-1, keepdims=True) + 1e-05)
    return center * scale, scale


def normalize_back(unit, scale, upstream):
    return scale * (
        upstream
        - jnp.mean(upstream, axis=-1, keepdims=True)
        - unit * jnp.mean(upstream * unit, axis=-1, keepdims=True)
    )


def params(**kw):
    return pltpu.CompilerParams(vmem_limit_bytes=LIMIT, **kw)


def cost(flops, moved, expos=0):
    return pl.CostEstimate(flops=flops, bytes_accessed=moved, transcendentals=expos)


def local_memory(array):
    return pltpu.with_memory_space_constraint(array, pltpu.VMEM)


def whole(shape):
    return pl.BlockSpec(shape, lambda *_: (0,) * len(shape))


def halves(exact):
    top = exact.astype(BF16)
    rest = (exact - top.astype(F32)).astype(BF16)
    return jnp.concatenate([top, rest], axis=1)


def joined_halves(pair):
    return pair[:, : pair.shape[1] // 2] + pair[:, pair.shape[1] // 2 :]


SMEM = pl.BlockSpec(memory_space=pltpu.SMEM)


def project_kernel(frames_ref, weight_ref, normed_ref, send_ref):
    @pl.when(pl.program_id(0) == 0)
    def _():
        unit, _ = normalize(frames_ref[...].astype(F32))
        normed_ref[...] = unit.astype(BF16)

    part = dot(normed_ref[...], weight_ref[...]).astype(BF16)
    send_ref[...] = part.T.reshape(send_ref.shape)


def project(frames, w_qkv):
    rows, width = frames.shape
    cols = 1024
    per = cols // HD
    groups = HEADS // per
    return pl.pallas_call(
        project_kernel,
        grid=(3 * groups,),
        in_specs=[whole(frames.shape), pl.BlockSpec((width, cols), lambda j: (0, j))],
        out_specs=[
            whole(frames.shape),
            pl.BlockSpec((per, HD, rows), lambda j: (j % groups, j // groups, 0)),
        ],
        out_shape=[
            jax.ShapeDtypeStruct(frames.shape, BF16),
            jax.ShapeDtypeStruct((HEADS, 3 * HD, rows), BF16),
        ],
        compiler_params=params(),
        name="project",
    )(frames, w_qkv)


def load_heads(length, heads_ref, query, keys, count, rows):
    extra = lax.broadcasted_iota(jnp.int32, (HD, rows), 0)
    frame = lax.broadcasted_iota(jnp.int32, (HD, rows), 1)
    for i in range(count):
        cols = slice(i * rows, (i + 1) * rows)
        query[0:HD, cols] = (heads_ref[i, 0:HD, :].astype(F32) * 0.125).astype(BF16)
        query[HD : 2 * HD, cols] = jnp.where(extra == 0, 1.0, 0.0).astype(BF16)
        masked = jnp.logical_and(extra == 0, frame + i * rows >= length)
        mask = jnp.where(masked, -1e30, 0.0).astype(BF16)
        joined = jnp.concatenate([heads_ref[i, HD : 2 * HD, :], mask], axis=0)
        keys[cols, :] = joined.T


def attend_kernel(
    scalars, heads_ref, send_ref, out_ref, lse_ref, query, keys, value, scores
):
    count, _, rows = heads_ref.shape
    total = count * rows
    load_heads(scalars[0], heads_ref, query, keys, count, rows)
    for i in range(count):
        value[:, i * rows : (i + 1) * rows] = heads_ref[i, 2 * HD : 3 * HD, :]

    def one_block(block, carry):
        cols = pl.ds(pl.multiple_of(block * QUERIES, QUERIES), QUERIES)
        query_cols = query[:, cols]
        peak = None
        for k in range(total // KEYS):
            part = dot(keys[k * KEYS : (k + 1) * KEYS, :], query_cols)
            scores[k * KEYS : (k + 1) * KEYS, :] = part
            top = jnp.max(part.reshape(KEYS // 8, 8, QUERIES), axis=0)
            peak = top if peak is None else jnp.maximum(peak, top)
        peak = jnp.max(peak, axis=0, keepdims=True)
        total_row = jnp.zeros((8, QUERIES), F32)
        acc = jnp.zeros((HD, QUERIES), F32)
        for k in range(total // KEYS):
            expo = jnp.exp(scores[k * KEYS : (k + 1) * KEYS, :] - peak)
            total_row = total_row + jnp.sum(expo.reshape(KEYS // 8, 8, QUERIES), axis=0)
            acc = acc + dot(value[:, k * KEYS : (k + 1) * KEYS], expo.astype(BF16))
        total_row = jnp.sum(total_row, axis=0, keepdims=True)
        out_ref[:, cols] = acc / total_row
        lse_ref[:, cols] = peak + jnp.log(total_row)
        return carry

    lax.fori_loop(0, total // QUERIES, one_block, 0, unroll=True)
    none = jnp.zeros((HD, HALO), F32)
    for i in range(count):
        send_ref[i, 0:HD, :] = out_ref[:, i * rows : (i + 1) * rows].astype(BF16)
        low = out_ref[:, i * rows - HALO : i * rows] if i else none
        high = out_ref[:, (i + 1) * rows : (i + 1) * rows + HALO] if i < count - 1 else none
        sides = jnp.concatenate([low, high], axis=1)
        packed = jnp.concatenate([sides[0 : HD // 2], sides[HD // 2 :]], axis=1)
        send_ref[i, HD : HD + HD // 2, :] = packed.astype(BF16)


def attend(scalars, heads):
    count, _, rows = heads.shape
    total = count * rows
    return pl.pallas_call(
        attend_kernel,
        in_specs=[SMEM, pl.BlockSpec(memory_space=pltpu.VMEM)],
        out_shape=[
            jax.ShapeDtypeStruct((count, HD + HD // 2, rows), BF16),
            jax.ShapeDtypeStruct((HD, total), F32),
            jax.ShapeDtypeStruct((1, total), F32),
        ],
        scratch_shapes=[
            pltpu.VMEM((2 * HD, total), BF16),
            pltpu.VMEM((total, 2 * HD), BF16),
            pltpu.VMEM((HD, total), BF16),
            pltpu.VMEM((total, QUERIES), F32),
        ],
        compiler_params=params(),
        cost_estimate=cost(2 * 2 * total * total * 256, heads.size * 2, total * total),
        name="attend",
    )(scalars, heads)


def middle_kernel(
    scalars,
    att_ref,
    frames_ref,
    grads_ref,
    low_ref,
    high_ref,
    w_out_ref,
    w_conv_ref,
    output_ref,
    res_grad_ref,
    send_ref,
    round_ref,
    pick_one,
    pick_two,
    pick_three,
    pick_four,
    taps_ref,
    conv_in,
    grad_all,
    residual,
    window,
    window_back,
    conv_grad,
):
    rows, width = frames_ref.shape
    heads = att_ref.shape[0]
    length = scalars[0]
    first = scalars[1]
    zero = scalars[2]
    half = HD // 2
    body = slice(HALO, HALO + rows)

    attended = att_ref[:, 0:HD, :].reshape(width, rows).T
    main = frames_ref[...].astype(F32) + dot(attended, w_out_ref[...])
    packed = att_ref[:, HD : HD + half, :].reshape(heads * half, rows).T
    split_w = w_out_ref[...].reshape(heads, 2, half, width)
    side = dot(packed[0 : 2 * HALO], split_w[:, 0].reshape(heads * half, width))
    side = side + dot(packed[2 * HALO :], split_w[:, 1].reshape(heads * half, width))
    side = jnp.concatenate([low_ref[0:HALO, :], high_ref[0:HALO, :]], axis=0).astype(F32) + side

    def keep_of(count, start):
        frame = lax.broadcasted_iota(jnp.int32, (count, 1), 0) + start
        return jnp.where(jnp.logical_and(frame >= 0, frame < length), 1.0, 0.0)

    main = main.astype(BF16).astype(F32)
    residual[...] = main
    unit, scale = normalize(main)
    keep = keep_of(rows, first)
    conv_in[body, :] = (unit * keep).astype(BF16).astype(F32)
    unit_side, _ = normalize(side.astype(BF16).astype(F32))
    low = unit_side[0:HALO] * keep_of(HALO, first - HALO)
    high = unit_side[HALO:] * keep_of(HALO, first + rows)
    conv_in[0:HALO, :] = low.astype(BF16).astype(F32)
    conv_in[HALO + rows :, :] = high.astype(BF16).astype(F32)
    reach = rows + HALO
    edge = HALO // 2
    grad_all[edge:HALO, :] = low_ref[HALO:, :].astype(F32)
    grad_all[body, :] = grads_ref[...].astype(F32)
    grad_all[HALO + rows : edge + reach, :] = high_ref[HALO:, :].astype(F32)

    def one_chunk(chunk, carry):
        lanes = pl.ds(pl.multiple_of(chunk * 128, 128), 128)
        window[...] = conv_in[:, lanes]
        acc = jnp.zeros((reach, 128), F32)
        for j in range(KW):
            acc = acc + w_conv_ref[j : j + 1, lanes] * window[pl.ds(zero + (1 + j), reach), :]
        gate = jax.nn.sigmoid(acc)
        back = grad_all[edge : edge + reach, lanes] * (gate + acc * gate * (1.0 - gate))
        window_back[...] = back
        gated = acc[edge : edge + rows] * gate[edge : edge + rows]
        output_ref[:, lanes] = (residual[:, lanes] + gated).astype(BF16)
        own = window_back[edge : edge + rows, :]
        acc = jnp.zeros((rows, 128), F32)
        for j in range(KW):
            acc = acc + w_conv_ref[j : j + 1, lanes] * window_back[
                pl.ds(zero + (KW - j), rows), :
            ]
            moved = window[pl.ds(zero + (edge + 1 + j), rows), :]
            taps_ref[j : j + 1, lanes] = jnp.sum(moved * own, axis=0, keepdims=True)
        taps_ref[KW : KW + 1, lanes] = jnp.zeros((1, 128), F32)
        conv_grad[:, lanes] = acc
        return carry

    lax.fori_loop(0, width // 128, one_chunk, 0)
    res_grad = grads_ref[...].astype(F32) + normalize_back(unit, scale, conv_grad[...] * keep)
    res_grad_ref[...] = res_grad
    rounded = res_grad.astype(BF16)
    round_ref[...] = rounded
    for k, pick_ref in enumerate((pick_one, pick_two, pick_three, pick_four)):
        first_head = pl.multiple_of((scalars[4] ^ k) * FAST, FAST)
        pick_ref[...] = att_ref[pl.ds(first_head, FAST), 0:HD, :].reshape(FAST * HD, rows)
    back = dot(w_out_ref[...], rounded, 1, 1).astype(BF16)
    send_ref[:, 0:HD, :] = back.reshape(heads, HD, rows)
    for h in range(heads):
        own = taps_ref[:, h * HD : (h + 1) * HD]
        middle_row = (KW + 1) // 2
        own = jnp.concatenate([own[0:middle_row], own[middle_row:]], axis=1)
        send_ref[h, HD:, :] = own.astype(BF16)


def middle(scalars, att, frames, grads, low, high, w_out, w_conv):
    rows, width = frames.shape
    vmem = pl.BlockSpec(memory_space=pltpu.VMEM)
    return pl.pallas_call(
        middle_kernel,
        in_specs=[SMEM] + [vmem] * 7,
        out_shape=[
            jax.ShapeDtypeStruct((rows, width), BF16),
            jax.ShapeDtypeStruct((rows, width), F32),
            jax.ShapeDtypeStruct((HEADS, HD + (KW + 1) // 2, rows), BF16),
            jax.ShapeDtypeStruct((rows, width), BF16),
        ]
        + [jax.ShapeDtypeStruct((FAST * HD, rows), BF16)] * SLOW,
        scratch_shapes=[
            pltpu.VMEM((KW + 1, width), F32),
            pltpu.VMEM((rows + 2 * HALO, width), F32),
            pltpu.VMEM((rows + 2 * HALO, width), F32),
            pltpu.VMEM((rows, width), F32),
            pltpu.VMEM((rows + 2 * HALO, 128), F32),
            pltpu.VMEM((rows + HALO, 128), F32),
            pltpu.VMEM((rows, width), F32),
        ],
        compiler_params=params(),
        name="middle",
    )(scalars, att, frames, grads, low, high, w_out, w_conv)


def attend_back_kernel(
    scalars, heads_ref, grads_ref, out_ref, lse_ref, send_ref,
    query, keys, value_t, grad_t, query_rows, grad_rows, query_grad, probs, score_grads,
):
    count, _, rows = heads_ref.shape
    total = count * rows
    load_heads(scalars[0], heads_ref, query, keys, count, rows)
    for i in range(count):
        cols = slice(i * rows, (i + 1) * rows)
        block = grads_ref[i, 0:HD, :]
        grad_t[:, cols] = block
        both = jnp.concatenate([query[0:HD, cols], block], axis=0).T
        query_rows[cols, :] = both[:, 0:HD]
        grad_rows[cols, :] = both[:, HD:]
        value_t[cols, :] = heads_ref[i, 2 * HD : 3 * HD, :].T
    query_grad[...] = jnp.zeros_like(query_grad)
    lse = lse_ref[...]
    delta = jnp.sum(grad_t[...].astype(F32) * out_ref[...], axis=0, keepdims=True)

    def one_block(block, carry):
        span = pl.ds(pl.multiple_of(block * KB, KB), KB)
        key_rows = keys[span, :]
        value_rows = value_t[span, :]
        for q in range(total // QB):
            cols = slice(q * QB, (q + 1) * QB)
            prob = jnp.exp(dot(key_rows, query[:, cols]) - lse[:, cols])
            prob_grad = dot(value_rows, grad_t[:, cols])
            probs[:, cols] = prob.astype(BF16)
            score_grads[:, cols] = (prob * (prob_grad - delta[:, cols])).astype(BF16)
        key_grad = dot(score_grads[...], query_rows[...])
        value_grad = dot(probs[...], grad_rows[...])
        key_cols = key_rows[:, 0:HD].T
        query_grad[...] += dot(key_cols, score_grads[...])
        joined = jnp.concatenate([key_grad, value_grad], axis=1).T.astype(BF16)
        for i in range(KB // rows):
            send_ref[block * (KB // rows) + i, HD : 3 * HD, :] = joined[:, i * rows : (i + 1) * rows]
        return carry

    lax.fori_loop(0, total // KB, one_block, 0, unroll=True)
    for i in range(count):
        cols = slice(i * rows, (i + 1) * rows)
        send_ref[i, 0:HD, :] = (query_grad[:, cols] * 0.125).astype(BF16)


def attend_back(scalars, heads, grads, out, lse):
    count, _, rows = heads.shape
    total = count * rows
    vmem = pl.BlockSpec(memory_space=pltpu.VMEM)
    return pl.pallas_call(
        attend_back_kernel,
        in_specs=[SMEM] + [vmem] * 4,
        out_shape=jax.ShapeDtypeStruct(heads.shape, BF16),
        scratch_shapes=[
            pltpu.VMEM((2 * HD, total), BF16),
            pltpu.VMEM((total, 2 * HD), BF16),
            pltpu.VMEM((total, HD), BF16),
            pltpu.VMEM((HD, total), BF16),
            pltpu.VMEM((total, HD), BF16),
            pltpu.VMEM((total, HD), BF16),
            pltpu.VMEM((HD, total), F32),
            pltpu.VMEM((KB, total), BF16),
            pltpu.VMEM((KB, total), BF16),
        ],
        compiler_params=params(),
        cost_estimate=cost(5 * 2 * total * total * 256, heads.size * 4, total * total),
        name="attend_back",
    )(scalars, heads, grads, out, lse)


def input_grad_kernel(joined_ref, weight_ref, frames_ref, res_grad_ref, out_ref, joined, grads):
    step = pl.program_id(0)
    heads = joined_ref.shape[0]

    @pl.when(step == 0)
    def _():
        for h in range(heads):
            for t in range(3):
                row = (t * heads + h) * HD
                joined[row : row + HD, :] = joined_ref[h, t * HD : (t + 1) * HD, :]

    block = weight_ref.shape[0]
    start = pl.multiple_of(step * block, block)
    grads[pl.ds(start, block), :] = dot(weight_ref[...], joined[...])

    @pl.when(step == pl.num_programs(0) - 1)
    def _():
        unit, scale = normalize(frames_ref[...].astype(F32))
        back = normalize_back(unit, scale, grads[...].T)
        out_ref[...] = (res_grad_ref[...] + back).astype(BF16)


def input_gradient(joined, w_qkv, frames, res_grad):
    rows, width = frames.shape
    block = 512
    return pl.pallas_call(
        input_grad_kernel,
        grid=(width // block,),
        in_specs=[
            pl.BlockSpec(memory_space=pltpu.VMEM),
            pl.BlockSpec((block, w_qkv.shape[1]), lambda j: (j, 0)),
            whole(frames.shape),
            whole(frames.shape),
        ],
        out_specs=whole(frames.shape),
        out_shape=jax.ShapeDtypeStruct(frames.shape, BF16),
        scratch_shapes=[
            pltpu.VMEM((w_qkv.shape[1], rows), BF16),
            pltpu.VMEM((width, rows), F32),
        ],
        compiler_params=params(),
        name="input_gradient",
    )(local_memory(joined), w_qkv, frames, res_grad)


def parts_kernel(scalars, grads_ref, back_ref, normed_ref, *rest):
    send_refs, columns = rest[:SLOW], rest[SLOW]
    count, wide, rows = grads_ref.shape

    @pl.when(pl.program_id(0) == 0)
    def _():
        taps = jnp.zeros(((KW + 1) // 2, rows), F32)
        for i in range(count):
            columns[:, i * rows : (i + 1) * rows] = grads_ref[i]
            taps = taps + back_ref[i, HD:, :].astype(F32)
        pair = halves(jnp.concatenate([taps[:, 0:HD], taps[:, HD:]], axis=0))
        for send_ref in send_refs:
            send_ref[TAPS:, :] = pair

    part = dot(columns[...], normed_ref[...])
    each = part.shape[1] // FAST
    pieces = []
    for i in range(FAST):
        piece = part[:, i * each : (i + 1) * each]
        pieces.append(jnp.concatenate([piece[0:CUT], piece[CUT:]], axis=1).astype(BF16))
    for k, send_ref in enumerate(send_refs):

        @pl.when(pl.program_id(0) == k)
        def _():
            for i, piece in enumerate(pieces):
                send_ref[i * CUT : (i + 1) * CUT, :] = piece


def gradient_parts(scalars, grads, back, normed_all):
    count, wide, rows = grads.shape
    total, width = normed_all.shape
    return pl.pallas_call(
        parts_kernel,
        grid_spec=pltpu.PrefetchScalarGridSpec(
            num_scalar_prefetch=1,
            grid=(SLOW,),
            in_specs=[
                pl.BlockSpec(grads.shape, lambda j, place: (0, 0, 0)),
                pl.BlockSpec(back.shape, lambda j, place: (0, 0, 0)),
                pl.BlockSpec((total, width // SLOW), lambda j, place: (0, place[4] ^ j)),
            ],
            out_specs=[pl.BlockSpec((TAPS + KW + 1, 128), lambda j, place: (0, 0))] * SLOW,
            scratch_shapes=[pltpu.VMEM((wide, total), BF16)],
        ),
        out_shape=[jax.ShapeDtypeStruct((TAPS + KW + 1, 128), BF16)] * SLOW,
        compiler_params=params(),
        name="gradient_parts",
    )(scalars, grads, back, normed_all)


def sum_four(own, one, two, three):
    return (own.astype(F32) + one.astype(F32)) + (two.astype(F32) + three.astype(F32))


def fold_first_kernel(scalars, one, two, three, four, round_ref, *rest):
    picks, send_refs = rest[:SLOW], rest[SLOW : SLOW + FAST]
    pieces, outer = rest[SLOW + FAST :]
    width = round_ref.shape[1]
    rows = picks[0].shape[1]
    right = []
    for k in range(SLOW):
        first = pl.multiple_of((scalars[4] ^ k) * rows, rows)
        right.append(round_ref[pl.ds(first, rows), :])
    left = jnp.concatenate([ref[...] for ref in picks], axis=1)
    outer[...] = dot(left, jnp.concatenate(right, axis=0))
    total = sum_four(one[...], two[...], three[...], four[...])
    pair = halves(joined_halves(total[TAPS:]))
    for i in range(FAST):
        pieces[i] = total[i * CUT : (i + 1) * CUT].astype(BF16)
    for k, send_ref in enumerate(send_refs):
        send_ref[0:CUT, :] = pieces[scalars[3] ^ k]
        send_ref[CUT:LAST, :] = pair
        own = pl.ds(pl.multiple_of((scalars[3] ^ k) * HD, HD), HD)
        for c in range(width // 128):
            at = LAST + c * HD
            send_ref[at : at + HD, :] = outer[own, c * 128 : (c + 1) * 128].astype(BF16)


def fold_first(scalars, blocks, rounded_all, picks):
    vmem = pl.BlockSpec(memory_space=pltpu.VMEM)
    return pl.pallas_call(
        fold_first_kernel,
        in_specs=[SMEM] + [vmem] * (5 + SLOW),
        out_shape=[jax.ShapeDtypeStruct((LAST + OUT, 128), BF16)] * FAST,
        scratch_shapes=[
            pltpu.VMEM((FAST, CUT, 128), BF16),
            pltpu.VMEM((FAST * HD, rounded_all.shape[1]), F32),
        ],
        compiler_params=params(),
        name="fold_first",
    )(scalars, *blocks, rounded_all, *picks)


def fold_last_kernel(*refs, scale):
    qkv_ref, send_ref = refs[4:]
    total = sum_four(*(ref[...] for ref in refs[0:4]))
    model_rows = (total[0:CUT] * scale).T
    qkv_ref[:, 0:CUT] = model_rows[0:HD]
    qkv_ref[:, CUT:] = model_rows[HD:]
    taps = joined_halves(total[CUT:LAST])
    half = (KW + 1) // 2
    pair = jnp.concatenate([taps[0:half], taps[half:]], axis=1).astype(BF16)
    outer = total[LAST:]
    count = send_ref.shape[0]
    each = HD // count
    for i in range(count):
        pieces = [outer[c * HD + i * each : c * HD + (i + 1) * each] for c in range(OUT // HD)]
        send_ref[i, 0 : OUT // count, :] = jnp.concatenate(pieces, axis=0).astype(BF16)
        send_ref[i, OUT // count :, :] = pair


def fold_last(blocks, seq_count, scale):
    vmem = pl.BlockSpec(memory_space=pltpu.VMEM)
    return pl.pallas_call(
        lambda *refs: fold_last_kernel(*refs, scale=scale),
        in_specs=[vmem] * 4,
        out_shape=[
            jax.ShapeDtypeStruct((HD, 3 * HD), F32),
            jax.ShapeDtypeStruct((seq_count, OUT // seq_count + (KW + 1) // 2, 128), BF16),
        ],
        compiler_params=params(),
        name="fold_last",
    )(*blocks)


def finish_kernel(recv_ref, out_ref, taps_ref, *, scale):
    count = recv_ref.shape[0]
    each = out_ref.shape[0]
    wide = OUT // count
    total = recv_ref[0, 0:wide, :].astype(F32)
    for i in range(1, count):
        total = total + recv_ref[i, 0:wide, :].astype(F32)
    total = total * scale
    for c in range(OUT // HD):
        out_ref[:, c * 128 : (c + 1) * 128] = total[c * each : (c + 1) * each]
    for i in range(count // 2):
        a = recv_ref[2 * i, wide:, :].astype(F32) * scale
        b = recv_ref[2 * i + 1, wide:, :].astype(F32) * scale
        lanes = slice(i * 2 * HD, (i + 1) * 2 * HD)
        half = (KW + 1) // 2
        taps_ref[0:half, lanes] = jnp.concatenate([a[:, 0:HD], b[:, 0:HD]], axis=1)
        upper = jnp.concatenate([a[:, HD:], b[:, HD:]], axis=1)
        taps_ref[half:KW, lanes] = upper[0 : KW - half]


def finish(recv, width, scale):
    count = recv.shape[0]
    vmem = pl.BlockSpec(memory_space=pltpu.VMEM)
    return pl.pallas_call(
        lambda *refs: finish_kernel(*refs, scale=scale),
        in_specs=[vmem],
        out_shape=[
            jax.ShapeDtypeStruct((HD // count, width), F32),
            jax.ShapeDtypeStruct((KW, width), F32),
        ],
        compiler_params=params(),
        name="finish",
    )(recv)


def exchange(blocks, step):
    pairs = lambda k: [(d, d ^ (step * k)) for d in range(FAST * SLOW)]
    moved = [
        local_memory(lax.ppermute(block, "dp", pairs(k))) for k, block in enumerate(blocks) if k
    ]
    return [blocks[0]] + moved


def local(frames, cotangent, w_qkv, w_out, w_conv, lengths):
    seq_count = lax.axis_size("seq")
    data_count = lax.axis_size("dp")
    rows, width = frames.shape[1:]
    first = lax.axis_index("seq") * rows
    grad_scale = 1.0 / math.sqrt(data_count * rows * seq_count)
    position = lax.axis_index("dp")
    fast = position % FAST
    slow = position // FAST
    place = [fast, slow]
    scalars = jnp.stack([lengths[0], first, jnp.zeros((), jnp.int32)] + place)
    x = frames[0]
    g = cotangent[0]

    forward = [(i, i + 1) for i in range(seq_count - 1)]
    backward = [(i + 1, i) for i in range(seq_count - 1)]
    edge = HALO // 2
    low = lax.ppermute(jnp.concatenate([x[-HALO:], g[-edge:]], axis=0), "seq", forward)
    high = lax.ppermute(jnp.concatenate([x[:HALO], g[:edge]], axis=0), "seq", backward)

    normed, send = project(x, w_qkv)
    heads = lax.all_to_all(send, "seq", 0, 0, tiled=True)
    heads, low, high = lax.optimization_barrier((heads, low, high))
    heads_near = local_memory(heads)
    low, high = local_memory(low), local_memory(high)
    normed_all = lax.all_gather(normed, "seq", axis=0, tiled=True)
    send, out, lse = attend(scalars, heads_near)
    att = local_memory(lax.all_to_all(send, "seq", 0, 0, tiled=True))
    output, res_grad, send, rounded, *picks = middle(scalars, att, x, g, low, high, w_out, w_conv)
    back = lax.all_to_all(send, "seq", 0, 0, tiled=True)
    far = [[FAST * i + j for i in range(SLOW)] for j in range(FAST)]
    rounded_all = lax.all_gather(rounded, "dp", axis=0, axis_index_groups=far, tiled=True)
    back, picks = lax.optimization_barrier((back, exchange(picks, FAST)))
    send = attend_back(scalars, heads, local_memory(back), out, lse)
    joined = lax.all_to_all(send, "seq", 0, 0, tiled=True)
    parts = exchange(gradient_parts(scalars, send, back, normed_all), FAST)
    parts = exchange(fold_first(scalars, parts, rounded_all, picks), 1)
    qkv, send = fold_last(parts, seq_count, grad_scale)
    input_grad = input_gradient(joined, w_qkv, x, res_grad)
    recv = lax.all_to_all(send, "seq", 0, 0, tiled=True)
    out_total, taps_total = finish(local_memory(recv), width, grad_scale)
    return (
        output[None],
        input_grad[None],
        qkv.reshape(width // data_count, 3, HD),
        out_total,
        taps_total,
    )


def solution(mesh):
    placed = (P("dp", "seq", None), P("dp", "seq", None), P(), P(), P(), P("dp"))
    return jax.shard_map(
        local,
        mesh=mesh,
        in_specs=placed,
        out_specs=(
            P("dp", "seq", None),
            P("dp", "seq", None),
            P("dp", None, "seq"),
            P(("dp", "seq"), None),
            P(),
        ),
        check_vma=False,
    )
```
